32 devices in a mesh: dp: 8 (over z, y), tensor: 4 (over x, core).
Axes of the slice: x: 2, y: 2, z: 4, core: 2. Of those that a mesh axis runs over, the one named last changes fastest.
Arguments:
- hidden_in: bfloat16 [4096, 1024], P(('dp', 'tensor')), may hold values from -5 to 5
- cotangent: bfloat16 [4096, 1024], P(('dp', 'tensor')), may hold values from -20 to 20
- segments: int32 [8, 512], P('dp'), may hold values from 0 to 3, as said below
- routes: int32 [4096, 8], P(('dp', 'tensor')), may hold values from 0 to 31, as said below
- gain_attn: float32 [1024], replicated, may hold values from 0.5 to 1.5
- w_query: bfloat16 [1024, 1024], P(None, 'tensor'), may hold values from -0.125 to 0.125
- key_matrix: bfloat16 [1024, 512], P(None, 'tensor'), may hold values from -0.125 to 0.125
- value_matrix: bfloat16 [1024, 512], P(None, 'tensor'), may hold values from -0.1875 to 0.1875
- attention_output_weight: bfloat16 [1024, 1024], P('tensor'), may hold values from -0.75 to 0.75
- gain_ffn: float32 [1024], replicated, may hold values from 0.5 to 1.5
- w_router: bfloat16 [1024, 32], replicated, may hold values from -0.34 to 0.34
- w_gate: bfloat16 [2, 1024, 512], P(None, None, 'tensor'), may hold values from -0.1875 to 0.1875
- w_up: bfloat16 [2, 1024, 512], P(None, None, 'tensor'), may hold values from -0.1875 to 0.1875
- w_down: bfloat16 [2, 512, 1024], P(None, 'tensor'), may hold values from -0.75 to 0.75
Outputs:
- output: bfloat16 [4096, 1024], P(('dp', 'tensor'))
- grad_in: float32 [4096, 1024], P(('dp', 'tensor'))
- grad_gain_attn: float32 [1024], replicated
- grad_w_query: float32 [1024, 1024], P(None, 'tensor')
- grad_w_key: float32 [1024, 512], P(None, 'tensor')
- grad_w_value: float32 [1024, 512], P(None, 'tensor')
- grad_w_out: float32 [1024, 1024], P('tensor')
- grad_gain_ffn: float32 [1024], replicated
- grad_router: float32 [1024, 32], replicated
- grad_gate: float32 [2, 1024, 512], P(None, None, 'tensor')
- grad_up: float32 [2, 1024, 512], P(None, None, 'tensor')
- grad_down: float32 [2, 512, 1024], P(None, 'tensor')
The draws below stay inside these ranges and needn't reach their ends.
Inputs may be any that keep to these rules, and one draw needn't show every extreme that they name: `segments`: numbers start at 0 and rise by one at each new document along a packed sequence; a packed sequence holds 2 to 4 documents, each of 102 to 256 tokens. `routes`: each token names 8 different experts.
All inputs are finite; a program needn't handle non-finite values.
Results may differ from the reference program's by a relative error of at most 0.034.
Values may be sent and summed in bfloat16 or wider, within the bound.
A program may use at most 128 MiB of HBM per device.

```python
import jax
import jax.numpy as jnp
from jax import lax

MODEL_WIDTH = 1024
QUERY_HEADS = 16
KEY_VALUE_HEADS = 8
HEAD_SIZE = 64
EXPERTS = 32
TOPK = 8
FF = 512
WIN = 2
DOCS = 4
SEQ = 512
TOKENS = 4096


def projection_drawn(private_key, heads):
    return jax.random.normal(private_key, (MODEL_WIDTH, heads * HEAD_SIZE)) * MODEL_WIDTH ** (-0.5)


def draw_w_query(key, part):
    private_key = jax.random.fold_in(key, 21)
    limit = 4.0 * MODEL_WIDTH ** (-0.5)
    drawn_values = projection_drawn(private_key, QUERY_HEADS)
    return jnp.clip(drawn_values, -limit, limit).astype(jnp.bfloat16)


def draw_key_matrix(key, part):
    private_key = jax.random.fold_in(key, 22)
    limit = 4.0 * MODEL_WIDTH ** (-0.5)
    drawn_values = projection_drawn(private_key, KEY_VALUE_HEADS)
    return jnp.clip(drawn_values, -limit, limit).astype(jnp.bfloat16)


def draw_w_router(key, part):
    private_key = jax.random.fold_in(key, 23)
    spread_scale = 0.7 * MODEL_WIDTH ** (-0.5)
    limit = 0.34
    drawn_values = jax.random.normal(private_key, (MODEL_WIDTH, EXPERTS)) * spread_scale
    return jnp.clip(drawn_values, -limit, limit).astype(jnp.bfloat16)


def draw_hidden_in(key, part):
    private_key = jax.random.fold_in(key, 24)
    drawn_values = jax.random.normal(private_key, (TOKENS, MODEL_WIDTH))
    return jnp.clip(drawn_values, -5.0, 5.0).astype(jnp.bfloat16)


def draw_cotangent(key, part):
    private_key = jax.random.fold_in(key, 25)
    row_index = jnp.arange(TOKENS).astype(jnp.float32)
    rise = jnp.exp(jnp.log(3.0) * row_index / TOKENS)[:, None]
    drawn_values = jnp.clip(jax.random.normal(private_key, (TOKENS, MODEL_WIDTH)), -5.0, 5.0) * rise
    return jnp.clip(drawn_values, -20.0, 20.0).astype(jnp.bfloat16)


def draw_routes(key, part):
    private_key = jax.random.fold_in(key, 27)
    score_key, favour_key = jax.random.split(private_key)
    raw_scores = jax.random.randint(score_key, (TOKENS, EXPERTS), 0, 2 ** 20, dtype=jnp.int32)
    favour_draw = jax.random.randint(favour_key, (TOKENS, EXPERTS), 0, 100, dtype=jnp.int32)
    expert_index = jnp.arange(EXPERTS, dtype=jnp.int32)[None, :]
    favoured = (favour_draw < 78) & (expert_index < WIN)
    scores = raw_scores * EXPERTS + expert_index + jnp.where(favoured, 2 ** 26, 0).astype(jnp.int32)
    picked_vals, picked = lax.top_k(scores, TOPK)
    return picked.astype(jnp.int32)


def draw_segments(key, part):
    private_key = jax.random.fold_in(key, 26)
    rows_count = TOKENS // SEQ
    low_len = SEQ // 5
    high_len = SEQ // 2
    count_key, order_key, length_key = jax.random.split(private_key, 3)
    doc_count = jax.random.randint(count_key, (rows_count,), 2, DOCS + 1)
    order = jax.random.permutation(order_key, rows_count)
    doc_count = jnp.where(order == 0, 2, doc_count)
    doc_count = jnp.where(order == 1, DOCS, doc_count)
    remain = jnp.full((rows_count,), SEQ, jnp.int32)
    cursor = jnp.zeros((rows_count,), jnp.int32)
    position = jnp.arange(SEQ)[None, :]
    seg_vals = jnp.zeros((rows_count, SEQ), jnp.int32)
    for slot in range(DOCS - 1):
        after = doc_count - 1 - slot
        active = after >= 1
        lower = jnp.maximum(low_len, remain - after * high_len)
        upper = jnp.minimum(high_len, remain - after * low_len)
        lower = jnp.where(active, lower, 0)
        upper = jnp.where(active, upper, 0)
        length = jax.random.randint(jax.random.fold_in(length_key, slot), (rows_count,), lower, upper + 1)
        length = jnp.where(active, length, 0)
        cursor = cursor + length
        remain = remain - length
        boundary = jnp.where(active, cursor, SEQ)
        seg_vals = seg_vals + (position >= boundary[:, None]).astype(jnp.int32)
    return seg_vals.astype(jnp.int32)


def shard_levels(rng, shape, cuts, smallest, largest):
    level, own = 1.0, jax.random.fold_in(rng, 6)
    for dim, blocks in cuts:
        draws = jnp.exp(jax.random.uniform(jax.random.fold_in(own, dim), (blocks,), jnp.float32, smallest / len(cuts), largest / len(cuts)))
        level = level * jnp.repeat(draws, shape[dim] // blocks).reshape([-1 if axis == dim else 1 for axis in range(len(shape))])
    return level


def centred(rng, extent, spread, reach, shards=(), held_as=jnp.bfloat16):
    entries = spread * jax.random.normal(rng, extent, jnp.float32)
    if shards:
        entries = entries * shard_levels(rng, extent, shards, -0.22, 0.18)
    return jnp.clip(entries, -reach, reach).astype(held_as)


def setup_inputs(seed: int = 0) -> dict:
    seeds = jax.random.split(jax.random.key(seed), 15)
    return {
        "hidden_in": draw_hidden_in(jax.random.fold_in(seeds[14], 71), 0),
        "cotangent": draw_cotangent(jax.random.fold_in(seeds[14], 71), 0),
        "segments": draw_segments(jax.random.fold_in(seeds[14], 71), 0),
        "routes": draw_routes(jax.random.fold_in(seeds[14], 71), 0),
        "gain_attn": jnp.clip(1.0 + 0.1 * jax.random.normal(seeds[4], (MODEL_WIDTH,), jnp.float32), 0.5, 1.5),
        "w_query": draw_w_query(jax.random.fold_in(seeds[14], 71), 0),
        "key_matrix": draw_key_matrix(jax.random.fold_in(seeds[14], 71), 0),
        "value_matrix": centred(seeds[7], (MODEL_WIDTH, KEY_VALUE_HEADS * HEAD_SIZE), MODEL_WIDTH ** -0.5, 0.1875, ((1, 4),)),
        "attention_output_weight": centred(seeds[8], (QUERY_HEADS * HEAD_SIZE, MODEL_WIDTH), HEAD_SIZE ** -0.5, 0.75, ((0, 4),)),
        "gain_ffn": jnp.clip(1.0 + 0.1 * jax.random.normal(seeds[9], (MODEL_WIDTH,), jnp.float32), 0.5, 1.5),
        "w_router": draw_w_router(jax.random.fold_in(seeds[14], 71), 0),
        "w_gate": centred(seeds[11], (WIN, MODEL_WIDTH, FF), MODEL_WIDTH ** -0.5, 0.1875, ((2, 4),)),
        "w_up": centred(seeds[12], (WIN, MODEL_WIDTH, FF), MODEL_WIDTH ** -0.5, 0.1875, ((2, 4),)),
        "w_down": centred(seeds[13], (WIN, FF, MODEL_WIDTH), (FF // 8) ** -0.5, 0.75, ((1, 4),)),
    }


EPS = 1e-06
THETA = 10000.0
NEGATIVE = -1e+30

def round_trip(array_in):
    return lax.optimization_barrier(array_in.astype(jnp.bfloat16)).astype(jnp.float32)

def inner_rows(left_op, right_op):
    return lax.dot_general(left_op, right_op, (((0,), (0,)), ((), ())), preferred_element_type=jnp.float32)

def outer_columns(left_op, right_op):
    return lax.dot_general(left_op, right_op, (((1,), (1,)), ((), ())), preferred_element_type=jnp.float32)

def rotary_tables(sequence_rows):
    half_dim = HEAD_SIZE // 2
    freq_table = THETA ** (-(jnp.arange(half_dim).astype(jnp.float32) * 2.0 / HEAD_SIZE))
    angles = jnp.arange(sequence_rows).astype(jnp.float32)[:, None] * freq_table[None, :]
    return (jnp.cos(angles)[:, None, :], jnp.sin(angles)[:, None, :])

def apply_rotary(vals_in, cosine_table, sine_values, direction):
    half_dim = vals_in.shape[-1] // 2
    first_half = vals_in[..., :half_dim]
    second_half = vals_in[..., half_dim:]
    return jnp.concatenate([first_half * cosine_table - direction * second_half * sine_values, second_half * cosine_table + direction * first_half * sine_values], axis=-1)

def norm_forward(row_vals, gain_vec):
    inverse = lax.rsqrt(lax.optimization_barrier(jnp.mean(row_vals * row_vals, axis=-1, keepdims=True)) + EPS)
    normed = row_vals * inverse
    return ((normed * gain_vec).astype(jnp.bfloat16), normed, inverse)

def norm_backward(grad_out, normed, inverse, gain_vec):
    grad_gain = lax.optimization_barrier(jnp.sum(grad_out * normed, axis=0))
    scaled = grad_out * gain_vec
    grad_rows = inverse * (scaled - normed * lax.optimization_barrier(jnp.mean(scaled * normed, axis=-1, keepdims=True)))
    return (grad_rows, grad_gain)

def gate_parts(gate_pre):
    sig_vals = jax.nn.sigmoid(gate_pre)
    return (gate_pre * sig_vals, sig_vals * (1.0 + gate_pre * (1.0 - sig_vals)))

def one_sequence(hidden_in, cotangent, seg_row, routes, gain_attn, w_query, key_matrix, value_matrix, attention_output_weight, gain_ffn, w_router, w_gate, w_up, w_down):
    sequence_rows = hidden_in.shape[0]
    query_groups = QUERY_HEADS // KEY_VALUE_HEADS
    scale_factor = HEAD_SIZE ** (-0.5)
    cosine_table, sine_values = rotary_tables(sequence_rows)
    rows_in = hidden_in.astype(jnp.float32)
    attention_normed, unit_attn, inverse_attn = norm_forward(rows_in, gain_attn)
    query_before_rotary = jnp.dot(attention_normed, w_query, preferred_element_type=jnp.float32).reshape(sequence_rows, QUERY_HEADS, HEAD_SIZE)
    key_before_rotary = jnp.dot(attention_normed, key_matrix, preferred_element_type=jnp.float32).reshape(sequence_rows, KEY_VALUE_HEADS, HEAD_SIZE)
    query_rows = apply_rotary(query_before_rotary, cosine_table, sine_values, 1.0).astype(jnp.bfloat16).reshape(sequence_rows, KEY_VALUE_HEADS, query_groups, HEAD_SIZE)
    keys_rot = apply_rotary(key_before_rotary, cosine_table, sine_values, 1.0).astype(jnp.bfloat16)
    value_inputs = jnp.dot(attention_normed, value_matrix, preferred_element_type=jnp.float32).astype(jnp.bfloat16).reshape(sequence_rows, KEY_VALUE_HEADS, HEAD_SIZE)
    positions = jnp.arange(sequence_rows)
    allowed = (seg_row[:, None] == seg_row[None, :]) & (positions[None, :] <= positions[:, None])
    scores = jnp.einsum('qhgd,khd->hgqk', query_rows.astype(jnp.float32), keys_rot.astype(jnp.float32)) * scale_factor
    scores = jnp.where(allowed[None, None], scores, NEGATIVE)
    peak_score = lax.optimization_barrier(jnp.max(scores, axis=-1, keepdims=True))
    log_total = peak_score + jnp.log(lax.optimization_barrier(jnp.sum(jnp.exp(scores - peak_score), axis=-1, keepdims=True)))
    probs_all = jnp.exp(scores - log_total)
    probs_bf = round_trip(probs_all)
    mixed_heads = jnp.einsum('hgqk,khd->qhgd', probs_bf, value_inputs.astype(jnp.float32)).astype(jnp.bfloat16)
    mixed_flat = mixed_heads.reshape(sequence_rows, QUERY_HEADS * HEAD_SIZE)
    attn_out = jnp.dot(mixed_flat, attention_output_weight, preferred_element_type=jnp.float32)
    after_attn = rows_in + attn_out
    normed_ffn, unit_ffn, inverse_ffn = norm_forward(after_attn, gain_ffn)
    router_logits = jnp.dot(normed_ffn, w_router, preferred_element_type=jnp.float32)
    router_probs = jax.nn.softmax(router_logits, axis=-1)
    chosen_probs = jnp.take_along_axis(router_probs, routes, axis=1)
    picked_mask = (routes[:, :, None] == jnp.arange(WIN)[None, None, :]).astype(jnp.float32)
    combine_used = round_trip(lax.optimization_barrier(jnp.sum(chosen_probs[:, :, None] * picked_mask, axis=1)))
    combined = jnp.zeros((sequence_rows, MODEL_WIDTH), jnp.float32)
    saved_parts = []
    for expert in range(WIN):
        gate_pre = jnp.dot(normed_ffn, w_gate[expert], preferred_element_type=jnp.float32)
        up_pre = jnp.dot(normed_ffn, w_up[expert], preferred_element_type=jnp.float32)
        silu_val, slope_val = gate_parts(gate_pre)
        inner_act = (silu_val * up_pre).astype(jnp.bfloat16)
        expert_out = jnp.dot(inner_act, w_down[expert], preferred_element_type=jnp.float32)
        combined = combined + combine_used[:, expert:expert + 1] * expert_out
        saved_parts.append((up_pre, silu_val, slope_val, inner_act, expert_out))
    output = (after_attn + combined).astype(jnp.bfloat16)
    grad_top = cotangent.astype(jnp.float32)
    grad_normed_ffn = jnp.zeros((sequence_rows, MODEL_WIDTH), jnp.float32)
    grad_combine_list, grad_gate_list, grad_up_list, grad_down_list = ([], [], [], [])
    for expert in range(WIN):
        up_pre, silu_val, slope_val, inner_act, expert_out = saved_parts[expert]
        grad_expert = (combine_used[:, expert:expert + 1] * grad_top).astype(jnp.bfloat16)
        grad_combine_list.append(lax.optimization_barrier(jnp.sum(grad_top * expert_out, axis=-1)))
        grad_down_list.append(inner_rows(inner_act, grad_expert))
        grad_inner = outer_columns(grad_expert, w_down[expert])
        grad_gate_pre = (grad_inner * up_pre * slope_val).astype(jnp.bfloat16)
        grad_up_pre = (grad_inner * silu_val).astype(jnp.bfloat16)
        grad_gate_list.append(inner_rows(normed_ffn, grad_gate_pre))
        grad_up_list.append(inner_rows(normed_ffn, grad_up_pre))
        grad_normed_ffn = grad_normed_ffn + outer_columns(grad_gate_pre, w_gate[expert]) + outer_columns(grad_up_pre, w_up[expert])
    grad_combine = jnp.stack(grad_combine_list, axis=1)
    route_counts = lax.optimization_barrier(jnp.sum(picked_mask, axis=1))
    grad_rprobs = jnp.concatenate([grad_combine * route_counts, jnp.zeros((sequence_rows, EXPERTS - WIN), jnp.float32)], axis=1)
    grad_logits = (router_probs * (grad_rprobs - lax.optimization_barrier(jnp.sum(router_probs * grad_rprobs, axis=-1, keepdims=True)))).astype(jnp.bfloat16)
    grad_router = inner_rows(normed_ffn, grad_logits)
    grad_normed_ffn = grad_normed_ffn + outer_columns(grad_logits, w_router)
    grad_after, grad_gain_ffn = norm_backward(grad_normed_ffn, unit_ffn, inverse_ffn, gain_ffn)
    grad_after = grad_after + grad_top
    gradient_after_half = grad_after.astype(jnp.bfloat16)
    grad_w_out = inner_rows(mixed_flat, gradient_after_half)
    mixed_gradient = outer_columns(gradient_after_half, attention_output_weight).astype(jnp.bfloat16).reshape(sequence_rows, KEY_VALUE_HEADS, query_groups, HEAD_SIZE)
    grad_mixed32 = mixed_gradient.astype(jnp.float32)
    delta_rows = jnp.transpose(lax.optimization_barrier(jnp.sum(grad_mixed32 * mixed_heads.astype(jnp.float32), axis=-1)), (1, 2, 0))[..., None]
    value_gradients = jnp.einsum('hgqk,qhgd->khd', probs_bf, grad_mixed32)
    grad_probs = jnp.einsum('qhgd,khd->hgqk', grad_mixed32, value_inputs.astype(jnp.float32))
    grad_scores = round_trip(probs_all * (grad_probs - delta_rows) * scale_factor)
    grad_query = jnp.einsum('hgqk,khd->qhgd', grad_scores, keys_rot.astype(jnp.float32))
    key_gradient = jnp.einsum('hgqk,qhgd->khd', grad_scores, query_rows.astype(jnp.float32))
    grad_query_bf = apply_rotary(grad_query.reshape(sequence_rows, QUERY_HEADS, HEAD_SIZE), cosine_table, sine_values, -1.0).astype(jnp.bfloat16).reshape(sequence_rows, QUERY_HEADS * HEAD_SIZE)
    key_gradient_half = apply_rotary(key_gradient, cosine_table, sine_values, -1.0).astype(jnp.bfloat16).reshape(sequence_rows, KEY_VALUE_HEADS * HEAD_SIZE)
    value_gradient_half = value_gradients.astype(jnp.bfloat16).reshape(sequence_rows, KEY_VALUE_HEADS * HEAD_SIZE)
    grad_w_query = inner_rows(attention_normed, grad_query_bf)
    grad_w_key = inner_rows(attention_normed, key_gradient_half)
    grad_w_value = inner_rows(attention_normed, value_gradient_half)
    grad_normed_attn = outer_columns(grad_query_bf, w_query) + outer_columns(key_gradient_half, key_matrix) + outer_columns(value_gradient_half, value_matrix)
    grad_in, grad_gain_attn = norm_backward(grad_normed_attn, unit_attn, inverse_attn, gain_attn)
    grad_in = grad_in + grad_after
    grads = (grad_gain_attn, grad_w_query, grad_w_key, grad_w_value, grad_w_out, grad_gain_ffn, grad_router, jnp.stack(grad_gate_list), jnp.stack(grad_up_list), jnp.stack(grad_down_list))
    return (output, grad_in, grads)

def reference(hidden_in, cotangent, segments, routes, gain_attn, w_query, key_matrix, value_matrix, attention_output_weight, gain_ffn, w_router, w_gate, w_up, w_down):
    seq_count = hidden_in.shape[0] // SEQ
    rows_seq = hidden_in.reshape(seq_count, SEQ, MODEL_WIDTH)
    cot_seq = cotangent.reshape(seq_count, SEQ, MODEL_WIDTH)
    route_seq = routes.reshape(seq_count, SEQ, TOPK)
    zero_grads = (jnp.zeros(gain_attn.shape, jnp.float32), jnp.zeros(w_query.shape, jnp.float32), jnp.zeros(key_matrix.shape, jnp.float32), jnp.zeros(value_matrix.shape, jnp.float32), jnp.zeros(attention_output_weight.shape, jnp.float32), jnp.zeros(gain_ffn.shape, jnp.float32), jnp.zeros(w_router.shape, jnp.float32), jnp.zeros(w_gate.shape, jnp.float32), jnp.zeros(w_up.shape, jnp.float32), jnp.zeros(w_down.shape, jnp.float32))

    def step_fn(carry, items):
        output, grad_in, grads = one_sequence(items[0], items[1], items[2], items[3], gain_attn, w_query, key_matrix, value_matrix, attention_output_weight, gain_ffn, w_router, w_gate, w_up, w_down)
        return (tuple((old + new for old, new in zip(carry, grads))), (output, grad_in))
    totals, stacked = lax.scan(step_fn, zero_grads, (rows_seq, cot_seq, segments, route_seq))
    output = stacked[0].reshape(seq_count * SEQ, MODEL_WIDTH)
    grad_in = stacked[1].reshape(seq_count * SEQ, MODEL_WIDTH)
    return (output, grad_in, totals[0], totals[1], totals[2], totals[3], totals[4], totals[5], totals[6], totals[7], totals[8], totals[9])
```

```python
import functools
import math
from types import SimpleNamespace

import jax
import jax.numpy as jnp
import numpy as np
from jax import lax
from jax.experimental import pallas as pl
from jax.experimental.pallas import tpu as pltpu
from jax.sharding import PartitionSpec as P

HEAD_SIZE = 64
LANES = 128
EPS = 1e-06
THETA = 10000.0
NEGATIVE = -1e30
MESH = pl.DeviceIdType.MESH
F32 = jnp.float32
BF16 = jnp.bfloat16

FFN, DOWN, OUT, ATT = range(4)
VMEM_LIMIT = 61 * 1024 * 1024


def nt(left, right):
    return lax.dot_general(left, right, (((1,), (1,)), ((), ())), preferred_element_type=F32)


def tn(left, right):
    return lax.dot_general(left, right, (((0,), (0,)), ((), ())), preferred_element_type=F32)


def nn(left, right):
    return jnp.dot(left, right, preferred_element_type=F32)


def piece_order(n, inner, first_is_inner):
    return (inner, n // inner) if first_is_inner else (n // inner, inner)


def layer_kernel(n, inner, orders, r):
    outer = n // inner
    me = lax.axis_index("dp")
    mt = lax.axis_index("tensor")
    y = me % inner
    z = me // inner
    xc = mt // 2
    core = mt % 2
    pair = xc * 2 + (1 - core)
    across = (1 - xc) * 2 + core

    R, W = r.hid.shape
    S = r.xa.shape[0]
    HC = r.wo.shape[0]

    def remote(src, dst, send, recv, device):
        return pltpu.make_async_remote_copy(
            src_ref=src, dst_ref=dst, send_sem=send, recv_sem=recv,
            device_id=device, device_id_type=MESH,
        )

    def block_of(k):
        return ((xc + 1 - k // 2) % 2) * 2 + (core + 1 - k % 2) % 2

    def rows_of(block):
        return pl.ds(pl.multiple_of(block * R, R), R)

    loads = [
        (r.hidden_hbm, r.hid),
        (r.cot_hbm, r.cot.at[rows_of(mt)]),
        (r.wq_hbm, r.wqkv.at[:, 0:256]),
        (r.wk_hbm, r.wqkv.at[:, 256:384]),
        (r.wv_hbm, r.wqkv.at[:, 384:512]),
        (r.cos_hbm, r.cos),
        (r.sin_hbm, r.sin),
        (r.wo_hbm, r.wo),
        (r.wg_hbm.at[0], r.wgu.at[:, 0:128]),
        (r.wg_hbm.at[1], r.wgu.at[:, 128:256]),
        (r.wu_hbm.at[0], r.wgu.at[:, 256:384]),
        (r.wu_hbm.at[1], r.wgu.at[:, 384:512]),
        (r.wd_hbm, r.wd),
    ]
    load = [pltpu.make_async_copy(a, b, r.load_sem.at[i]) for i, (a, b) in enumerate(loads)]
    for copy in load:
        copy.start()

    barrier = pltpu.get_barrier_semaphore()
    for k in range(1, 4):
        pl.semaphore_signal(barrier, inc=1, device_id=(me, (mt + k) % 4), device_id_type=MESH)
    for k in range(1, inner):
        pl.semaphore_signal(
            barrier, inc=1, device_id=(z * inner + (y + k) % inner, mt), device_id_type=MESH
        )
    for k in range(1, outer):
        pl.semaphore_signal(
            barrier, inc=1, device_id=(((z + k) % outer) * inner + y, mt), device_id_type=MESH
        )

    def gather(i, buf):
        own = buf.at[rows_of(mt)]
        far = buf.at[rows_of(across)]
        ss, rs = r.ag_send, r.ag_recv
        return (
            remote(own, own, ss.at[i, 0], rs.at[i, 0], (me, across)),
            remote(own, own, ss.at[i, 1], rs.at[i, 1], (me, pair)),
            remote(far, far, ss.at[i, 2], rs.at[i, 2], (me, pair)),
        )

    def gather_start(g):
        g[0].start()
        g[1].start()

    def gather_step(k, *gs):
        @pl.when(k == 1)
        def _():
            for g in gs:
                g[1].wait_recv()

        @pl.when(k == 2)
        def _():
            for g in gs:
                g[0].wait_recv()
                g[2].start()

        @pl.when(k == 3)
        def _():
            for g in gs:
                g[2].wait_recv()

    def scatter(i, c):
        sb, sx, rp, rx = r.sb[i], r.sx[i], r.rp[i], r.rx[i]
        ss, rs = r.rs_send, r.rs_recv
        return (
            remote(sb.at[0], rp.at[0], ss.at[i, 0], rs.at[i, 0], (me, pair)),
            remote(sx, rx, ss.at[i, 1], rs.at[i, 1], (me, across)),
            remote(sb.at[1], rp.at[1], ss.at[i, 2], rs.at[i, 2], (me, pair)),
        )

    def scatter_step(k, i, c, part):
        sb, sx, rp = r.sb[i], r.sx[i], r.rp[i]

        @pl.when(k == 0)
        def _():
            sb[0] = part[...].astype(BF16)
            c[0].start()

        @pl.when(k == 1)
        def _():
            c[0].wait_recv()
            sx[...] = (part[...] + rp[0].astype(F32)).astype(BF16)
            c[1].start()

        @pl.when(k == 2)
        def _():
            sb[1] = part[...].astype(BF16)
            c[2].start()

    pieces = []
    for p, first_is_inner in enumerate(orders):
        na, nb = piece_order(n, inner, first_is_inner)
        ma, mb = (y, z) if first_is_inner else (z, y)
        pieces.append((na, nb, ma, mb, first_is_inner))

    def dp_device(p, a, b):
        return (b * inner + a, mt) if pieces[p][4] else (a * inner + b, mt)

    def stage1(p):
        na, nb, ma, mb, _ = pieces[p]
        out = []
        for k in range(1, na):
            to = (ma + k) % na
            out.append(remote(
                r.loc[p].at[pl.ds(to * nb, nb)], r.first[p].at[k - 1],
                r.s1[p].at[k - 1], r.r1[p].at[k - 1], dp_device(p, to, mb),
            ))
        return out

    def stage2(p):
        na, nb, ma, mb, _ = pieces[p]
        out = []
        for k in range(1, nb):
            to = (mb + k) % nb
            out.append(remote(
                r.held[p].at[to], r.second[p].at[k - 1],
                r.s2[p].at[k - 1], r.r2[p].at[k - 1], dp_device(p, ma, to),
            ))
        return out

    def stage3(p):
        na, nb, ma, mb, _ = pieces[p]
        out = []
        mine = r.full[p].at[ma * nb + mb]
        for k in range(1, nb):
            out.append(remote(
                mine, mine, r.s3[p].at[k - 1], r.r3[p].at[k - 1],
                dp_device(p, ma, (mb + k) % nb),
            ))
        return out

    def stage4(p):
        na, nb, ma, mb, _ = pieces[p]
        out = []
        mine = r.full[p].at[pl.ds(ma * nb, nb)]
        for k in range(1, na):
            out.append(remote(
                mine, mine, r.s4[p].at[k - 1], r.r4[p].at[k - 1],
                dp_device(p, (ma + k) % na, mb),
            ))
        return out

    def start(copies):
        for copy in copies:
            copy.start()

    def arrive(copies):
        for copy in copies:
            copy.wait_recv()

    def to_stage2(p):
        na, nb, ma, mb, _ = pieces[p]
        arrive(stage1(p))

        def step(o, _):
            acc = r.loc[p][ma * nb + o].astype(F32)
            for k in range(na - 1):
                acc = acc + r.first[p][k, o].astype(F32)
            r.held[p][o] = acc.astype(BF16)
            return 0

        lax.fori_loop(0, nb, step, 0)
        start(stage2(p))

    def to_stage3(p):
        na, nb, ma, mb, _ = pieces[p]
        arrive(stage2(p))
        acc = r.held[p][mb].astype(F32)
        for k in range(nb - 1):
            acc = acc + r.second[p][k].astype(F32)
        r.full[p][ma * nb + mb] = acc.astype(BF16)
        start(stage3(p))

    def to_stage4(p):
        arrive(stage3(p))
        start(stage4(p))

    outs = []

    def write_out(src, dst):
        copy = pltpu.make_async_copy(src, dst, r.out_sem.at[len(outs)])
        copy.start()
        outs.append(copy)

    def small_exchange(g, src, axis):
        size = outer if axis else inner
        out = []
        for k in range(1, size):
            if axis:
                to = ((z + k) % outer) * inner + y
            else:
                to = z * inner + (y + k) % inner
            out.append(remote(
                src, g.inbox[axis].at[k - 1], g.send[axis].at[k - 1], g.recv[axis].at[k - 1], (to, mt)
            ))
        return out

    def small_tensor(g, src, slots):
        return [
            remote(
                src, slots(k), g.send[2].at[k - 1], g.recv[2].at[k - 1], (me, (mt + k) % 4)
            )
            for k in range(1, 4)
        ]

    gn, rt = SimpleNamespace(**r.gn), SimpleNamespace(**r.rt)
    lane = lax.broadcasted_iota(jnp.int32, (R, LANES), 1)
    low = lane < HEAD_SIZE
    first_half = (lane % HEAD_SIZE) < HEAD_SIZE // 2

    def swap(v):
        return jnp.where(first_half, pltpu.roll(v, 96, 1), pltpu.roll(v, 32, 1))

    CH = 32

    def row_chunks(body):
        def step(i, _):
            body(pl.ds(pl.multiple_of(i * CH, CH), CH))
            return 0

        lax.fori_loop(0, R // CH, step, 0)

    def own_chunk(rows):
        return pl.ds(pl.multiple_of(mt * R + rows.start, CH), CH)

    load[0].wait()

    def norm_rows(rows):
        h = r.hid[rows, :].astype(F32)
        inv = lax.rsqrt(jnp.mean(h * h, axis=-1, keepdims=True) + EPS)
        r.xa[own_chunk(rows), :] = (h * inv * r.gain_attn[...]).astype(BF16)

    row_chunks(norm_rows)

    pl.semaphore_wait(barrier, 3 + (inner - 1) + (outer - 1))

    ag_xa = gather(0, r.xa)
    gather_start(ag_xa)
    load[1].wait()
    ag_cot = gather(1, r.cot)
    ag_cot[1].start()
    for copy in load[2:7]:
        copy.wait()

    r.gk[...] = jnp.zeros_like(r.gk)
    r.gv[...] = jnp.zeros_like(r.gv)
    gn.own[...] = jnp.zeros_like(gn.own)

    def project(k, _):
        gather_step(k, ag_xa)
        b = block_of(3 - k)
        rows = rows_of(b)
        qkv = nn(r.xa[rows, :], r.wqkv[...])
        cos, sin = r.cos[rows, :], r.sin[rows, :]

        def rope(v):
            return v * cos + swap(v) * sin

        zero = jnp.zeros((R, LANES), F32)
        q0 = rope(qkv[:, 0:128]) * HEAD_SIZE ** (-0.5)
        q1 = rope(qkv[:, 128:256]) * HEAD_SIZE ** (-0.5)
        kk = rope(qkv[:, 256:384])
        vv = qkv[:, 384:512]
        r.q[rows, 0:128] = q0.astype(BF16)
        r.q[rows, 128:256] = q1.astype(BF16)
        r.qp[b, 0 * R:1 * R, :] = jnp.where(low, q0, zero).astype(BF16)
        r.qp[b, 1 * R:2 * R, :] = jnp.where(low, pltpu.roll(q0, 64, 1), zero).astype(BF16)
        r.qp[b, 2 * R:3 * R, :] = jnp.where(low, zero, pltpu.roll(q1, 64, 1)).astype(BF16)
        r.qp[b, 3 * R:4 * R, :] = jnp.where(low, zero, q1).astype(BF16)
        for dst, val in ((r.klh, kk), (r.vlh, vv)):
            turned = pltpu.roll(val, 64, 1)
            dst[0, rows, :] = jnp.where(low, val, zero).astype(BF16)
            dst[1, rows, :] = jnp.where(low, zero, turned).astype(BF16)
            dst[2, rows, :] = jnp.where(low, turned, zero).astype(BF16)
            dst[3, rows, :] = jnp.where(low, zero, val).astype(BF16)
        return 0

    lax.fori_loop(0, 4, project, 0)
    ag_cot[0].start()
    load[7].wait()

    KW = 3 * R
    rs1 = scatter(0, W)

    def attend(k, _):
        b = block_of(k)
        rows = rows_of(b)
        wstart = (b // 3) * R
        win = pl.ds(pl.multiple_of(wstart, R), KW)
        seg_q = r.seg[0:1, rows].astype(F32)
        seg_col = jnp.transpose(jnp.broadcast_to(seg_q, (R, R)))[:, 0:1]
        seg_k = r.seg[0:1, win].astype(F32)
        at_q = lax.broadcasted_iota(jnp.int32, (R, KW), 0) + (b * R - wstart)
        at_k = lax.broadcasted_iota(jnp.int32, (R, KW), 1)
        bias = jnp.where((seg_col == seg_k) & (at_k <= at_q), 0.0, NEGATIVE)
        for kv in range(2):
            q = r.q[rows, kv * LANES:(kv + 1) * LANES]
            mixed = jnp.zeros((R, LANES), F32)
            for h in range(2):
                i = kv * 2 + h
                s = nt(q, r.klh[i, win, :]) + bias
                e = jnp.exp(s - jnp.max(s, axis=-1, keepdims=True))
                prob = (e * (1.0 / jnp.sum(e, axis=-1, keepdims=True))).astype(BF16)
                r.prob[b, i * R:(i + 1) * R, :] = prob
                mixed = mixed + nn(prob, r.vlh[i, win, :])
            r.mixed[rows, kv * LANES:(kv + 1) * LANES] = mixed.astype(BF16)
        r.part[...] = nn(r.mixed[rows, :], r.wo[...])
        scatter_step(k, 0, rs1, r.part)
        return 0

    lax.fori_loop(0, 4, attend, 0)
    for copy in load[8:13]:
        copy.wait()
    rs1[2].wait_recv()
    rs1[1].wait_recv()

    def after_rows(rows):
        a = r.hid[rows, :].astype(F32) + (
            r.part[rows, :] + r.rp[0][1, rows, :].astype(F32) + r.rx[0][rows, :].astype(F32)
        )
        r.after[rows, :] = a
        inv = lax.rsqrt(jnp.mean(a * a, axis=-1, keepdims=True) + EPS)
        r.xf[own_chunk(rows), :] = (a * inv * r.gain_ffn[...]).astype(BF16)

    row_chunks(after_rows)
    ag_xf = gather(2, r.xf)
    gather_start(ag_xf)

    E = r.wr.shape[0]
    expert = lax.broadcasted_iota(jnp.int32, (R, E), 1)
    logits = nt(r.xf[rows_of(mt), :], r.wr[...])
    el = jnp.exp(logits - jnp.max(logits, axis=-1, keepdims=True))
    router_probs = el / jnp.sum(el, axis=-1, keepdims=True)
    routes = r.routes[...]

    def count(e):
        named = jnp.sum((routes == e).astype(F32), axis=0, keepdims=True)
        return jnp.transpose(jnp.broadcast_to(named, (R, R)))[:, 0:1]

    count0, count1 = count(0), count(1)
    counts = jnp.where(expert == 0, count0, jnp.where(expert == 1, count1, 0.0))
    r.rprobs[...] = router_probs
    r.counts[...] = counts
    r.cb[rows_of(mt), :] = jnp.zeros((R, LANES), BF16)
    r.cb[rows_of(mt), 0:E] = (router_probs * counts).astype(BF16)
    ag_cb = gather(3, r.cb)
    gather_start(ag_cb)

    ag_cot[1].wait_recv()
    ag_cot[0].wait_recv()
    ag_cot[2].start()
    H2 = r.wd.shape[0]

    def experts(k, _):
        gather_step(k, ag_xf, ag_cb)

        @pl.when(k == 3)
        def _():
            ag_cot[2].wait_recv()

        b = block_of(3 - k)
        rows = rows_of(b)
        gu = nn(r.xf[rows, :], r.wgu[...])
        down = nt(r.cot[rows, :], r.wd[...])
        cb = r.cb[rows, :].astype(F32)
        gcol = jnp.zeros((R, LANES), F32)
        for e in range(2):
            cols = slice(e * LANES, (e + 1) * LANES)
            up_cols = slice(H2 + e * LANES, H2 + (e + 1) * LANES)
            g, u, a = gu[:, cols], gu[:, up_cols], down[:, cols]
            c = cb[:, e:e + 1]
            sig = 1.0 / (1.0 + jnp.exp(-g))
            silu = g * sig
            act = silu * u
            ga = c * a
            r.ci[rows, cols] = (c * act).astype(BF16)
            r.dgu[rows, cols] = (ga * u * (sig * (1.0 + g * (1.0 - sig)))).astype(BF16)
            r.dgu[rows, up_cols] = (ga * silu).astype(BF16)
            gcol = jnp.where(lane == e, jnp.sum(act * a, axis=-1, keepdims=True), gcol)
        r.pr[rows, 0:W] = nt(r.dgu[rows, :], r.wgu[...])
        r.pr[rows, W:W + LANES] = gcol
        return 0

    lax.fori_loop(0, 4, experts, 0)
    rs2 = scatter(1, W + LANES)
    for k in (0, 2, 1):
        scatter_step(k, 1, rs2, r.pr.at[rows_of(block_of(k))])

    depth = W // n

    def store_piece(p, row, tile, col, cols):
        count = tile.shape[0] // depth
        r.loc[p][pl.ds(row * count, count), :, col:col + cols] = tile.astype(BF16).reshape(
            count, depth, cols
        )

    def tiles(p, left, right):
        def step(i, _):
            cols = pl.ds(pl.multiple_of(i * 256, 256), 256)
            tile = tn(left[:, cols], right[...])
            store_piece(p, i, tile, 0, tile.shape[1])
            return 0

        lax.fori_loop(0, W // 256, step, 0)
        start(stage1(p))

    def tiles_by_columns(p, left, right):
        def step(i, _):
            cols = pl.ds(pl.multiple_of(i * 256, 256), 256)
            tile = tn(left[...], right[:, cols])
            store_piece(p, i, tile, 0, tile.shape[1])
            return 0

        lax.fori_loop(0, W // 256, step, 0)
        start(stage1(p))

    tiles(FFN, r.xf, r.dgu)
    tiles_by_columns(DOWN, r.ci, r.cot)

    rs2[2].wait_recv()
    rs2[1].wait_recv()
    own = rows_of(mt)
    gcomb = (
        r.pr[own, W:W + LANES]
        + r.rp[1][1, :, W:W + LANES].astype(F32)
        + r.rx[1][:, W:W + LANES].astype(F32)
    )[:, 0:E]
    grp = gcomb * r.counts[...]
    rp = r.rprobs[...]
    glog = (rp * (grp - jnp.sum(rp * grp, axis=-1, keepdims=True))).astype(BF16)
    r.ga[own, W:W + LANES] = jnp.zeros((R, LANES), BF16)
    r.ga[own, W:W + E] = glog
    r.part[...] = nn(glog, r.wr[...])

    def grad_after_rows(rows):
        a = r.after[rows, :]
        inv = lax.rsqrt(jnp.mean(a * a, axis=-1, keepdims=True) + EPS)
        unit = a * inv
        g = (
            r.part[rows, :]
            + r.pr[own_chunk(rows), 0:W]
            + r.rp[1][1, rows, 0:W].astype(F32)
            + r.rx[1][rows, 0:W].astype(F32)
        )
        gn.own[0:1, :] += jnp.sum(g * unit, axis=0, keepdims=True)
        scaled = g * r.gain_ffn[...]
        back = inv * (scaled - unit * jnp.mean(scaled * unit, axis=-1, keepdims=True))
        ga = back + r.cot[own_chunk(rows), :].astype(F32)
        r.ga_own[rows, :] = ga
        r.ga[own_chunk(rows), 0:W] = ga.astype(BF16)

    row_chunks(grad_after_rows)
    ag_ga = gather(4, r.ga)
    gather_start(ag_ga)

    def attend_back(k, _):
        gather_step(k, ag_ga)
        b = block_of(3 - k)
        rows = rows_of(b)
        wstart = (b // 3) * R
        win = pl.ds(pl.multiple_of(wstart, R), KW)
        gm = nt(r.ga[rows, 0:W], r.wo[...])
        zero = jnp.zeros((R, LANES), F32)
        for kv in range(2):
            cols = slice(kv * LANES, (kv + 1) * LANES)
            gmk = gm[:, cols].astype(BF16)
            gmf = gmk.astype(F32)
            turned = pltpu.roll(gmf, 64, 1)
            if kv == 0:
                r.gmp[0 * R:1 * R, :] = jnp.where(low, gmf, zero).astype(BF16)
                r.gmp[1 * R:2 * R, :] = jnp.where(low, turned, zero).astype(BF16)
            else:
                r.gmp[2 * R:3 * R, :] = jnp.where(low, zero, turned).astype(BF16)
                r.gmp[3 * R:4 * R, :] = jnp.where(low, zero, gmf).astype(BF16)
            prod = gmf * r.mixed[rows, cols].astype(F32)
            delta_lo = jnp.sum(jnp.where(low, prod, zero), axis=-1, keepdims=True)
            delta_hi = jnp.sum(jnp.where(low, zero, prod), axis=-1, keepdims=True)
            gq = zero
            for h, delta in ((0, delta_lo), (1, delta_hi)):
                i = kv * 2 + h
                head = slice(i * R, (i + 1) * R)
                dp = nt(gmk, r.vlh[i, win, :])
                ds = (r.prob[b, head, :].astype(F32) * (dp - delta)).astype(BF16)
                r.ds[head, :] = ds
                gq = gq + nn(ds, r.klh[i, win, :])
            gq = gq * HEAD_SIZE ** (-0.5)
            gq = gq * r.cos[rows, :] - swap(gq) * r.sin[rows, :]
            r.dqkv[rows, cols] = gq.astype(BF16)
        r.gk[win, :] += tn(r.ds[...], r.qp[b])
        r.gv[win, :] += tn(r.prob[b], r.gmp[...])
        return 0

    lax.fori_loop(0, 4, attend_back, 0)


    def out_step(i, _):
        cols = pl.ds(pl.multiple_of(i * 256, 256), 256)
        tile = tn(r.mixed[...], r.ga[:, cols])
        store_piece(OUT, i, tile, 0, tile.shape[1])
        return 0

    def finish_kv(k, _):
        rows = rows_of(k)
        gk = r.gk[rows, :]
        gk = gk * r.cos[rows, :] - swap(gk) * r.sin[rows, :]
        r.dqkv[rows, 256:384] = gk.astype(BF16)
        r.dqkv[rows, 384:512] = r.gv[rows, :].astype(BF16)
        return 0

    lax.fori_loop(0, 4, finish_kv, 0)
    lax.fori_loop(0, W // 256, out_step, 0)
    start(stage1(OUT))
    tiles(ATT, r.xa, r.dqkv)

    to_stage2(FFN)

    rs3 = scatter(2, W)

    def input_part(k, _):
        r.part[...] = nt(r.dqkv[rows_of(block_of(k)), :], r.wqkv[...])
        scatter_step(k, 2, rs3, r.part)
        return 0

    lax.fori_loop(0, 4, input_part, 0)

    to_stage2(DOWN)
    quarter = pl.ds(pl.multiple_of(mt * (W // 4), W // 4), W // 4)
    rt.own[...] = tn(r.ga[:, W:W + LANES], r.xf[:, quarter])[0:E, :]
    rt0 = small_exchange(rt, rt.own, 0)
    start(rt0)

    rs3[2].wait_recv()
    rs3[1].wait_recv()

    def grad_in_rows(rows):
        h = r.hid[rows, :].astype(F32)
        inv = lax.rsqrt(jnp.mean(h * h, axis=-1, keepdims=True) + EPS)
        unit = h * inv
        g = r.part[rows, :] + r.rp[2][1, rows, :].astype(F32) + r.rx[2][rows, :].astype(F32)
        gn.own[1:2, :] += jnp.sum(g * unit, axis=0, keepdims=True)
        scaled = g * r.gain_attn[...]
        back = inv * (scaled - unit * jnp.mean(scaled * unit, axis=-1, keepdims=True))
        r.grad_in_v[rows, :] = back + r.ga_own[rows, :]

    row_chunks(grad_in_rows)
    write_out(r.grad_in_v, r.grad_in)
    gt = small_tensor(gn, gn.own, lambda k: gn.inbox[2].at[k - 1])
    start(gt)
    to_stage2(OUT)
    to_stage3(FFN)

    rs4 = scatter(3, W)

    def output_part(k, _):
        r.part[...] = nn(r.ci[rows_of(block_of(k)), :], r.wd[...])
        scatter_step(k, 3, rs4, r.part)
        return 0

    lax.fori_loop(0, 4, output_part, 0)

    arrive(gt)
    total = gn.own[...]
    for k in range(3):
        total = total + gn.inbox[2][k]
    gn.first[...] = total
    g0 = small_exchange(gn, gn.first, 0)
    start(g0)
    arrive(rt0)
    total = rt.own[...]
    for k in range(inner - 1):
        total = total + rt.inbox[0][k]
    rt.first[...] = total
    rt1 = small_exchange(rt, rt.first, 1)
    start(rt1)

    to_stage3(DOWN)
    to_stage2(ATT)
    rs4[2].wait_recv()
    rs4[1].wait_recv()

    def output_rows(rows):
        a = r.part[rows, :] + r.rp[3][1, rows, :].astype(F32) + r.rx[3][rows, :].astype(F32)
        r.output_v[rows, :] = (r.after[rows, :] + a).astype(BF16)

    row_chunks(output_rows)
    write_out(r.output_v, r.output)

    arrive(g0)
    total = gn.first[...]
    for k in range(inner - 1):
        total = total + gn.inbox[0][k]
    gn.second[...] = total
    g1 = small_exchange(gn, gn.second, 1)
    start(g1)
    arrive(rt1)
    total = rt.first[...]
    for k in range(outer - 1):
        total = total + rt.inbox[1][k]
    r.router_v[mt] = total
    rtt = small_tensor(rt, r.router_v.at[mt], lambda k: r.router_v.at[mt])
    start(rtt)

    to_stage4(FFN)
    to_stage3(OUT)
    to_stage4(DOWN)
    to_stage4(OUT)
    to_stage3(ATT)
    arrive(g1)
    total = gn.second[...]
    for k in range(outer - 1):
        total = total + gn.inbox[1][k]
    r.gains_v[...] = total
    write_out(r.gains_v, r.gains)
    arrive(rtt)
    write_out(r.router_v, r.router)
    to_stage4(ATT)
    for p in range(4):
        arrive(stage4(p))
        write_out(r.full[p], r.pieces[p])

    for copy in outs:
        copy.wait()

    for g in (ag_xa, ag_cot, ag_xf, ag_cb, ag_ga, rs1, rs2, rs3, rs4, rt0, rt1, rtt, gt, g0, g1):
        for copy in g:
            copy.wait_send()
    for p in range(4):
        for stage in (stage1, stage2, stage3, stage4):
            for copy in stage(p):
                copy.wait_send()


def finish_kernel(r):
    copies = []

    def put(src, dst):
        copy = pltpu.make_async_copy(src, dst, r.sem.at[len(copies)])
        copy.start()
        copies.append(copy)
        return copy

    loads = [
        put(src, dst)
        for src, dst in (
            (r.ffn, r.v_ffn), (r.down, r.v_down), (r.wo, r.v_wo), (r.att, r.v_att),
            (r.router, r.v_router), (r.output, r.v_output), (r.grad_in, r.v_grad_in), (r.gains, r.v_gains),
        )
    ]
    experts = r.o_gate.shape[0]
    hidden = r.o_gate.shape[2]
    loads[0].wait()
    for e in range(experts):
        r.t_gate[e] = r.v_ffn[:, e * hidden:(e + 1) * hidden].astype(F32)
    put(r.t_gate, r.o_gate)
    for e in range(experts):
        at = (experts + e) * hidden
        r.t_up[e] = r.v_ffn[:, at:at + hidden].astype(F32)
    put(r.t_up, r.o_up)
    for load, src, dst, out in (
        (loads[1], r.v_down, r.t_down, r.o_down), (loads[2], r.v_wo, r.t_wo, r.o_wo)
    ):
        load.wait()
        rows, cols = dst.shape[0], src.shape[1]
        for i in range(src.shape[0] // rows):
            dst[:, i * cols:(i + 1) * cols] = src[i * rows:(i + 1) * rows, :].astype(F32)
        put(dst, out)
    loads[3].wait()
    at = 0
    for dst, out in ((r.t_wq, r.o_wq), (r.t_wk, r.o_wk), (r.t_wv, r.o_wv)):
        cols = dst.shape[1]
        dst[...] = r.v_att[:, at:at + cols].astype(F32)
        put(dst, out)
        at += cols
    for load in loads[4:]:
        load.wait()
    put(r.v_output, r.o_output)
    put(r.v_grad_in, r.o_grad_in)
    r.t_gain_ffn[...] = r.v_gains[0:1, :]
    r.t_gain_attn[...] = r.v_gains[1:2, :]
    put(r.t_gain_ffn, r.o_gain_ffn)
    put(r.t_gain_attn, r.o_gain_attn)
    cols = r.v_router.shape[2]
    for i in range(r.v_router.shape[0]):
        r.t_router[:, i * cols:(i + 1) * cols] = r.v_router[i]
    put(r.t_router, r.o_router)
    for copy in copies[len(loads):]:
        copy.wait()


def rotary_tables(rows):
    half = HEAD_SIZE // 2
    freq = THETA ** (-(np.arange(half, dtype=np.float64) * 2.0 / HEAD_SIZE))
    angles = np.arange(rows, dtype=np.float64)[:, None] * freq[None, :]
    cos, sin = np.cos(angles), np.sin(angles)
    cos = np.concatenate([cos] * 4, axis=1).astype(np.float32)
    sin = np.concatenate([-sin, sin] * 2, axis=1).astype(np.float32)
    return jnp.asarray(cos), jnp.asarray(sin)


def on_device(
    hidden_in,
    cotangent,
    segments,
    routes,
    gain_attn,
    w_query,
    key_matrix,
    value_matrix,
    attention_output_weight,
    gain_ffn,
    w_router,
    w_gate,
    w_up,
    w_down,
):
    n = lax.axis_size("dp")
    inner = math.isqrt(n)
    outer = n // inner
    R, W = hidden_in.shape
    S = segments.shape[1]
    E = w_router.shape[1]
    depth = W // n
    head_cols = attention_output_weight.shape[0]
    down_rows = w_down.shape[0] * w_down.shape[1]
    cos, sin = rotary_tables(S)
    orders = (True, True, True, True)
    piece_cols = (512, 256, 256, 512)

    hbm = pl.BlockSpec(memory_space=pl.ANY)
    vmem = pl.BlockSpec(memory_space=pltpu.VMEM)
    in_hbm = dict(
        hidden_hbm=hidden_in,
        cot_hbm=cotangent,
        wq_hbm=w_query,
        wk_hbm=key_matrix,
        wv_hbm=value_matrix,
        cos_hbm=cos,
        sin_hbm=sin,
        wo_hbm=attention_output_weight,
        wg_hbm=w_gate,
        wu_hbm=w_up,
        wd_hbm=w_down.reshape(down_rows, W),
    )
    in_vmem = dict(
        seg=segments,
        routes=routes.T,
        gain_attn=gain_attn.reshape(1, W),
        gain_ffn=gain_ffn.reshape(1, W),
        wr=w_router.T,
    )
    shape = jax.ShapeDtypeStruct
    results = dict(
        output=shape((R, W), BF16),
        grad_in=shape((R, W), F32),
        gains=shape((2, W), F32),
        router=shape((4, E, W // 4), F32),
        pieces=[shape((n, depth, c), BF16) for c in piece_cols],
    )

    dma = pltpu.SemaphoreType.DMA
    half = functools.partial(pltpu.VMEM, dtype=BF16)
    full = functools.partial(pltpu.VMEM, dtype=F32)

    def small(rows, cols):
        return dict(
            own=full((rows, cols)),
            first=full((rows, cols)),
            second=full((rows, cols)),
            inbox=[full((size, rows, cols)) for size in (inner - 1, outer - 1, 3)],
            send=[dma((size,)) for size in (inner - 1, outer - 1, 3)],
            recv=[dma((size,)) for size in (inner - 1, outer - 1, 3)],
        )

    split = [piece_order(n, inner, order) for order in orders]
    sizes = [(na, nb, c) for (na, nb), c in zip(split, piece_cols)]
    sums = (W, W + LANES, W, W)
    scratch = dict(
        hid=half((R, W)),
        cot=half((S, W)),
        wqkv=half((W, 512)),
        cos=full((S, LANES)),
        sin=full((S, LANES)),
        wo=half((head_cols, W)),
        wgu=half((W, 512)),
        wd=half((down_rows, W)),
        xa=half((S, W)),
        xf=half((S, W)),
        cb=half((S, LANES)),
        ga=half((S, W + LANES)),
        q=half((S, 256)),
        qp=half((4, 4 * R, LANES)),
        klh=half((4, S, LANES)),
        vlh=half((4, S, LANES)),
        prob=half((4, 4 * R, 3 * R)),
        ds=half((4 * R, 3 * R)),
        gmp=half((4 * R, LANES)),
        mixed=half((S, head_cols)),
        part=full((R, W)),
        after=full((R, W)),
        rprobs=full((R, E)),
        counts=full((R, E)),
        ci=half((S, down_rows)),
        dgu=half((S, 512)),
        pr=full((S, W + LANES)),
        ga_own=full((R, W)),
        gk=full((S, LANES)),
        gv=full((S, LANES)),
        dqkv=half((S, 512)),
        gn=small(2, W),
        rt=small(E, W // 4),
        output_v=half((R, W)),
        grad_in_v=full((R, W)),
        gains_v=full((2, W)),
        router_v=full((4, E, W // 4)),
        full=[half((n, depth, c)) for c in piece_cols],
        load_sem=dma((13,)),
        out_sem=dma((8,)),
        ag_send=dma((5, 3)),
        ag_recv=dma((5, 3)),
        rs_send=dma((4, 3)),
        rs_recv=dma((4, 3)),
        sb=[half((2, R, c)) for c in sums],
        sx=[half((R, c)) for c in sums],
        rp=[half((2, R, c)) for c in sums],
        rx=[half((R, c)) for c in sums],
        loc=[half((n, depth, c)) for c in piece_cols],
        first=[half((na - 1, nb, depth, c)) for na, nb, c in sizes],
        held=[half((nb, depth, c)) for na, nb, c in sizes],
        second=[half((nb - 1, depth, c)) for na, nb, c in sizes],
        s1=[dma((na - 1,)) for na, nb, c in sizes],
        r1=[dma((na - 1,)) for na, nb, c in sizes],
        s2=[dma((nb - 1,)) for na, nb, c in sizes],
        r2=[dma((nb - 1,)) for na, nb, c in sizes],
        s3=[dma((nb - 1,)) for na, nb, c in sizes],
        r3=[dma((nb - 1,)) for na, nb, c in sizes],
        s4=[dma((na - 1,)) for na, nb, c in sizes],
        r4=[dma((na - 1,)) for na, nb, c in sizes],
    )

    def call(kernel, specs, operands, results, result_spec, scratch, params):
        given, in_tree = jax.tree.flatten(operands)
        shapes, out_tree = jax.tree.flatten(results)
        inner_shapes, scratch_tree = jax.tree.flatten(scratch)

        def body(*refs):
            a, b = len(given), len(given) + len(shapes)
            named = jax.tree.unflatten(in_tree, refs[:a])
            named.update(jax.tree.unflatten(out_tree, refs[a:b]))
            named.update(jax.tree.unflatten(scratch_tree, refs[b:]))
            kernel(SimpleNamespace(**named))

        got = pl.pallas_call(
            body,
            out_shape=shapes,
            in_specs=jax.tree.flatten(specs)[0],
            out_specs=[result_spec] * len(shapes),
            scratch_shapes=inner_shapes,
            compiler_params=params,
        )(*given)
        return SimpleNamespace(**jax.tree.unflatten(out_tree, got))

    specs = {key: hbm for key in in_hbm} | {key: vmem for key in in_vmem}
    got = call(
        functools.partial(layer_kernel, n, inner, orders),
        specs, in_hbm | in_vmem, results, hbm, scratch,
        pltpu.CompilerParams(collective_id=0, has_side_effects=True, vmem_limit_bytes=VMEM_LIMIT),
    )

    ready = dict(
        output=got.output,
        grad_in=got.grad_in,
        gains=got.gains,
        router=got.router,
        ffn=got.pieces[FFN].reshape(W, -1),
        down=got.pieces[DOWN].reshape(W, -1),
        wo=got.pieces[OUT].reshape(W, -1),
        att=got.pieces[ATT].reshape(W, -1),
    )
    finals = dict(
        o_output=shape((R, W), BF16),
        o_grad_in=shape((R, W), F32),
        o_gain_ffn=shape((1, W), F32),
        o_gain_attn=shape((1, W), F32),
        o_gate=shape(w_gate.shape, F32),
        o_up=shape(w_up.shape, F32),
        o_down=shape((down_rows, W), F32),
        o_wo=shape(attention_output_weight.shape, F32),
        o_wq=shape(w_query.shape, F32),
        o_wk=shape(key_matrix.shape, F32),
        o_wv=shape(value_matrix.shape, F32),
        o_router=shape((E, W), F32),
    )
    temps = dict(
        t_gate=full(w_gate.shape),
        t_up=full(w_up.shape),
        t_down=full((down_rows, W)),
        t_wo=full(attention_output_weight.shape),
        t_wq=full(w_query.shape),
        t_wk=full(key_matrix.shape),
        t_wv=full(value_matrix.shape),
        t_router=full((E, W)),
        v_ffn=half((W, piece_cols[FFN])),
        v_down=half((W, piece_cols[DOWN])),
        v_wo=half((W, piece_cols[OUT])),
        v_att=half((W, piece_cols[ATT])),
        v_router=full((4, E, W // 4)),
        v_output=half((R, W)),
        v_grad_in=full((R, W)),
        v_gains=full((2, W)),
        t_gain_ffn=full((1, W)),
        t_gain_attn=full((1, W)),
        sem=dma((len(finals) + 8,)),
    )
    done = call(
        finish_kernel, {key: hbm for key in ready}, ready, finals, hbm, temps,
        pltpu.CompilerParams(vmem_limit_bytes=VMEM_LIMIT),
    )
    return (
        done.o_output,
        done.o_grad_in,
        done.o_gain_attn.reshape(W),
        done.o_wq,
        done.o_wk,
        done.o_wv,
        done.o_wo,
        done.o_gain_ffn.reshape(W),
        done.o_router.T,
        done.o_gate,
        done.o_up,
        done.o_down.reshape(w_down.shape),
    )


def solution(mesh):
    rows = P(("dp", "tensor"), None)
    columns = P(None, "tensor")
    return jax.shard_map(
        on_device,
        mesh=mesh,
        in_specs=(
            rows, rows, P("dp", None), rows, P(), columns, columns, columns,
            P("tensor", None), P(), P(), P(None, None, "tensor"), P(None, None, "tensor"),
            P(None, "tensor", None),
        ),
        out_specs=(
            rows, rows, P(), columns, columns, columns, P("tensor", None), P(), P(),
            P(None, None, "tensor"), P(None, None, "tensor"), P(None, "tensor", None),
        ),
        check_vma=False,
    )
```

```python
import functools
import math
from types import SimpleNamespace

import jax
import jax.numpy as jnp
import numpy as np
from jax import lax
from jax.experimental import pallas as pl
from jax.experimental.pallas import tpu as pltpu
from jax.sharding import PartitionSpec as P

HEAD_SIZE = 64
LANES = 128
EPS = 1e-06
THETA = 10000.0
NEGATIVE = -1e30
MESH = pl.DeviceIdType.MESH
F32 = jnp.float32
BF16 = jnp.bfloat16

GATE, UP, DOWN, OUT, QUERY, KEYS = range(6)
INNER_FIRST = (True, False, True, True, True, False)
PIECE_COLS = 256
VMEM_LIMIT = 61 * 1024 * 1024


def nt(left, right):
    return lax.dot_general(left, right, (((1,), (1,)), ((), ())), preferred_element_type=F32)


def tn(left, right):
    return lax.dot_general(left, right, (((0,), (0,)), ((), ())), preferred_element_type=F32)


def nn(left, right):
    return jnp.dot(left, right, preferred_element_type=F32)


def layer_kernel(n, inner, orders, r):
    outer = n // inner
    me = lax.axis_index("dp")
    mt = lax.axis_index("tensor")
    y = me % inner
    z = me // inner
    xc = mt // 2
    core = mt % 2
    pair = xc * 2 + (1 - core)
    across = (1 - xc) * 2 + core

    R, W = r.hid.shape
    S = r.xa.shape[0]
    HC = r.wo.shape[0]

    def remote(src, dst, send, recv, device):
        return pltpu.make_async_remote_copy(
            src_ref=src, dst_ref=dst, send_sem=send, recv_sem=recv,
            device_id=device, device_id_type=MESH,
        )

    def block_of(k):
        return ((xc + 1 - k // 2) % 2) * 2 + (core + 1 - k % 2) % 2

    def rows_of(block):
        return pl.ds(pl.multiple_of(block * R, R), R)

    loads = [
        (r.hidden_hbm, r.hid),
        (r.cot_hbm, r.cot.at[rows_of(mt)]),
        (r.wq_hbm, r.wqkv.at[:, 0:256]),
        (r.wk_hbm, r.wqkv.at[:, 256:384]),
        (r.wv_hbm, r.wqkv.at[:, 384:512]),
        (r.cos_hbm, r.cos),
        (r.sin_hbm, r.sin),
        (r.wo_hbm, r.wo),
        (r.wg_hbm.at[0], r.wgu.at[:, 0:128]),
        (r.wg_hbm.at[1], r.wgu.at[:, 128:256]),
        (r.wu_hbm.at[0], r.wgu.at[:, 256:384]),
        (r.wu_hbm.at[1], r.wgu.at[:, 384:512]),
        (r.wd_hbm, r.wd),
        (r.wr_hbm, r.wr),
        (r.routes_hbm, r.routes),
        (r.gain_ffn_hbm, r.gain_ffn),
        (r.seg_hbm, r.seg),
        (r.gain_attn_hbm, r.gain_attn),
    ]
    load = [pltpu.make_async_copy(a, b, r.load_sem.at[i]) for i, (a, b) in enumerate(loads)]
    for copy in load:
        copy.start()

    barrier = pltpu.get_barrier_semaphore()
    for k in range(1, 4):
        pl.semaphore_signal(barrier, inc=1, device_id=(me, (mt + k) % 4), device_id_type=MESH)
    for k in range(1, inner):
        pl.semaphore_signal(
            barrier, inc=1, device_id=(z * inner + (y + k) % inner, mt), device_id_type=MESH
        )
    for k in range(1, outer):
        pl.semaphore_signal(
            barrier, inc=1, device_id=(((z + k) % outer) * inner + y, mt), device_id_type=MESH
        )

    def gather(i, buf):
        own = buf.at[rows_of(mt)]
        far = buf.at[rows_of(across)]
        ss, rs = r.ag_send, r.ag_recv
        return (
            remote(own, own, ss.at[i, 0], rs.at[i, 0], (me, across)),
            remote(own, own, ss.at[i, 1], rs.at[i, 1], (me, pair)),
            remote(far, far, ss.at[i, 2], rs.at[i, 2], (me, pair)),
        )

    def gather_start(g):
        g[0].start()
        g[1].start()

    def gather_step(k, *gs):
        @pl.when(k == 1)
        def _():
            for g in gs:
                g[1].wait_recv()

        @pl.when(k == 2)
        def _():
            for g in gs:
                g[0].wait_recv()
                g[2].start()

        @pl.when(k == 3)
        def _():
            for g in gs:
                g[2].wait_recv()

    def scatter(i, c):
        sb, sx, rp, rx = r.sb[i], r.sx[i], r.rp[i], r.rx[i]
        ss, rs = r.rs_send, r.rs_recv
        return (
            remote(sb.at[0], rp.at[0], ss.at[i, 0], rs.at[i, 0], (me, pair)),
            remote(sx, rx, ss.at[i, 1], rs.at[i, 1], (me, across)),
            remote(sb.at[1], rp.at[1], ss.at[i, 2], rs.at[i, 2], (me, pair)),
        )

    def scatter_step(k, i, c, part):
        sb, sx, rp = r.sb[i], r.sx[i], r.rp[i]

        @pl.when(k == 0)
        def _():
            sb[0] = part[...].astype(BF16)
            c[0].start()

        @pl.when(k == 1)
        def _():
            c[0].wait_recv()
            sx[...] = (part[...] + rp[0].astype(F32)).astype(BF16)
            c[1].start()

        @pl.when(k == 2)
        def _():
            sb[1] = part[...].astype(BF16)
            c[2].start()

    def start(copies):
        for copy in copies:
            copy.start()

    def arrive(copies):
        for copy in copies:
            copy.wait_recv()

    last = outer - 1
    ahead = ((z + 1) * inner + y, mt)
    behind = ((z - 1) * inner + y, mt)

    def chunk(p, j):
        if orders[p]:
            return pl.ds(y * outer + j, 1)
        return pl.ds(j * inner, inner)

    def partial(p, j):
        return r.held[p].at[pl.ds(j, 1)] if orders[p] else r.loc[p].at[chunk(p, j)]

    def chain_up(p, j):
        return remote(partial(p, j), r.up_in[p].at[j], r.c_su[p].at[j], r.c_ru[p].at[j], ahead)

    def chain_down(p, j):
        return remote(partial(p, j), r.down_in[p].at[j], r.c_sd[p].at[j], r.c_rd[p].at[j], behind)

    def spread_up(p, j):
        block = r.full[p].at[chunk(p, j)]
        return remote(block, block, r.g_su[p].at[j], r.g_r[p].at[j], ahead)

    def spread_down(p, j):
        block = r.full[p].at[chunk(p, j)]
        return remote(block, block, r.g_sd[p].at[j], r.g_r[p].at[j], behind)

    def chain_start(p):
        @pl.when(z == 0)
        def _():
            for d in range(last, 0, -1):
                chain_up(p, d).start()

        @pl.when(z == last)
        def _():
            for d in range(last, 0, -1):
                chain_down(p, last - d).start()

    def pass_on(copy, mine, came):
        copy.wait_recv()
        mine[...] = (mine[...].astype(F32) + came[...].astype(F32)).astype(BF16)
        copy.start()

    def chain_forward(p, hops):
        for hop in hops:
            @pl.when(z == hop)
            def _():
                for j in range(last, hop, -1):
                    pass_on(chain_up(p, j), partial(p, j), r.up_in[p].at[j])

            @pl.when(z == last - hop)
            def _():
                for j in range(last - hop):
                    pass_on(chain_down(p, j), partial(p, j), r.down_in[p].at[j])

    def chain_finish(p, dst):
        mine = partial(p, z)

        @pl.when(z == 0)
        def _():
            chain_down(p, z).wait_recv()
            dst[...] = (mine[...].astype(F32) + r.down_in[p][z].astype(F32)).astype(BF16)

        @pl.when(z == last)
        def _():
            chain_up(p, z).wait_recv()
            dst[...] = (mine[...].astype(F32) + r.up_in[p][z].astype(F32)).astype(BF16)

        @pl.when((z > 0) & (z < last))
        def _():
            chain_down(p, z).wait_recv()
            chain_up(p, z).wait_recv()
            dst[...] = (
                mine[...].astype(F32) + r.up_in[p][z].astype(F32) + r.down_in[p][z].astype(F32)
            ).astype(BF16)

    def spread_start(p):
        @pl.when(z < last)
        def _():
            spread_up(p, z).start()

        @pl.when(z > 0)
        def _():
            spread_down(p, z).start()

    def spread_forward(p, hops):
        for d in hops:
            @pl.when(z - d >= 0)
            def _():
                spread_up(p, z - d).wait_recv()

                @pl.when(z < last)
                def _():
                    spread_up(p, z - d).start()

            @pl.when(z + d < outer)
            def _():
                spread_down(p, z + d).wait_recv()

                @pl.when(z > 0)
                def _():
                    spread_down(p, z + d).start()

    def chain_sent(p):
        for d in range(1, outer):
            @pl.when(z + d < outer)
            def _():
                chain_up(p, z + d).wait_send()

            @pl.when(z - d >= 0)
            def _():
                chain_down(p, z - d).wait_send()

        for d in range(outer):
            @pl.when((z < last) & (z - d >= 0))
            def _():
                spread_up(p, z - d).wait_send()

            @pl.when((z > 0) & (z + d < outer))
            def _():
                spread_down(p, z + d).wait_send()

    def peers(p, src, dst, send, recv):
        return [
            remote(
                src((y + k) % inner), dst(k - 1), send[p].at[k - 1], recv[p].at[k - 1],
                (z * inner + (y + k) % inner, mt),
            )
            for k in range(1, inner)
        ]

    def inner_sum(p):
        if orders[p]:
            return peers(
                p, lambda to: r.loc[p].at[pl.ds(to * outer, outer)], lambda k: r.inbox[p].at[k], r.i_s, r.i_r
            )
        return peers(
            p, lambda to: r.held[p].at[pl.ds(to, 1)], lambda k: r.inbox[p].at[k], r.i_s, r.i_r
        )

    def inner_spread(p):
        if orders[p]:
            block = r.full[p].at[pl.ds(y * outer, outer)]
        else:
            block = r.full[p].at[pl.ds(z * inner + y, 1)]
        return peers(p, lambda to: block, lambda k: block, r.o_s, r.o_r)

    def advance(step, *which):
        for p in which:
            if orders[p]:
                inner_first_step(step, p)
            else:
                outer_first_step(step, p)

    sum_hops = np.array_split(np.arange(1, last), 2)
    spread_hops = np.array_split(np.arange(1, outer), 3)

    def inner_first_step(step, p):
        if step == 0:
            start(inner_sum(p))
        elif step == 1:
            arrive(inner_sum(p))
            acc = r.loc[p][pl.ds(y * outer, outer)].astype(F32)
            for k in range(inner - 1):
                acc = acc + r.inbox[p][k].astype(F32)
            r.held[p][...] = acc.astype(BF16)
            chain_start(p)
        elif step <= 3:
            chain_forward(p, sum_hops[step - 2].tolist())
        elif step == 4:
            chain_finish(p, r.full[p].at[chunk(p, z)])
            spread_start(p)
        elif step <= 7:
            spread_forward(p, spread_hops[step - 5].tolist())
            if step == 7:
                start(inner_spread(p))
        else:
            arrive(inner_spread(p))

    def outer_first_step(step, p):
        if step == 0:
            chain_start(p)
        elif step <= 2:
            chain_forward(p, sum_hops[step - 1].tolist())
        elif step == 3:
            chain_finish(p, r.held[p])
            start(inner_sum(p))
        elif step == 4:
            arrive(inner_sum(p))
            acc = r.held[p][pl.ds(y, 1)].astype(F32)
            for k in range(inner - 1):
                acc = acc + r.inbox[p][k].astype(F32)
            r.full[p][pl.ds(z * inner + y, 1)] = acc.astype(BF16)
            start(inner_spread(p))
        elif step == 5:
            arrive(inner_spread(p))
            spread_start(p)
        else:
            spread_forward(p, spread_hops[step - 6].tolist())

    outs = []

    def write_out(src, dst):
        copy = pltpu.make_async_copy(src, dst, r.out_sem.at[len(outs)])
        copy.start()
        outs.append(copy)

    def small_exchange(g, src, axis):
        size = outer if axis else inner
        out = []
        for k in range(1, size):
            if axis:
                to = ((z + k) % outer) * inner + y
            else:
                to = z * inner + (y + k) % inner
            out.append(remote(
                src, g.inbox[axis].at[k - 1], g.send[axis].at[k - 1], g.recv[axis].at[k - 1], (to, mt)
            ))
        return out

    def small_tensor(g, src, slots):
        return [
            remote(
                src, slots(k), g.send[2].at[k - 1], g.recv[2].at[k - 1], (me, (mt + k) % 4)
            )
            for k in range(1, 4)
        ]

    gn, rt = SimpleNamespace(**r.gn), SimpleNamespace(**r.rt)
    lane = lax.broadcasted_iota(jnp.int32, (R, LANES), 1)
    low = lane < HEAD_SIZE
    first_half = (lane % HEAD_SIZE) < HEAD_SIZE // 2

    def swap(v):
        return jnp.where(first_half, pltpu.roll(v, 96, 1), pltpu.roll(v, 32, 1))

    CH = 32

    def row_chunks(body):
        def step(i, _):
            body(pl.ds(pl.multiple_of(i * CH, CH), CH))
            return 0

        lax.fori_loop(0, R // CH, step, 0)

    def own_chunk(rows):
        return pl.ds(pl.multiple_of(mt * R + rows.start, CH), CH)

    load[0].wait()
    load[17].wait()

    def norm_rows(rows):
        h = r.hid[rows, :].astype(F32)
        inv = lax.rsqrt(jnp.mean(h * h, axis=-1, keepdims=True) + EPS)
        r.xa[own_chunk(rows), :] = (h * inv * r.gain_attn[...]).astype(BF16)

    row_chunks(norm_rows)

    pl.semaphore_wait(barrier, 3 + (inner - 1) + (outer - 1))

    ag_xa = gather(0, r.xa)
    gather_start(ag_xa)
    load[1].wait()
    ag_cot = gather(1, r.cot)
    ag_cot[1].start()
    for copy in load[2:7] + load[16:17]:
        copy.wait()

    r.gk[...] = jnp.zeros_like(r.gk)
    r.gv[...] = jnp.zeros_like(r.gv)
    gn.own[...] = jnp.zeros_like(gn.own)

    def project(k, _):
        gather_step(k, ag_xa)
        b = block_of(3 - k)
        rows = rows_of(b)
        qkv = nn(r.xa[rows, :], r.wqkv[...])
        cos, sin = r.cos[rows, :], r.sin[rows, :]

        def rope(v):
            return v * cos + swap(v) * sin

        zero = jnp.zeros((R, LANES), F32)
        q0 = rope(qkv[:, 0:128]) * HEAD_SIZE ** (-0.5)
        q1 = rope(qkv[:, 128:256]) * HEAD_SIZE ** (-0.5)
        kk = rope(qkv[:, 256:384])
        vv = qkv[:, 384:512]
        r.q[rows, 0:128] = q0.astype(BF16)
        r.q[rows, 128:256] = q1.astype(BF16)
        r.qp[b, 0 * R:1 * R, :] = jnp.where(low, q0, zero).astype(BF16)
        r.qp[b, 1 * R:2 * R, :] = jnp.where(low, pltpu.roll(q0, 64, 1), zero).astype(BF16)
        r.qp[b, 2 * R:3 * R, :] = jnp.where(low, zero, pltpu.roll(q1, 64, 1)).astype(BF16)
        r.qp[b, 3 * R:4 * R, :] = jnp.where(low, zero, q1).astype(BF16)
        for dst, val in ((r.klh, kk), (r.vlh, vv)):
            turned = pltpu.roll(val, 64, 1)
            dst[0, rows, :] = jnp.where(low, val, zero).astype(BF16)
            dst[1, rows, :] = jnp.where(low, zero, turned).astype(BF16)
            dst[2, rows, :] = jnp.where(low, turned, zero).astype(BF16)
            dst[3, rows, :] = jnp.where(low, zero, val).astype(BF16)
        return 0

    lax.fori_loop(0, 4, project, 0)
    ag_cot[0].start()
    load[7].wait()

    KW = 3 * R
    rs1 = scatter(0, W)

    def attend(k, _):
        b = block_of(k)
        rows = rows_of(b)
        wstart = (b // 3) * R
        win = pl.ds(pl.multiple_of(wstart, R), KW)
        seg_q = r.seg[0:1, rows].astype(F32)
        seg_col = jnp.transpose(jnp.broadcast_to(seg_q, (R, R)))[:, 0:1]
        seg_k = r.seg[0:1, win].astype(F32)
        at_q = lax.broadcasted_iota(jnp.int32, (R, KW), 0) + (b * R - wstart)
        at_k = lax.broadcasted_iota(jnp.int32, (R, KW), 1)
        bias = jnp.where((seg_col == seg_k) & (at_k <= at_q), 0.0, NEGATIVE)
        for kv in range(2):
            q = r.q[rows, kv * LANES:(kv + 1) * LANES]
            mixed = jnp.zeros((R, LANES), F32)
            for h in range(2):
                i = kv * 2 + h
                s = nt(q, r.klh[i, win, :]) + bias
                e = jnp.exp(s - jnp.max(s, axis=-1, keepdims=True))
                prob = (e * (1.0 / jnp.sum(e, axis=-1, keepdims=True))).astype(BF16)
                r.prob[b, i * R:(i + 1) * R, :] = prob
                mixed = mixed + nn(prob, r.vlh[i, win, :])
            r.mixed[rows, kv * LANES:(kv + 1) * LANES] = mixed.astype(BF16)
        r.part[...] = nn(r.mixed[rows, :], r.wo[...])
        scatter_step(k, 0, rs1, r.part)
        return 0

    lax.fori_loop(0, 4, attend, 0)
    for copy in load[8:16]:
        copy.wait()
    rs1[2].wait_recv()
    rs1[1].wait_recv()

    def after_rows(rows):
        a = r.hid[rows, :].astype(F32) + (
            r.part[rows, :] + r.rp[0][1, rows, :].astype(F32) + r.rx[0][rows, :].astype(F32)
        )
        r.after[rows, :] = a
        inv = lax.rsqrt(jnp.mean(a * a, axis=-1, keepdims=True) + EPS)
        r.xf[own_chunk(rows), :] = (a * inv * r.gain_ffn[...]).astype(BF16)

    row_chunks(after_rows)
    ag_xf = gather(2, r.xf)
    gather_start(ag_xf)

    E = r.wr.shape[0]
    expert = lax.broadcasted_iota(jnp.int32, (R, E), 1)
    logits = nt(r.xf[rows_of(mt), :], r.wr[...])
    el = jnp.exp(logits - jnp.max(logits, axis=-1, keepdims=True))
    router_probs = el / jnp.sum(el, axis=-1, keepdims=True)
    routes = r.routes[...]

    def count(e):
        named = jnp.sum((routes == e).astype(F32), axis=0, keepdims=True)
        return jnp.transpose(jnp.broadcast_to(named, (R, R)))[:, 0:1]

    count0, count1 = count(0), count(1)
    counts = jnp.where(expert == 0, count0, jnp.where(expert == 1, count1, 0.0))
    r.rprobs[...] = router_probs
    r.counts[...] = counts
    r.cb[rows_of(mt), :] = jnp.zeros((R, LANES), BF16)
    r.cb[rows_of(mt), 0:E] = (router_probs * counts).astype(BF16)
    ag_cb = gather(3, r.cb)
    gather_start(ag_cb)

    ag_cot[1].wait_recv()
    ag_cot[0].wait_recv()
    ag_cot[2].start()
    H2 = r.wd.shape[0]

    def experts(k, _):
        gather_step(k, ag_xf, ag_cb)

        @pl.when(k == 3)
        def _():
            ag_cot[2].wait_recv()

        b = block_of(3 - k)
        rows = rows_of(b)
        gu = nn(r.xf[rows, :], r.wgu[...])
        down = nt(r.cot[rows, :], r.wd[...])
        cb = r.cb[rows, :].astype(F32)
        gcol = jnp.zeros((R, LANES), F32)
        for e in range(2):
            cols = slice(e * LANES, (e + 1) * LANES)
            up_cols = slice(H2 + e * LANES, H2 + (e + 1) * LANES)
            g, u, a = gu[:, cols], gu[:, up_cols], down[:, cols]
            c = cb[:, e:e + 1]
            sig = 1.0 / (1.0 + jnp.exp(-g))
            silu = g * sig
            act = silu * u
            ga = c * a
            r.ci[rows, cols] = (c * act).astype(BF16)
            r.dgu[rows, cols] = (ga * u * (sig * (1.0 + g * (1.0 - sig)))).astype(BF16)
            r.dgu[rows, up_cols] = (ga * silu).astype(BF16)
            gcol = jnp.where(lane == e, jnp.sum(act * a, axis=-1, keepdims=True), gcol)
        r.pr[rows, 0:W] = nt(r.dgu[rows, :], r.wgu[...])
        r.pr[rows, W:W + LANES] = gcol
        return 0

    lax.fori_loop(0, 4, experts, 0)
    rs2 = scatter(1, W + LANES)
    for k in (0, 2, 1):
        scatter_step(k, 1, rs2, r.pr.at[rows_of(block_of(k))])

    depth = W // n

    def store_piece(p, row, tile):
        count = tile.shape[0] // depth
        r.loc[p][pl.ds(row * count, count)] = tile.astype(BF16).reshape(count, depth, PIECE_COLS)

    def tiles(first, second, left, right):
        def step(i, _):
            cols = pl.ds(pl.multiple_of(i * 256, 256), 256)
            tile = tn(left[:, cols], right[...])
            store_piece(first, i, tile[:, 0:PIECE_COLS])
            store_piece(second, i, tile[:, PIECE_COLS:])
            return 0

        lax.fori_loop(0, W // 256, step, 0)
        advance(0, first, second)

    def tiles_by_columns(p, left, right):
        def step(i, _):
            cols = pl.ds(pl.multiple_of(i * 256, 256), 256)
            store_piece(p, i, tn(left[...], right[:, cols]))
            return 0

        lax.fori_loop(0, W // 256, step, 0)
        advance(0, p)

    tiles(GATE, UP, r.xf, r.dgu)
    tiles_by_columns(DOWN, r.ci, r.cot)

    rs2[2].wait_recv()
    rs2[1].wait_recv()
    own = rows_of(mt)
    gcomb = (
        r.pr[own, W:W + LANES]
        + r.rp[1][1, :, W:W + LANES].astype(F32)
        + r.rx[1][:, W:W + LANES].astype(F32)
    )[:, 0:E]
    grp = gcomb * r.counts[...]
    rp = r.rprobs[...]
    glog = (rp * (grp - jnp.sum(rp * grp, axis=-1, keepdims=True))).astype(BF16)
    r.ga[own, W:W + LANES] = jnp.zeros((R, LANES), BF16)
    r.ga[own, W:W + E] = glog
    r.part[...] = nn(glog, r.wr[...])

    def grad_after_rows(rows):
        a = r.after[rows, :]
        inv = lax.rsqrt(jnp.mean(a * a, axis=-1, keepdims=True) + EPS)
        unit = a * inv
        g = (
            r.part[rows, :]
            + r.pr[own_chunk(rows), 0:W]
            + r.rp[1][1, rows, 0:W].astype(F32)
            + r.rx[1][rows, 0:W].astype(F32)
        )
        gn.own[0:1, :] += jnp.sum(g * unit, axis=0, keepdims=True)
        scaled = g * r.gain_ffn[...]
        back = inv * (scaled - unit * jnp.mean(scaled * unit, axis=-1, keepdims=True))
        ga = back + r.cot[own_chunk(rows), :].astype(F32)
        r.ga_own[rows, :] = ga
        r.ga[own_chunk(rows), 0:W] = ga.astype(BF16)

    row_chunks(grad_after_rows)
    ag_ga = gather(4, r.ga)
    gather_start(ag_ga)
    advance(1, GATE, UP)

    def attend_back(k, _):
        @pl.when(k == 2)
        def _():
            advance(2, GATE, UP)
            advance(1, DOWN)

        gather_step(k, ag_ga)

        @pl.when(k == 3)
        def _():
            advance(3, GATE, UP)

        b = block_of(3 - k)
        rows = rows_of(b)
        wstart = (b // 3) * R
        win = pl.ds(pl.multiple_of(wstart, R), KW)
        gm = nt(r.ga[rows, 0:W], r.wo[...])
        zero = jnp.zeros((R, LANES), F32)
        for kv in range(2):
            cols = slice(kv * LANES, (kv + 1) * LANES)
            gmk = gm[:, cols].astype(BF16)
            gmf = gmk.astype(F32)
            turned = pltpu.roll(gmf, 64, 1)
            if kv == 0:
                r.gmp[0 * R:1 * R, :] = jnp.where(low, gmf, zero).astype(BF16)
                r.gmp[1 * R:2 * R, :] = jnp.where(low, turned, zero).astype(BF16)
            else:
                r.gmp[2 * R:3 * R, :] = jnp.where(low, zero, turned).astype(BF16)
                r.gmp[3 * R:4 * R, :] = jnp.where(low, zero, gmf).astype(BF16)
            prod = gmf * r.mixed[rows, cols].astype(F32)
            delta_lo = jnp.sum(jnp.where(low, prod, zero), axis=-1, keepdims=True)
            delta_hi = jnp.sum(jnp.where(low, zero, prod), axis=-1, keepdims=True)
            gq = zero
            for h, delta in ((0, delta_lo), (1, delta_hi)):
                i = kv * 2 + h
                head = slice(i * R, (i + 1) * R)
                dp = nt(gmk, r.vlh[i, win, :])
                ds = (r.prob[b, head, :].astype(F32) * (dp - delta)).astype(BF16)
                r.ds[head, :] = ds
                gq = gq + nn(ds, r.klh[i, win, :])
            gq = gq * HEAD_SIZE ** (-0.5)
            gq = gq * r.cos[rows, :] - swap(gq) * r.sin[rows, :]
            r.dqkv[rows, cols] = gq.astype(BF16)
        r.gk[win, :] += tn(r.ds[...], r.qp[b])
        r.gv[win, :] += tn(r.prob[b], r.gmp[...])
        return 0

    lax.fori_loop(0, 4, attend_back, 0)
    advance(4, GATE, UP)
    advance(2, DOWN)


    def finish_kv(k, _):
        rows = rows_of(k)
        gk = r.gk[rows, :]
        gk = gk * r.cos[rows, :] - swap(gk) * r.sin[rows, :]
        r.dqkv[rows, 256:384] = gk.astype(BF16)
        r.dqkv[rows, 384:512] = r.gv[rows, :].astype(BF16)
        return 0

    lax.fori_loop(0, 4, finish_kv, 0)
    tiles(QUERY, KEYS, r.xa, r.dqkv)
    tiles_by_columns(OUT, r.mixed, r.ga)
    advance(5, GATE, UP)
    advance(3, DOWN)
    rs3 = scatter(2, W)

    def input_part(k, _):
        r.part[...] = nt(r.dqkv[rows_of(block_of(k)), :], r.wqkv[...])
        scatter_step(k, 2, rs3, r.part)
        return 0

    lax.fori_loop(0, 4, input_part, 0)
    advance(6, GATE, UP)
    advance(4, DOWN)
    quarter = pl.ds(pl.multiple_of(mt * (W // 4), W // 4), W // 4)
    rt.own[...] = tn(r.ga[:, W:W + LANES], r.xf[:, quarter])[0:E, :]
    rt0 = small_exchange(rt, rt.own, 0)
    start(rt0)

    advance(1, QUERY, KEYS, OUT)
    advance(7, GATE, UP)
    advance(5, DOWN)
    rs3[2].wait_recv()
    rs3[1].wait_recv()

    def grad_in_rows(rows):
        h = r.hid[rows, :].astype(F32)
        inv = lax.rsqrt(jnp.mean(h * h, axis=-1, keepdims=True) + EPS)
        unit = h * inv
        g = r.part[rows, :] + r.rp[2][1, rows, :].astype(F32) + r.rx[2][rows, :].astype(F32)
        gn.own[1:2, :] += jnp.sum(g * unit, axis=0, keepdims=True)
        scaled = g * r.gain_attn[...]
        back = inv * (scaled - unit * jnp.mean(scaled * unit, axis=-1, keepdims=True))
        r.grad_in_v[rows, :] = back + r.ga_own[rows, :]

    row_chunks(grad_in_rows)
    write_out(r.grad_in_v, r.grad_in)
    gt = small_tensor(gn, gn.own, lambda k: gn.inbox[2].at[k - 1])
    start(gt)
    advance(2, QUERY, KEYS, OUT)
    advance(6, DOWN)
    advance(8, UP)

    rs4 = scatter(3, W)

    def output_part(k, _):
        r.part[...] = nn(r.ci[rows_of(block_of(k)), :], r.wd[...])
        scatter_step(k, 3, rs4, r.part)
        return 0

    lax.fori_loop(0, 4, output_part, 0)
    advance(3, QUERY, KEYS, OUT)
    advance(7, DOWN)

    arrive(gt)
    total = gn.own[...]
    for k in range(3):
        total = total + gn.inbox[2][k]
    gn.first[...] = total
    g0 = small_exchange(gn, gn.first, 0)
    start(g0)
    arrive(rt0)
    total = rt.own[...]
    for k in range(inner - 1):
        total = total + rt.inbox[0][k]
    rt.first[...] = total
    rt1 = small_exchange(rt, rt.first, 1)
    start(rt1)
    advance(4, QUERY, KEYS, OUT)

    rs4[2].wait_recv()
    rs4[1].wait_recv()

    def output_rows(rows):
        a = r.part[rows, :] + r.rp[3][1, rows, :].astype(F32) + r.rx[3][rows, :].astype(F32)
        r.output_v[rows, :] = (r.after[rows, :] + a).astype(BF16)

    row_chunks(output_rows)
    write_out(r.output_v, r.output)
    advance(5, QUERY, KEYS, OUT)

    arrive(g0)
    total = gn.first[...]
    for k in range(inner - 1):
        total = total + gn.inbox[0][k]
    gn.second[...] = total
    g1 = small_exchange(gn, gn.second, 1)
    start(g1)
    arrive(rt1)
    total = rt.first[...]
    for k in range(outer - 1):
        total = total + rt.inbox[1][k]
    r.router_v[mt] = total
    rtt = small_tensor(rt, r.router_v.at[mt], lambda k: r.router_v.at[mt])
    start(rtt)
    advance(6, QUERY, KEYS, OUT)

    arrive(g1)
    total = gn.second[...]
    for k in range(outer - 1):
        total = total + gn.inbox[1][k]
    r.gains_v[...] = total
    write_out(r.gains_v, r.gains)
    arrive(rtt)
    write_out(r.router_v, r.router)
    advance(7, QUERY, KEYS, OUT)
    for p in (UP, GATE, DOWN, KEYS, QUERY, OUT):
        if p != UP:
            advance(8, p)
        write_out(r.full[p], r.pieces[p])

    for copy in outs:
        copy.wait()

    for g in (ag_xa, ag_cot, ag_xf, ag_cb, ag_ga, rs1, rs2, rs3, rs4, rt0, rt1, rtt, gt, g0, g1):
        for copy in g:
            copy.wait_send()
    for p in range(6):
        chain_sent(p)
        for copy in inner_sum(p) + inner_spread(p):
            copy.wait_send()


def finish_kernel(r):
    copies = []

    def put(src, dst):
        copy = pltpu.make_async_copy(src, dst, r.sem.at[len(copies)])
        copy.start()
        copies.append(copy)
        return copy

    loads = [
        put(src, dst)
        for src, dst in list(zip(r.pieces, r.v_pieces))
        + [(r.router, r.v_router), (r.output, r.v_output), (r.grad_in, r.v_grad_in), (r.gains, r.v_gains)]
    ]
    experts, _, hidden = r.o_gate.shape
    for p, dst, out in ((GATE, r.t_gate, r.o_gate), (UP, r.t_up, r.o_up)):
        loads[p].wait()
        for e in range(experts):
            dst[e] = r.v_pieces[p][:, e * hidden:(e + 1) * hidden].astype(F32)
        put(dst, out)
    for p, dst, out in ((DOWN, r.t_down, r.o_down), (OUT, r.t_wo, r.o_wo)):
        loads[p].wait()
        rows, cols = dst.shape[0], PIECE_COLS
        for i in range(r.v_pieces[p].shape[0] // rows):
            dst[:, i * cols:(i + 1) * cols] = r.v_pieces[p][i * rows:(i + 1) * rows, :].astype(F32)
        put(dst, out)
    loads[QUERY].wait()
    r.t_wq[...] = r.v_pieces[QUERY][...].astype(F32)
    put(r.t_wq, r.o_wq)
    loads[KEYS].wait()
    cols = r.t_wk.shape[1]
    r.t_wk[...] = r.v_pieces[KEYS][:, 0:cols].astype(F32)
    put(r.t_wk, r.o_wk)
    r.t_wv[...] = r.v_pieces[KEYS][:, cols:2 * cols].astype(F32)
    put(r.t_wv, r.o_wv)
    for load in loads[KEYS + 1:]:
        load.wait()
    put(r.v_output, r.o_output)
    put(r.v_grad_in, r.o_grad_in)
    r.t_gain_ffn[...] = r.v_gains[0:1, :]
    r.t_gain_attn[...] = r.v_gains[1:2, :]
    put(r.t_gain_ffn, r.o_gain_ffn)
    put(r.t_gain_attn, r.o_gain_attn)
    cols = r.v_router.shape[2]
    for i in range(r.v_router.shape[0]):
        r.t_router[:, i * cols:(i + 1) * cols] = r.v_router[i]
    put(r.t_router, r.o_router)
    for copy in copies[len(loads):]:
        copy.wait()


def rotary_tables(rows):
    half = HEAD_SIZE // 2
    freq = THETA ** (-(np.arange(half, dtype=np.float64) * 2.0 / HEAD_SIZE))
    angles = np.arange(rows, dtype=np.float64)[:, None] * freq[None, :]
    cos, sin = np.cos(angles), np.sin(angles)
    cos = np.concatenate([cos] * 4, axis=1).astype(np.float32)
    sin = np.concatenate([-sin, sin] * 2, axis=1).astype(np.float32)
    return jnp.asarray(cos), jnp.asarray(sin)


def on_device(
    hidden_in,
    cotangent,
    segments,
    routes,
    gain_attn,
    w_query,
    key_matrix,
    value_matrix,
    attention_output_weight,
    gain_ffn,
    w_router,
    w_gate,
    w_up,
    w_down,
):
    n = lax.axis_size("dp")
    inner = math.isqrt(n)
    outer = n // inner
    R, W = hidden_in.shape
    S = segments.shape[1]
    E = w_router.shape[1]
    depth = W // n
    head_cols = attention_output_weight.shape[0]
    down_rows = w_down.shape[0] * w_down.shape[1]
    cos, sin = rotary_tables(S)
    orders = INNER_FIRST
    piece_cols = (PIECE_COLS,) * len(orders)

    hbm = pl.BlockSpec(memory_space=pl.ANY)
    in_hbm = dict(
        hidden_hbm=hidden_in,
        cot_hbm=cotangent,
        wq_hbm=w_query,
        wk_hbm=key_matrix,
        wv_hbm=value_matrix,
        cos_hbm=cos,
        sin_hbm=sin,
        wo_hbm=attention_output_weight,
        wg_hbm=w_gate,
        wu_hbm=w_up,
        wd_hbm=w_down.reshape(down_rows, W),
        seg_hbm=segments,
        routes_hbm=routes.T,
        gain_attn_hbm=gain_attn.reshape(1, W),
        gain_ffn_hbm=gain_ffn.reshape(1, W),
        wr_hbm=w_router.T,
    )
    shape = jax.ShapeDtypeStruct
    results = dict(
        output=shape((R, W), BF16),
        grad_in=shape((R, W), F32),
        gains=shape((2, W), F32),
        router=shape((4, E, W // 4), F32),
        pieces=[shape((n, depth, c), BF16) for c in piece_cols],
    )

    dma = pltpu.SemaphoreType.DMA
    half = functools.partial(pltpu.VMEM, dtype=BF16)
    full = functools.partial(pltpu.VMEM, dtype=F32)

    def small(rows, cols):
        return dict(
            own=full((rows, cols)),
            first=full((rows, cols)),
            second=full((rows, cols)),
            inbox=[full((size, rows, cols)) for size in (inner - 1, outer - 1, 3)],
            send=[dma((size,)) for size in (inner - 1, outer - 1, 3)],
            recv=[dma((size,)) for size in (inner - 1, outer - 1, 3)],
        )

    sizes = [(1, outer, outer) if order else (inner, 1, inner) for order in orders]
    sums = (W, W + LANES, W, W)
    scratch = dict(
        hid=half((R, W)),
        cot=half((S, W)),
        wqkv=half((W, 512)),
        cos=full((S, LANES)),
        sin=full((S, LANES)),
        wo=half((head_cols, W)),
        wgu=half((W, 512)),
        wd=half((down_rows, W)),
        xa=half((S, W)),
        xf=half((S, W)),
        cb=half((S, LANES)),
        ga=half((S, W + LANES)),
        q=half((S, 256)),
        qp=half((4, 4 * R, LANES)),
        klh=half((4, S, LANES)),
        vlh=half((4, S, LANES)),
        prob=half((4, 4 * R, 3 * R)),
        ds=half((4 * R, 3 * R)),
        gmp=half((4 * R, LANES)),
        mixed=half((S, head_cols)),
        part=full((R, W)),
        after=full((R, W)),
        rprobs=full((R, E)),
        counts=full((R, E)),
        ci=half((S, down_rows)),
        dgu=half((S, 512)),
        pr=full((S, W + LANES)),
        ga_own=full((R, W)),
        gk=full((S, LANES)),
        gv=full((S, LANES)),
        dqkv=half((S, 512)),
        gn=small(2, W),
        rt=small(E, W // 4),
        output_v=half((R, W)),
        grad_in_v=full((R, W)),
        gains_v=full((2, W)),
        router_v=full((4, E, W // 4)),
        full=[half((n, depth, c)) for c in piece_cols],
        seg=pltpu.VMEM((1, S), jnp.int32),
        routes=pltpu.VMEM((routes.shape[1], R), jnp.int32),
        gain_attn=full((1, W)),
        gain_ffn=full((1, W)),
        wr=half((E, W)),
        load_sem=dma((18,)),
        out_sem=dma((10,)),
        ag_send=dma((5, 3)),
        ag_recv=dma((5, 3)),
        rs_send=dma((4, 3)),
        rs_recv=dma((4, 3)),
        sb=[half((2, R, c)) for c in sums],
        sx=[half((R, c)) for c in sums],
        rp=[half((2, R, c)) for c in sums],
        rx=[half((R, c)) for c in sums],
        loc=[half((n, depth, c)) for c in piece_cols],
        held=[half((kept, depth, PIECE_COLS)) for _, _, kept in sizes],
        up_in=[half((outer, part, depth, PIECE_COLS)) for part, _, _ in sizes],
        down_in=[half((outer, part, depth, PIECE_COLS)) for part, _, _ in sizes],
        inbox=[half((inner - 1, part, depth, PIECE_COLS)) for _, part, _ in sizes],
        c_su=[dma((outer,)) for _ in sizes],
        c_ru=[dma((outer,)) for _ in sizes],
        c_sd=[dma((outer,)) for _ in sizes],
        c_rd=[dma((outer,)) for _ in sizes],
        g_su=[dma((outer,)) for _ in sizes],
        g_sd=[dma((outer,)) for _ in sizes],
        g_r=[dma((outer,)) for _ in sizes],
        i_s=[dma((inner - 1,)) for _ in sizes],
        i_r=[dma((inner - 1,)) for _ in sizes],
        o_s=[dma((inner - 1,)) for _ in sizes],
        o_r=[dma((inner - 1,)) for _ in sizes],
    )

    def call(kernel, specs, operands, results, result_spec, scratch, params):
        given, in_tree = jax.tree.flatten(operands)
        shapes, out_tree = jax.tree.flatten(results)
        inner_shapes, scratch_tree = jax.tree.flatten(scratch)

        def body(*refs):
            a, b = len(given), len(given) + len(shapes)
            named = jax.tree.unflatten(in_tree, refs[:a])
            named.update(jax.tree.unflatten(out_tree, refs[a:b]))
            named.update(jax.tree.unflatten(scratch_tree, refs[b:]))
            kernel(SimpleNamespace(**named))

        got = pl.pallas_call(
            body,
            out_shape=shapes,
            in_specs=jax.tree.flatten(specs)[0],
            out_specs=[result_spec] * len(shapes),
            scratch_shapes=inner_shapes,
            compiler_params=params,
        )(*given)
        return SimpleNamespace(**jax.tree.unflatten(out_tree, got))

    specs = {key: hbm for key in in_hbm}
    got = call(
        functools.partial(layer_kernel, n, inner, orders),
        specs, in_hbm, results, hbm, scratch,
        pltpu.CompilerParams(collective_id=0, has_side_effects=True, vmem_limit_bytes=VMEM_LIMIT),
    )

    ready = dict(
        output=got.output,
        grad_in=got.grad_in,
        gains=got.gains,
        router=got.router,
        pieces=[piece.reshape(W, PIECE_COLS) for piece in got.pieces],
    )
    finals = dict(
        o_output=shape((R, W), BF16),
        o_grad_in=shape((R, W), F32),
        o_gain_ffn=shape((1, W), F32),
        o_gain_attn=shape((1, W), F32),
        o_gate=shape(w_gate.shape, F32),
        o_up=shape(w_up.shape, F32),
        o_down=shape((down_rows, W), F32),
        o_wo=shape(attention_output_weight.shape, F32),
        o_wq=shape(w_query.shape, F32),
        o_wk=shape(key_matrix.shape, F32),
        o_wv=shape(value_matrix.shape, F32),
        o_router=shape((E, W), F32),
    )
    temps = dict(
        t_gate=full(w_gate.shape),
        t_up=full(w_up.shape),
        t_down=full((down_rows, W)),
        t_wo=full(attention_output_weight.shape),
        t_wq=full(w_query.shape),
        t_wk=full(key_matrix.shape),
        t_wv=full(value_matrix.shape),
        t_router=full((E, W)),
        v_pieces=[half((W, PIECE_COLS)) for _ in piece_cols],
        v_router=full((4, E, W // 4)),
        v_output=half((R, W)),
        v_grad_in=full((R, W)),
        v_gains=full((2, W)),
        t_gain_ffn=full((1, W)),
        t_gain_attn=full((1, W)),
        sem=dma((len(finals) + 10,)),
    )
    done = call(
        finish_kernel, jax.tree.map(lambda _: hbm, ready), ready, finals, hbm, temps,
        pltpu.CompilerParams(vmem_limit_bytes=VMEM_LIMIT),
    )
    return (
        done.o_output,
        done.o_grad_in,
        done.o_gain_attn.reshape(W),
        done.o_wq,
        done.o_wk,
        done.o_wv,
        done.o_wo,
        done.o_gain_ffn.reshape(W),
        done.o_router.T,
        done.o_gate,
        done.o_up,
        done.o_down.reshape(w_down.shape),
    )


def solution(mesh):
    rows = P(("dp", "tensor"), None)
    columns = P(None, "tensor")
    return jax.shard_map(
        on_device,
        mesh=mesh,
        in_specs=(
            rows, rows, P("dp", None), rows, P(), columns, columns, columns,
            P("tensor", None), P(), P(), P(None, None, "tensor"), P(None, None, "tensor"),
            P(None, "tensor", None),
        ),
        out_specs=(
            rows, rows, P(), columns, columns, columns, P("tensor", None), P(), P(),
            P(None, None, "tensor"), P(None, None, "tensor"), P(None, "tensor", None),
        ),
        check_vma=False,
    )
```

```python
import functools
import math
from types import SimpleNamespace

import jax
import jax.numpy as jnp
import numpy as np
from jax import lax
from jax.experimental import pallas as pl
from jax.experimental.pallas import tpu as pltpu
from jax.sharding import PartitionSpec as P

HEAD_SIZE = 64
LANES = 128
EPS = 1e-06
THETA = 10000.0
NEGATIVE = -1e30
MESH = pl.DeviceIdType.MESH
F32 = jnp.float32
BF16 = jnp.bfloat16

GATE, UP, DOWN, OUT, QUERY, KEYS = range(6)
INNER_FIRST = (True, False, True, True, True, False)
PIECE_COLS = 256
VMEM_LIMIT = 61 * 1024 * 1024


def nt(left, right):
    return lax.dot_general(left, right, (((1,), (1,)), ((), ())), preferred_element_type=F32)


def tn(left, right):
    return lax.dot_general(left, right, (((0,), (0,)), ((), ())), preferred_element_type=F32)


def nn(left, right):
    return jnp.dot(left, right, preferred_element_type=F32)


def layer_kernel(n, inner, orders, r):
    outer = n // inner
    me = lax.axis_index("dp")
    mt = lax.axis_index("tensor")
    y = me % inner
    z = me // inner
    xc = mt // 2
    core = mt % 2
    pair = xc * 2 + (1 - core)
    across = (1 - xc) * 2 + core

    R, W = r.hid.shape
    S = r.xa.shape[0]
    HC = r.wo.shape[0]

    def remote(src, dst, send, recv, device):
        return pltpu.make_async_remote_copy(
            src_ref=src, dst_ref=dst, send_sem=send, recv_sem=recv,
            device_id=device, device_id_type=MESH,
        )

    def block_of(k):
        return ((xc + 1 - k // 2) % 2) * 2 + (core + 1 - k % 2) % 2

    def rows_of(block):
        return pl.ds(pl.multiple_of(block * R, R), R)

    loads = [
        (r.hidden_hbm, r.hid),
        (r.cot_hbm, r.cot.at[rows_of(mt)]),
        (r.wq_hbm, r.wqkv.at[:, 0:256]),
        (r.wk_hbm, r.wqkv.at[:, 256:384]),
        (r.wv_hbm, r.wqkv.at[:, 384:512]),
        (r.cos_hbm, r.cos),
        (r.sin_hbm, r.sin),
        (r.wo_hbm, r.wo),
        (r.wg_hbm.at[0], r.wgu.at[:, 0:128]),
        (r.wg_hbm.at[1], r.wgu.at[:, 128:256]),
        (r.wu_hbm.at[0], r.wgu.at[:, 256:384]),
        (r.wu_hbm.at[1], r.wgu.at[:, 384:512]),
        (r.wd_hbm, r.wd),
        (r.wr_hbm, r.wr),
        (r.routes_hbm, r.routes),
        (r.gain_ffn_hbm, r.gain_ffn),
        (r.seg_hbm, r.seg),
        (r.gain_attn_hbm, r.gain_attn),
    ]
    load = [pltpu.make_async_copy(a, b, r.load_sem.at[i]) for i, (a, b) in enumerate(loads)]
    for copy in load:
        copy.start()

    barrier = pltpu.get_barrier_semaphore()
    for k in range(1, 4):
        pl.semaphore_signal(barrier, inc=1, device_id=(me, (mt + k) % 4), device_id_type=MESH)
    for k in range(1, inner):
        pl.semaphore_signal(
            barrier, inc=1, device_id=(z * inner + (y + k) % inner, mt), device_id_type=MESH
        )
    for k in range(1, outer):
        pl.semaphore_signal(
            barrier, inc=1, device_id=(((z + k) % outer) * inner + y, mt), device_id_type=MESH
        )

    def gather(i, buf):
        own = buf.at[rows_of(mt)]
        far = buf.at[rows_of(across)]
        ss, rs = r.ag_send, r.ag_recv
        return (
            remote(own, own, ss.at[i, 0], rs.at[i, 0], (me, across)),
            remote(own, own, ss.at[i, 1], rs.at[i, 1], (me, pair)),
            remote(far, far, ss.at[i, 2], rs.at[i, 2], (me, pair)),
        )

    def gather_start(g):
        g[0].start()
        g[1].start()

    def gather_step(k, *gs):
        @pl.when(k == 1)
        def _():
            for g in gs:
                g[1].wait_recv()

        @pl.when(k == 2)
        def _():
            for g in gs:
                g[0].wait_recv()
                g[2].start()

        @pl.when(k == 3)
        def _():
            for g in gs:
                g[2].wait_recv()

    def scatter(i, c):
        sb, sx, rp, rx = r.sb[i], r.sx[i], r.rp[i], r.rx[i]
        ss, rs = r.rs_send, r.rs_recv
        return (
            remote(sb.at[0], rp.at[0], ss.at[i, 0], rs.at[i, 0], (me, pair)),
            remote(sx, rx, ss.at[i, 1], rs.at[i, 1], (me, across)),
            remote(sb.at[1], rp.at[1], ss.at[i, 2], rs.at[i, 2], (me, pair)),
        )

    def scatter_step(k, i, c, part):
        sb, sx, rp = r.sb[i], r.sx[i], r.rp[i]

        @pl.when(k == 0)
        def _():
            sb[0] = part[...].astype(BF16)
            c[0].start()

        @pl.when(k == 1)
        def _():
            c[0].wait_recv()
            sx[...] = (part[...] + rp[0].astype(F32)).astype(BF16)
            c[1].start()

        @pl.when(k == 2)
        def _():
            sb[1] = part[...].astype(BF16)
            c[2].start()

    def start(copies):
        for copy in copies:
            copy.start()

    def arrive(copies):
        for copy in copies:
            copy.wait_recv()

    last = outer - 1
    ahead = ((z + 1) * inner + y, mt)
    behind = ((z - 1) * inner + y, mt)

    def chunk(p, j):
        if orders[p]:
            return pl.ds(y * outer + j, 1)
        return pl.ds(j * inner, inner)

    def partial(p, j):
        return r.held[p].at[pl.ds(j, 1)] if orders[p] else r.loc[p].at[chunk(p, j)]

    def chain_up(p, j):
        return remote(partial(p, j), r.up_in[p].at[j], r.c_su[p].at[j], r.c_ru[p].at[j], ahead)

    def chain_down(p, j):
        return remote(partial(p, j), r.down_in[p].at[j], r.c_sd[p].at[j], r.c_rd[p].at[j], behind)

    def spread_up(p, j):
        block = r.full[p].at[chunk(p, j)]
        return remote(block, block, r.g_su[p].at[j], r.g_r[p].at[j], ahead)

    def spread_down(p, j):
        block = r.full[p].at[chunk(p, j)]
        return remote(block, block, r.g_sd[p].at[j], r.g_r[p].at[j], behind)

    def chain_start(p):
        @pl.when(z == 0)
        def _():
            for d in range(last, 0, -1):
                chain_up(p, d).start()

        @pl.when(z == last)
        def _():
            for d in range(last, 0, -1):
                chain_down(p, last - d).start()

    def pass_on(copy, mine, came):
        copy.wait_recv()
        mine[...] = (mine[...].astype(F32) + came[...].astype(F32)).astype(BF16)
        copy.start()

    def chain_forward(p, hops):
        for hop in hops:
            @pl.when(z == hop)
            def _():
                for j in range(last, hop, -1):
                    pass_on(chain_up(p, j), partial(p, j), r.up_in[p].at[j])

            @pl.when(z == last - hop)
            def _():
                for j in range(last - hop):
                    pass_on(chain_down(p, j), partial(p, j), r.down_in[p].at[j])

    def chain_finish(p, dst):
        mine = partial(p, z)

        @pl.when(z == 0)
        def _():
            chain_down(p, z).wait_recv()
            dst[...] = (mine[...].astype(F32) + r.down_in[p][z].astype(F32)).astype(BF16)

        @pl.when(z == last)
        def _():
            chain_up(p, z).wait_recv()
            dst[...] = (mine[...].astype(F32) + r.up_in[p][z].astype(F32)).astype(BF16)

        @pl.when((z > 0) & (z < last))
        def _():
            chain_down(p, z).wait_recv()
            chain_up(p, z).wait_recv()
            dst[...] = (
                mine[...].astype(F32) + r.up_in[p][z].astype(F32) + r.down_in[p][z].astype(F32)
            ).astype(BF16)

    def spread_start(p):
        @pl.when(z < last)
        def _():
            spread_up(p, z).start()

        @pl.when(z > 0)
        def _():
            spread_down(p, z).start()

    def spread_forward(p, hops):
        for d in hops:
            @pl.when(z - d >= 0)
            def _():
                spread_up(p, z - d).wait_recv()
                if orders[p]:
                    start(row_spread(p, z - d))

                @pl.when(z < last)
                def _():
                    spread_up(p, z - d).start()

            @pl.when(z + d < outer)
            def _():
                spread_down(p, z + d).wait_recv()
                if orders[p]:
                    start(row_spread(p, z + d))

                @pl.when(z > 0)
                def _():
                    spread_down(p, z + d).start()

    def chain_sent(p):
        for d in range(1, outer):
            @pl.when(z + d < outer)
            def _():
                chain_up(p, z + d).wait_send()

            @pl.when(z - d >= 0)
            def _():
                chain_down(p, z - d).wait_send()

        for d in range(outer):
            @pl.when((z < last) & (z - d >= 0))
            def _():
                spread_up(p, z - d).wait_send()

            @pl.when((z > 0) & (z + d < outer))
            def _():
                spread_down(p, z + d).wait_send()

    def peers(p, src, dst, send, recv):
        return [
            remote(
                src((y + k) % inner), dst(k - 1), send[p].at[k - 1], recv[p].at[k - 1],
                (z * inner + (y + k) % inner, mt),
            )
            for k in range(1, inner)
        ]

    def inner_sum(p):
        if orders[p]:
            return peers(
                p, lambda to: r.loc[p].at[pl.ds(to * outer, outer)], lambda k: r.inbox[p].at[k], r.i_s, r.i_r
            )
        return peers(
            p, lambda to: r.held[p].at[pl.ds(to, 1)], lambda k: r.inbox[p].at[k], r.i_s, r.i_r
        )

    def row_spread(p, j):
        block = r.full[p].at[chunk(p, j)]
        return [
            remote(
                block, block, r.o_s[p].at[k - 1, j], r.o_r[p].at[k - 1, j],
                (z * inner + (y + k) % inner, mt),
            )
            for k in range(1, inner)
        ]

    def inner_spread(p):
        if orders[p]:
            return [copy for j in range(outer) for copy in row_spread(p, j)]
        block = r.full[p].at[pl.ds(z * inner + y, 1)]
        return [
            remote(
                block, block, r.o_s[p].at[k - 1, 0], r.o_r[p].at[k - 1, 0],
                (z * inner + (y + k) % inner, mt),
            )
            for k in range(1, inner)
        ]

    def advance(step, *which):
        for p in which:
            if orders[p]:
                inner_first_step(step, p)
            else:
                outer_first_step(step, p)

    sum_hops = np.array_split(np.arange(1, last), 2)
    spread_hops = np.array_split(np.arange(1, outer), 3)

    def inner_first_step(step, p):
        if step == 0:
            start(inner_sum(p))
        elif step == 1:
            arrive(inner_sum(p))
            acc = r.loc[p][pl.ds(y * outer, outer)].astype(F32)
            for k in range(inner - 1):
                acc = acc + r.inbox[p][k].astype(F32)
            r.held[p][...] = acc.astype(BF16)
            chain_start(p)
        elif step <= 3:
            chain_forward(p, sum_hops[step - 2].tolist())
        elif step == 4:
            chain_finish(p, r.full[p].at[chunk(p, z)])
            spread_start(p)
            start(row_spread(p, z))
        elif step <= 7:
            spread_forward(p, spread_hops[step - 5].tolist())
        else:
            arrive(inner_spread(p))

    def outer_first_step(step, p):
        if step == 0:
            chain_start(p)
        elif step <= 2:
            chain_forward(p, sum_hops[step - 1].tolist())
        elif step == 3:
            chain_finish(p, r.held[p])
            start(inner_sum(p))
        elif step == 4:
            arrive(inner_sum(p))
            acc = r.held[p][pl.ds(y, 1)].astype(F32)
            for k in range(inner - 1):
                acc = acc + r.inbox[p][k].astype(F32)
            r.full[p][pl.ds(z * inner + y, 1)] = acc.astype(BF16)
            start(inner_spread(p))
        elif step == 5:
            arrive(inner_spread(p))
            spread_start(p)
        else:
            spread_forward(p, spread_hops[step - 6].tolist())

    outs = []

    def write_out(src, dst):
        copy = pltpu.make_async_copy(src, dst, r.out_sem.at[len(outs)])
        copy.start()
        outs.append(copy)

    def small_exchange(g, src, axis):
        size = outer if axis else inner
        out = []
        for k in range(1, size):
            if axis:
                to = ((z + k) % outer) * inner + y
            else:
                to = z * inner + (y + k) % inner
            out.append(remote(
                src, g.inbox[axis].at[k - 1], g.send[axis].at[k - 1], g.recv[axis].at[k - 1], (to, mt)
            ))
        return out

    def small_tensor(g, src, slots):
        return [
            remote(
                src, slots(k), g.send[2].at[k - 1], g.recv[2].at[k - 1], (me, (mt + k) % 4)
            )
            for k in range(1, 4)
        ]

    gn, rt = SimpleNamespace(**r.gn), SimpleNamespace(**r.rt)
    lane = lax.broadcasted_iota(jnp.int32, (R, LANES), 1)
    low = lane < HEAD_SIZE
    first_half = (lane % HEAD_SIZE) < HEAD_SIZE // 2

    def swap(v):
        return jnp.where(first_half, pltpu.roll(v, 96, 1), pltpu.roll(v, 32, 1))

    CH = 32

    def row_chunks(body):
        def step(i, _):
            body(pl.ds(pl.multiple_of(i * CH, CH), CH))
            return 0

        lax.fori_loop(0, R // CH, step, 0)

    def own_chunk(rows):
        return pl.ds(pl.multiple_of(mt * R + rows.start, CH), CH)

    load[0].wait()
    load[17].wait()

    def norm_rows(rows):
        h = r.hid[rows, :].astype(F32)
        inv = lax.rsqrt(jnp.mean(h * h, axis=-1, keepdims=True) + EPS)
        r.xa[own_chunk(rows), :] = (h * inv * r.gain_attn[...]).astype(BF16)

    row_chunks(norm_rows)

    pl.semaphore_wait(barrier, 3 + (inner - 1) + (outer - 1))

    ag_xa = gather(0, r.xa)
    gather_start(ag_xa)
    load[1].wait()
    ag_cot = gather(1, r.cot)
    ag_cot[1].start()
    for copy in load[2:7] + load[16:17]:
        copy.wait()

    r.gk[...] = jnp.zeros_like(r.gk)
    r.gv[...] = jnp.zeros_like(r.gv)
    gn.own[...] = jnp.zeros_like(gn.own)

    def project(k, _):
        gather_step(k, ag_xa)
        b = block_of(3 - k)
        rows = rows_of(b)
        qkv = nn(r.xa[rows, :], r.wqkv[...])
        cos, sin = r.cos[rows, :], r.sin[rows, :]

        def rope(v):
            return v * cos + swap(v) * sin

        zero = jnp.zeros((R, LANES), F32)
        q0 = rope(qkv[:, 0:128]) * HEAD_SIZE ** (-0.5)
        q1 = rope(qkv[:, 128:256]) * HEAD_SIZE ** (-0.5)
        kk = rope(qkv[:, 256:384])
        vv = qkv[:, 384:512]
        r.q[rows, 0:128] = q0.astype(BF16)
        r.q[rows, 128:256] = q1.astype(BF16)
        r.qp[b, 0 * R:1 * R, :] = jnp.where(low, q0, zero).astype(BF16)
        r.qp[b, 1 * R:2 * R, :] = jnp.where(low, pltpu.roll(q0, 64, 1), zero).astype(BF16)
        r.qp[b, 2 * R:3 * R, :] = jnp.where(low, zero, pltpu.roll(q1, 64, 1)).astype(BF16)
        r.qp[b, 3 * R:4 * R, :] = jnp.where(low, zero, q1).astype(BF16)
        for dst, val in ((r.klh, kk), (r.vlh, vv)):
            turned = pltpu.roll(val, 64, 1)
            dst[0, rows, :] = jnp.where(low, val, zero).astype(BF16)
            dst[1, rows, :] = jnp.where(low, zero, turned).astype(BF16)
            dst[2, rows, :] = jnp.where(low, turned, zero).astype(BF16)
            dst[3, rows, :] = jnp.where(low, zero, val).astype(BF16)
        return 0

    lax.fori_loop(0, 4, project, 0)
    ag_cot[0].start()
    load[7].wait()

    KW = 3 * R
    rs1 = scatter(0, W)

    def attend(k, _):
        b = block_of(k)
        rows = rows_of(b)
        wstart = (b // 3) * R
        win = pl.ds(pl.multiple_of(wstart, R), KW)
        seg_q = r.seg[0:1, rows].astype(F32)
        seg_col = jnp.transpose(jnp.broadcast_to(seg_q, (R, R)))[:, 0:1]
        seg_k = r.seg[0:1, win].astype(F32)
        at_q = lax.broadcasted_iota(jnp.int32, (R, KW), 0) + (b * R - wstart)
        at_k = lax.broadcasted_iota(jnp.int32, (R, KW), 1)
        bias = jnp.where((seg_col == seg_k) & (at_k <= at_q), 0.0, NEGATIVE)
        for kv in range(2):
            q = r.q[rows, kv * LANES:(kv + 1) * LANES]
            mixed = jnp.zeros((R, LANES), F32)
            for h in range(2):
                i = kv * 2 + h
                s = nt(q, r.klh[i, win, :]) + bias
                e = jnp.exp(s - jnp.max(s, axis=-1, keepdims=True))
                prob = (e * (1.0 / jnp.sum(e, axis=-1, keepdims=True))).astype(BF16)
                r.prob[b, i * R:(i + 1) * R, :] = prob
                mixed = mixed + nn(prob, r.vlh[i, win, :])
            r.mixed[rows, kv * LANES:(kv + 1) * LANES] = mixed.astype(BF16)
        r.part[...] = nn(r.mixed[rows, :], r.wo[...])
        scatter_step(k, 0, rs1, r.part)
        return 0

    lax.fori_loop(0, 4, attend, 0)
    for copy in load[8:16]:
        copy.wait()
    rs1[2].wait_recv()
    rs1[1].wait_recv()

    def after_rows(rows):
        a = r.hid[rows, :].astype(F32) + (
            r.part[rows, :] + r.rp[0][1, rows, :].astype(F32) + r.rx[0][rows, :].astype(F32)
        )
        r.after[rows, :] = a
        inv = lax.rsqrt(jnp.mean(a * a, axis=-1, keepdims=True) + EPS)
        r.xf[own_chunk(rows), :] = (a * inv * r.gain_ffn[...]).astype(BF16)

    row_chunks(after_rows)
    ag_xf = gather(2, r.xf)
    gather_start(ag_xf)

    E = r.wr.shape[0]
    expert = lax.broadcasted_iota(jnp.int32, (R, E), 1)
    logits = nt(r.xf[rows_of(mt), :], r.wr[...])
    el = jnp.exp(logits - jnp.max(logits, axis=-1, keepdims=True))
    router_probs = el / jnp.sum(el, axis=-1, keepdims=True)
    routes = r.routes[...]

    def count(e):
        named = jnp.sum((routes == e).astype(F32), axis=0, keepdims=True)
        return jnp.transpose(jnp.broadcast_to(named, (R, R)))[:, 0:1]

    count0, count1 = count(0), count(1)
    counts = jnp.where(expert == 0, count0, jnp.where(expert == 1, count1, 0.0))
    r.rprobs[...] = router_probs
    r.counts[...] = counts
    r.cb[rows_of(mt), :] = jnp.zeros((R, LANES), BF16)
    r.cb[rows_of(mt), 0:E] = (router_probs * counts).astype(BF16)
    ag_cb = gather(3, r.cb)
    gather_start(ag_cb)

    ag_cot[1].wait_recv()
    ag_cot[0].wait_recv()
    ag_cot[2].start()
    H2 = r.wd.shape[0]

    def experts(k, _):
        gather_step(k, ag_xf, ag_cb)

        @pl.when(k == 3)
        def _():
            ag_cot[2].wait_recv()

        b = block_of(3 - k)
        rows = rows_of(b)
        gu = nn(r.xf[rows, :], r.wgu[...])
        down = nt(r.cot[rows, :], r.wd[...])
        cb = r.cb[rows, :].astype(F32)
        gcol = jnp.zeros((R, LANES), F32)
        for e in range(2):
            cols = slice(e * LANES, (e + 1) * LANES)
            up_cols = slice(H2 + e * LANES, H2 + (e + 1) * LANES)
            g, u, a = gu[:, cols], gu[:, up_cols], down[:, cols]
            c = cb[:, e:e + 1]
            sig = 1.0 / (1.0 + jnp.exp(-g))
            silu = g * sig
            act = silu * u
            ga = c * a
            r.ci[rows, cols] = (c * act).astype(BF16)
            r.dgu[rows, cols] = (ga * u * (sig * (1.0 + g * (1.0 - sig)))).astype(BF16)
            r.dgu[rows, up_cols] = (ga * silu).astype(BF16)
            gcol = jnp.where(lane == e, jnp.sum(act * a, axis=-1, keepdims=True), gcol)
        r.pr[rows, 0:W] = nt(r.dgu[rows, :], r.wgu[...])
        r.pr[rows, W:W + LANES] = gcol
        return 0

    lax.fori_loop(0, 4, experts, 0)
    rs2 = scatter(1, W + LANES)
    for k in (0, 2, 1):
        scatter_step(k, 1, rs2, r.pr.at[rows_of(block_of(k))])

    depth = W // n

    def store_piece(p, row, tile):
        count = tile.shape[0] // depth
        r.loc[p][pl.ds(row * count, count)] = tile.astype(BF16).reshape(count, depth, PIECE_COLS)

    def tiles(first, second, left, right):
        def step(i, _):
            cols = pl.ds(pl.multiple_of(i * 256, 256), 256)
            tile = tn(left[:, cols], right[...])
            store_piece(first, i, tile[:, 0:PIECE_COLS])
            store_piece(second, i, tile[:, PIECE_COLS:])
            return 0

        lax.fori_loop(0, W // 256, step, 0)
        advance(0, first, second)

    def tiles_by_columns(p, left, right):
        def step(i, _):
            cols = pl.ds(pl.multiple_of(i * 256, 256), 256)
            store_piece(p, i, tn(left[...], right[:, cols]))
            return 0

        lax.fori_loop(0, W // 256, step, 0)
        advance(0, p)

    tiles(GATE, UP, r.xf, r.dgu)
    tiles_by_columns(DOWN, r.ci, r.cot)

    rs2[2].wait_recv()
    rs2[1].wait_recv()
    own = rows_of(mt)
    gcomb = (
        r.pr[own, W:W + LANES]
        + r.rp[1][1, :, W:W + LANES].astype(F32)
        + r.rx[1][:, W:W + LANES].astype(F32)
    )[:, 0:E]
    grp = gcomb * r.counts[...]
    rp = r.rprobs[...]
    glog = (rp * (grp - jnp.sum(rp * grp, axis=-1, keepdims=True))).astype(BF16)
    r.ga[own, W:W + LANES] = jnp.zeros((R, LANES), BF16)
    r.ga[own, W:W + E] = glog
    r.part[...] = nn(glog, r.wr[...])

    def grad_after_rows(rows):
        a = r.after[rows, :]
        inv = lax.rsqrt(jnp.mean(a * a, axis=-1, keepdims=True) + EPS)
        unit = a * inv
        g = (
            r.part[rows, :]
            + r.pr[own_chunk(rows), 0:W]
            + r.rp[1][1, rows, 0:W].astype(F32)
            + r.rx[1][rows, 0:W].astype(F32)
        )
        gn.own[0:1, :] += jnp.sum(g * unit, axis=0, keepdims=True)
        scaled = g * r.gain_ffn[...]
        back = inv * (scaled - unit * jnp.mean(scaled * unit, axis=-1, keepdims=True))
        ga = back + r.cot[own_chunk(rows), :].astype(F32)
        r.ga_own[rows, :] = ga
        r.ga[own_chunk(rows), 0:W] = ga.astype(BF16)

    row_chunks(grad_after_rows)
    ag_ga = gather(4, r.ga)
    gather_start(ag_ga)
    advance(1, GATE, UP)

    def attend_back(k, _):
        @pl.when(k == 2)
        def _():
            advance(2, GATE, UP)
            advance(1, DOWN)

        gather_step(k, ag_ga)

        @pl.when(k == 3)
        def _():
            advance(3, GATE, UP)

        b = block_of(3 - k)
        rows = rows_of(b)
        wstart = (b // 3) * R
        win = pl.ds(pl.multiple_of(wstart, R), KW)
        gm = nt(r.ga[rows, 0:W], r.wo[...])
        zero = jnp.zeros((R, LANES), F32)
        for kv in range(2):
            cols = slice(kv * LANES, (kv + 1) * LANES)
            gmk = gm[:, cols].astype(BF16)
            gmf = gmk.astype(F32)
            turned = pltpu.roll(gmf, 64, 1)
            if kv == 0:
                r.gmp[0 * R:1 * R, :] = jnp.where(low, gmf, zero).astype(BF16)
                r.gmp[1 * R:2 * R, :] = jnp.where(low, turned, zero).astype(BF16)
            else:
                r.gmp[2 * R:3 * R, :] = jnp.where(low, zero, turned).astype(BF16)
                r.gmp[3 * R:4 * R, :] = jnp.where(low, zero, gmf).astype(BF16)
            prod = gmf * r.mixed[rows, cols].astype(F32)
            delta_lo = jnp.sum(jnp.where(low, prod, zero), axis=-1, keepdims=True)
            delta_hi = jnp.sum(jnp.where(low, zero, prod), axis=-1, keepdims=True)
            gq = zero
            for h, delta in ((0, delta_lo), (1, delta_hi)):
                i = kv * 2 + h
                head = slice(i * R, (i + 1) * R)
                dp = nt(gmk, r.vlh[i, win, :])
                ds = (r.prob[b, head, :].astype(F32) * (dp - delta)).astype(BF16)
                r.ds[head, :] = ds
                gq = gq + nn(ds, r.klh[i, win, :])
            gq = gq * HEAD_SIZE ** (-0.5)
            gq = gq * r.cos[rows, :] - swap(gq) * r.sin[rows, :]
            r.dqkv[rows, cols] = gq.astype(BF16)
        r.gk[win, :] += tn(r.ds[...], r.qp[b])
        r.gv[win, :] += tn(r.prob[b], r.gmp[...])
        return 0

    lax.fori_loop(0, 4, attend_back, 0)
    advance(4, GATE, UP)
    advance(2, DOWN)


    def finish_kv(k, _):
        rows = rows_of(k)
        gk = r.gk[rows, :]
        gk = gk * r.cos[rows, :] - swap(gk) * r.sin[rows, :]
        r.dqkv[rows, 256:384] = gk.astype(BF16)
        r.dqkv[rows, 384:512] = r.gv[rows, :].astype(BF16)
        return 0

    lax.fori_loop(0, 4, finish_kv, 0)
    tiles(QUERY, KEYS, r.xa, r.dqkv)
    tiles_by_columns(OUT, r.mixed, r.ga)
    advance(5, GATE, UP)
    advance(3, DOWN)
    rs3 = scatter(2, W)

    def input_part(k, _):
        r.part[...] = nt(r.dqkv[rows_of(block_of(k)), :], r.wqkv[...])
        scatter_step(k, 2, rs3, r.part)
        return 0

    lax.fori_loop(0, 4, input_part, 0)
    advance(6, GATE, UP)
    advance(4, DOWN)
    quarter = pl.ds(pl.multiple_of(mt * (W // 4), W // 4), W // 4)
    rt.own[...] = tn(r.ga[:, W:W + LANES], r.xf[:, quarter])[0:E, :]
    rt0 = small_exchange(rt, rt.own, 0)
    start(rt0)

    advance(1, QUERY, KEYS, OUT)
    advance(7, GATE, UP)
    advance(5, DOWN)
    advance(2, QUERY, KEYS, OUT)
    rs3[2].wait_recv()
    rs3[1].wait_recv()

    def grad_in_rows(rows):
        h = r.hid[rows, :].astype(F32)
        inv = lax.rsqrt(jnp.mean(h * h, axis=-1, keepdims=True) + EPS)
        unit = h * inv
        g = r.part[rows, :] + r.rp[2][1, rows, :].astype(F32) + r.rx[2][rows, :].astype(F32)
        gn.own[1:2, :] += jnp.sum(g * unit, axis=0, keepdims=True)
        scaled = g * r.gain_attn[...]
        back = inv * (scaled - unit * jnp.mean(scaled * unit, axis=-1, keepdims=True))
        r.grad_in_v[rows, :] = back + r.ga_own[rows, :]

    row_chunks(grad_in_rows)
    write_out(r.grad_in_v, r.grad_in)
    gt = small_tensor(gn, gn.own, lambda k: gn.inbox[2].at[k - 1])
    start(gt)
    advance(6, DOWN)
    advance(8, UP)
    advance(3, QUERY, KEYS, OUT)

    rs4 = scatter(3, W)

    def output_part(k, _):
        r.part[...] = nn(r.ci[rows_of(block_of(k)), :], r.wd[...])
        scatter_step(k, 3, rs4, r.part)
        return 0

    lax.fori_loop(0, 4, output_part, 0)
    advance(4, QUERY, KEYS, OUT)
    advance(7, DOWN)

    arrive(gt)
    total = gn.own[...]
    for k in range(3):
        total = total + gn.inbox[2][k]
    gn.first[...] = total
    g0 = small_exchange(gn, gn.first, 0)
    start(g0)
    arrive(rt0)
    total = rt.own[...]
    for k in range(inner - 1):
        total = total + rt.inbox[0][k]
    rt.first[...] = total
    rt1 = small_exchange(rt, rt.first, 1)
    start(rt1)
    advance(5, QUERY, KEYS, OUT)

    rs4[2].wait_recv()
    rs4[1].wait_recv()

    def output_rows(rows):
        a = r.part[rows, :] + r.rp[3][1, rows, :].astype(F32) + r.rx[3][rows, :].astype(F32)
        r.output_v[rows, :] = (r.after[rows, :] + a).astype(BF16)

    row_chunks(output_rows)
    write_out(r.output_v, r.output)
    advance(6, QUERY, KEYS, OUT)

    arrive(g0)
    total = gn.first[...]
    for k in range(inner - 1):
        total = total + gn.inbox[0][k]
    gn.second[...] = total
    g1 = small_exchange(gn, gn.second, 1)
    start(g1)
    arrive(rt1)
    total = rt.first[...]
    for k in range(outer - 1):
        total = total + rt.inbox[1][k]
    r.router_v[mt] = total
    rtt = small_tensor(rt, r.router_v.at[mt], lambda k: r.router_v.at[mt])
    start(rtt)
    advance(7, QUERY, KEYS, OUT)

    arrive(g1)
    total = gn.second[...]
    for k in range(outer - 1):
        total = total + gn.inbox[1][k]
    r.gains_v[...] = total
    write_out(r.gains_v, r.gains)
    arrive(rtt)
    write_out(r.router_v, r.router)
    for p in (UP, GATE, DOWN, KEYS, QUERY, OUT):
        if p != UP:
            advance(8, p)
        write_out(r.full[p], r.pieces[p])

    for copy in outs:
        copy.wait()

    for g in (ag_xa, ag_cot, ag_xf, ag_cb, ag_ga, rs1, rs2, rs3, rs4, rt0, rt1, rtt, gt, g0, g1):
        for copy in g:
            copy.wait_send()
    for p in range(6):
        chain_sent(p)
        for copy in inner_sum(p) + inner_spread(p):
            copy.wait_send()


def finish_kernel(r):
    copies = []

    def put(src, dst):
        copy = pltpu.make_async_copy(src, dst, r.sem.at[len(copies)])
        copy.start()
        copies.append(copy)
        return copy

    loads = [
        put(src, dst)
        for src, dst in list(zip(r.pieces, r.v_pieces))
        + [(r.router, r.v_router), (r.output, r.v_output), (r.grad_in, r.v_grad_in), (r.gains, r.v_gains)]
    ]
    experts, _, hidden = r.o_gate.shape
    for p, dst, out in ((GATE, r.t_gate, r.o_gate), (UP, r.t_up, r.o_up)):
        loads[p].wait()
        for e in range(experts):
            dst[e] = r.v_pieces[p][:, e * hidden:(e + 1) * hidden].astype(F32)
        put(dst, out)
    for p, dst, out in ((DOWN, r.t_down, r.o_down), (OUT, r.t_wo, r.o_wo)):
        loads[p].wait()
        rows, cols = dst.shape[0], PIECE_COLS
        for i in range(r.v_pieces[p].shape[0] // rows):
            dst[:, i * cols:(i + 1) * cols] = r.v_pieces[p][i * rows:(i + 1) * rows, :].astype(F32)
        put(dst, out)
    loads[QUERY].wait()
    r.t_wq[...] = r.v_pieces[QUERY][...].astype(F32)
    put(r.t_wq, r.o_wq)
    loads[KEYS].wait()
    cols = r.t_wk.shape[1]
    r.t_wk[...] = r.v_pieces[KEYS][:, 0:cols].astype(F32)
    put(r.t_wk, r.o_wk)
    r.t_wv[...] = r.v_pieces[KEYS][:, cols:2 * cols].astype(F32)
    put(r.t_wv, r.o_wv)
    for load in loads[KEYS + 1:]:
        load.wait()
    put(r.v_output, r.o_output)
    put(r.v_grad_in, r.o_grad_in)
    r.t_gain_ffn[...] = r.v_gains[0:1, :]
    r.t_gain_attn[...] = r.v_gains[1:2, :]
    put(r.t_gain_ffn, r.o_gain_ffn)
    put(r.t_gain_attn, r.o_gain_attn)
    cols = r.v_router.shape[2]
    for i in range(r.v_router.shape[0]):
        r.t_router[:, i * cols:(i + 1) * cols] = r.v_router[i]
    put(r.t_router, r.o_router)
    for copy in copies[len(loads):]:
        copy.wait()


def rotary_tables(rows):
    half = HEAD_SIZE // 2
    freq = THETA ** (-(np.arange(half, dtype=np.float64) * 2.0 / HEAD_SIZE))
    angles = np.arange(rows, dtype=np.float64)[:, None] * freq[None, :]
    cos, sin = np.cos(angles), np.sin(angles)
    cos = np.concatenate([cos] * 4, axis=1).astype(np.float32)
    sin = np.concatenate([-sin, sin] * 2, axis=1).astype(np.float32)
    return jnp.asarray(cos), jnp.asarray(sin)


def on_device(
    hidden_in,
    cotangent,
    segments,
    routes,
    gain_attn,
    w_query,
    key_matrix,
    value_matrix,
    attention_output_weight,
    gain_ffn,
    w_router,
    w_gate,
    w_up,
    w_down,
):
    n = lax.axis_size("dp")
    inner = math.isqrt(n)
    outer = n // inner
    R, W = hidden_in.shape
    S = segments.shape[1]
    E = w_router.shape[1]
    depth = W // n
    head_cols = attention_output_weight.shape[0]
    down_rows = w_down.shape[0] * w_down.shape[1]
    cos, sin = rotary_tables(S)
    orders = INNER_FIRST
    piece_cols = (PIECE_COLS,) * len(orders)

    hbm = pl.BlockSpec(memory_space=pl.ANY)
    in_hbm = dict(
        hidden_hbm=hidden_in,
        cot_hbm=cotangent,
        wq_hbm=w_query,
        wk_hbm=key_matrix,
        wv_hbm=value_matrix,
        cos_hbm=cos,
        sin_hbm=sin,
        wo_hbm=attention_output_weight,
        wg_hbm=w_gate,
        wu_hbm=w_up,
        wd_hbm=w_down.reshape(down_rows, W),
        seg_hbm=segments,
        routes_hbm=routes.T,
        gain_attn_hbm=gain_attn.reshape(1, W),
        gain_ffn_hbm=gain_ffn.reshape(1, W),
        wr_hbm=w_router.T,
    )
    shape = jax.ShapeDtypeStruct
    results = dict(
        output=shape((R, W), BF16),
        grad_in=shape((R, W), F32),
        gains=shape((2, W), F32),
        router=shape((4, E, W // 4), F32),
        pieces=[shape((n, depth, c), BF16) for c in piece_cols],
    )

    dma = pltpu.SemaphoreType.DMA
    half = functools.partial(pltpu.VMEM, dtype=BF16)
    full = functools.partial(pltpu.VMEM, dtype=F32)

    def small(rows, cols):
        return dict(
            own=full((rows, cols)),
            first=full((rows, cols)),
            second=full((rows, cols)),
            inbox=[full((size, rows, cols)) for size in (inner - 1, outer - 1, 3)],
            send=[dma((size,)) for size in (inner - 1, outer - 1, 3)],
            recv=[dma((size,)) for size in (inner - 1, outer - 1, 3)],
        )

    sizes = [(1, outer, outer) if order else (inner, 1, inner) for order in orders]
    sums = (W, W + LANES, W, W)
    scratch = dict(
        hid=half((R, W)),
        cot=half((S, W)),
        wqkv=half((W, 512)),
        cos=full((S, LANES)),
        sin=full((S, LANES)),
        wo=half((head_cols, W)),
        wgu=half((W, 512)),
        wd=half((down_rows, W)),
        xa=half((S, W)),
        xf=half((S, W)),
        cb=half((S, LANES)),
        ga=half((S, W + LANES)),
        q=half((S, 256)),
        qp=half((4, 4 * R, LANES)),
        klh=half((4, S, LANES)),
        vlh=half((4, S, LANES)),
        prob=half((4, 4 * R, 3 * R)),
        ds=half((4 * R, 3 * R)),
        gmp=half((4 * R, LANES)),
        mixed=half((S, head_cols)),
        part=full((R, W)),
        after=full((R, W)),
        rprobs=full((R, E)),
        counts=full((R, E)),
        ci=half((S, down_rows)),
        dgu=half((S, 512)),
        pr=full((S, W + LANES)),
        ga_own=full((R, W)),
        gk=full((S, LANES)),
        gv=full((S, LANES)),
        dqkv=half((S, 512)),
        gn=small(2, W),
        rt=small(E, W // 4),
        output_v=half((R, W)),
        grad_in_v=full((R, W)),
        gains_v=full((2, W)),
        router_v=full((4, E, W // 4)),
        full=[half((n, depth, c)) for c in piece_cols],
        seg=pltpu.VMEM((1, S), jnp.int32),
        routes=pltpu.VMEM((routes.shape[1], R), jnp.int32),
        gain_attn=full((1, W)),
        gain_ffn=full((1, W)),
        wr=half((E, W)),
        load_sem=dma((18,)),
        out_sem=dma((10,)),
        ag_send=dma((5, 3)),
        ag_recv=dma((5, 3)),
        rs_send=dma((4, 3)),
        rs_recv=dma((4, 3)),
        sb=[half((2, R, c)) for c in sums],
        sx=[half((R, c)) for c in sums],
        rp=[half((2, R, c)) for c in sums],
        rx=[half((R, c)) for c in sums],
        loc=[half((n, depth, c)) for c in piece_cols],
        held=[half((kept, depth, PIECE_COLS)) for _, _, kept in sizes],
        up_in=[half((outer, part, depth, PIECE_COLS)) for part, _, _ in sizes],
        down_in=[half((outer, part, depth, PIECE_COLS)) for part, _, _ in sizes],
        inbox=[half((inner - 1, part, depth, PIECE_COLS)) for _, part, _ in sizes],
        c_su=[dma((outer,)) for _ in sizes],
        c_ru=[dma((outer,)) for _ in sizes],
        c_sd=[dma((outer,)) for _ in sizes],
        c_rd=[dma((outer,)) for _ in sizes],
        g_su=[dma((outer,)) for _ in sizes],
        g_sd=[dma((outer,)) for _ in sizes],
        g_r=[dma((outer,)) for _ in sizes],
        i_s=[dma((inner - 1,)) for _ in sizes],
        i_r=[dma((inner - 1,)) for _ in sizes],
        o_s=[dma((inner - 1, outer)) for _ in sizes],
        o_r=[dma((inner - 1, outer)) for _ in sizes],
    )

    def call(kernel, specs, operands, results, result_spec, scratch, params):
        given, in_tree = jax.tree.flatten(operands)
        shapes, out_tree = jax.tree.flatten(results)
        inner_shapes, scratch_tree = jax.tree.flatten(scratch)

        def body(*refs):
            a, b = len(given), len(given) + len(shapes)
            named = jax.tree.unflatten(in_tree, refs[:a])
            named.update(jax.tree.unflatten(out_tree, refs[a:b]))
            named.update(jax.tree.unflatten(scratch_tree, refs[b:]))
            kernel(SimpleNamespace(**named))

        got = pl.pallas_call(
            body,
            out_shape=shapes,
            in_specs=jax.tree.flatten(specs)[0],
            out_specs=[result_spec] * len(shapes),
            scratch_shapes=inner_shapes,
            compiler_params=params,
        )(*given)
        return SimpleNamespace(**jax.tree.unflatten(out_tree, got))

    specs = {key: hbm for key in in_hbm}
    got = call(
        functools.partial(layer_kernel, n, inner, orders),
        specs, in_hbm, results, hbm, scratch,
        pltpu.CompilerParams(collective_id=0, has_side_effects=True, vmem_limit_bytes=VMEM_LIMIT),
    )

    ready = dict(
        output=got.output,
        grad_in=got.grad_in,
        gains=got.gains,
        router=got.router,
        pieces=[piece.reshape(W, PIECE_COLS) for piece in got.pieces],
    )
    finals = dict(
        o_output=shape((R, W), BF16),
        o_grad_in=shape((R, W), F32),
        o_gain_ffn=shape((1, W), F32),
        o_gain_attn=shape((1, W), F32),
        o_gate=shape(w_gate.shape, F32),
        o_up=shape(w_up.shape, F32),
        o_down=shape((down_rows, W), F32),
        o_wo=shape(attention_output_weight.shape, F32),
        o_wq=shape(w_query.shape, F32),
        o_wk=shape(key_matrix.shape, F32),
        o_wv=shape(value_matrix.shape, F32),
        o_router=shape((E, W), F32),
    )
    temps = dict(
        t_gate=full(w_gate.shape),
        t_up=full(w_up.shape),
        t_down=full((down_rows, W)),
        t_wo=full(attention_output_weight.shape),
        t_wq=full(w_query.shape),
        t_wk=full(key_matrix.shape),
        t_wv=full(value_matrix.shape),
        t_router=full((E, W)),
        v_pieces=[half((W, PIECE_COLS)) for _ in piece_cols],
        v_router=full((4, E, W // 4)),
        v_output=half((R, W)),
        v_grad_in=full((R, W)),
        v_gains=full((2, W)),
        t_gain_ffn=full((1, W)),
        t_gain_attn=full((1, W)),
        sem=dma((len(finals) + 10,)),
    )
    done = call(
        finish_kernel, jax.tree.map(lambda _: hbm, ready), ready, finals, hbm, temps,
        pltpu.CompilerParams(vmem_limit_bytes=VMEM_LIMIT),
    )
    return (
        done.o_output,
        done.o_grad_in,
        done.o_gain_attn.reshape(W),
        done.o_wq,
        done.o_wk,
        done.o_wv,
        done.o_wo,
        done.o_gain_ffn.reshape(W),
        done.o_router.T,
        done.o_gate,
        done.o_up,
        done.o_down.reshape(w_down.shape),
    )


def solution(mesh):
    rows = P(("dp", "tensor"), None)
    columns = P(None, "tensor")
    return jax.shard_map(
        on_device,
        mesh=mesh,
        in_specs=(
            rows, rows, P("dp", None), rows, P(), columns, columns, columns,
            P("tensor", None), P(), P(), P(None, None, "tensor"), P(None, None, "tensor"),
            P(None, "tensor", None),
        ),
        out_specs=(
            rows, rows, P(), columns, columns, columns, P("tensor", None), P(), P(),
            P(None, None, "tensor"), P(None, None, "tensor"), P(None, "tensor", None),
        ),
        check_vma=False,
    )
```

```python
import functools
import math
from types import SimpleNamespace

import jax
import jax.numpy as jnp
import numpy as np
from jax import lax
from jax.experimental import pallas as pl
from jax.experimental.pallas import tpu as pltpu
from jax.sharding import PartitionSpec as P

HEAD_SIZE = 64
LANES = 128
EPS = 1e-06
THETA = 10000.0
NEGATIVE = -1e30
MESH = pl.DeviceIdType.MESH
F32 = jnp.float32
BF16 = jnp.bfloat16

GATE, UP, DOWN, OUT, QUERY, KEYS = range(6)
INNER_FIRST = (True, False, True, True, True, True)
PIECE_COLS = 256
VMEM_LIMIT = 61 * 1024 * 1024


def nt(left, right):
    return lax.dot_general(left, right, (((1,), (1,)), ((), ())), preferred_element_type=F32)


def tn(left, right):
    return lax.dot_general(left, right, (((0,), (0,)), ((), ())), preferred_element_type=F32)


def nn(left, right):
    return jnp.dot(left, right, preferred_element_type=F32)


def layer_kernel(n, inner, orders, r):
    outer = n // inner
    me = lax.axis_index("dp")
    mt = lax.axis_index("tensor")
    y = me % inner
    z = me // inner
    xc = mt // 2
    core = mt % 2
    pair = xc * 2 + (1 - core)
    across = (1 - xc) * 2 + core

    R, W = r.hid.shape
    S = r.xa.shape[0]
    HC = r.wo.shape[0]

    def remote(src, dst, send, recv, device):
        return pltpu.make_async_remote_copy(
            src_ref=src, dst_ref=dst, send_sem=send, recv_sem=recv,
            device_id=device, device_id_type=MESH,
        )

    def block_of(k):
        return ((xc + 1 - k // 2) % 2) * 2 + (core + 1 - k % 2) % 2

    def rows_of(block):
        return pl.ds(pl.multiple_of(block * R, R), R)

    loads = [
        (r.hidden_hbm, r.hid),
        (r.cot_hbm, r.cot.at[rows_of(mt)]),
        (r.wq_hbm, r.wqkv.at[:, 0:256]),
        (r.wk_hbm, r.wqkv.at[:, 256:384]),
        (r.wv_hbm, r.wqkv.at[:, 384:512]),
        (r.cos_hbm, r.cos),
        (r.sin_hbm, r.sin),
        (r.wo_hbm, r.wo),
        (r.wg_hbm.at[0], r.wgu.at[:, 0:128]),
        (r.wg_hbm.at[1], r.wgu.at[:, 128:256]),
        (r.wu_hbm.at[0], r.wgu.at[:, 256:384]),
        (r.wu_hbm.at[1], r.wgu.at[:, 384:512]),
        (r.wd_hbm, r.wd),
        (r.wr_hbm, r.wr),
        (r.routes_hbm, r.routes),
        (r.gain_ffn_hbm, r.gain_ffn),
        (r.seg_hbm, r.seg),
        (r.gain_attn_hbm, r.gain_attn),
    ]
    load = [pltpu.make_async_copy(a, b, r.load_sem.at[i]) for i, (a, b) in enumerate(loads)]
    for copy in load:
        copy.start()

    barrier = pltpu.get_barrier_semaphore()
    for k in range(1, 4):
        pl.semaphore_signal(barrier, inc=1, device_id=(me, (mt + k) % 4), device_id_type=MESH)
    for k in range(1, inner):
        pl.semaphore_signal(
            barrier, inc=1, device_id=(z * inner + (y + k) % inner, mt), device_id_type=MESH
        )
    for k in range(1, outer):
        pl.semaphore_signal(
            barrier, inc=1, device_id=(((z + k) % outer) * inner + y, mt), device_id_type=MESH
        )

    def gather(i, buf):
        own = buf.at[rows_of(mt)]
        far = buf.at[rows_of(across)]
        ss, rs = r.ag_send, r.ag_recv
        return (
            remote(own, own, ss.at[i, 0], rs.at[i, 0], (me, across)),
            remote(own, own, ss.at[i, 1], rs.at[i, 1], (me, pair)),
            remote(far, far, ss.at[i, 2], rs.at[i, 2], (me, pair)),
        )

    def gather_start(g):
        g[0].start()
        g[1].start()

    def gather_step(k, *gs):
        @pl.when(k == 1)
        def _():
            for g in gs:
                g[1].wait_recv()

        @pl.when(k == 2)
        def _():
            for g in gs:
                g[0].wait_recv()
                g[2].start()

        @pl.when(k == 3)
        def _():
            for g in gs:
                g[2].wait_recv()

    def scatter(i, c):
        sb, sx, rp, rx = r.sb[i], r.sx[i], r.rp[i], r.rx[i]
        ss, rs = r.rs_send, r.rs_recv
        return (
            remote(sb.at[0], rp.at[0], ss.at[i, 0], rs.at[i, 0], (me, pair)),
            remote(sx, rx, ss.at[i, 1], rs.at[i, 1], (me, across)),
            remote(sb.at[1], rp.at[1], ss.at[i, 2], rs.at[i, 2], (me, pair)),
        )

    def scatter_step(k, i, c, part):
        sb, sx, rp = r.sb[i], r.sx[i], r.rp[i]

        @pl.when(k == 0)
        def _():
            sb[0] = part[...].astype(BF16)
            c[0].start()

        @pl.when(k == 1)
        def _():
            c[0].wait_recv()
            sx[...] = (part[...] + rp[0].astype(F32)).astype(BF16)
            c[1].start()

        @pl.when(k == 2)
        def _():
            sb[1] = part[...].astype(BF16)
            c[2].start()

    def start(copies):
        for copy in copies:
            copy.start()

    def arrive(copies):
        for copy in copies:
            copy.wait_recv()

    last = outer - 1
    ahead = ((z + 1) * inner + y, mt)
    behind = ((z - 1) * inner + y, mt)

    def chunk(p, j):
        if orders[p]:
            return pl.ds(y * outer + j, 1)
        return pl.ds(j * inner, inner)

    def partial(p, j):
        return r.held[p].at[pl.ds(j, 1)] if orders[p] else r.loc[p].at[chunk(p, j)]

    def chain_up(p, j):
        return remote(partial(p, j), r.up_in[p].at[j], r.c_su[p].at[j], r.c_ru[p].at[j], ahead)

    def chain_down(p, j):
        return remote(partial(p, j), r.down_in[p].at[j], r.c_sd[p].at[j], r.c_rd[p].at[j], behind)

    def spread_up(p, j):
        block = r.full[p].at[chunk(p, j)]
        return remote(block, block, r.g_su[p].at[j], r.g_r[p].at[j], ahead)

    def spread_down(p, j):
        block = r.full[p].at[chunk(p, j)]
        return remote(block, block, r.g_sd[p].at[j], r.g_r[p].at[j], behind)

    def chain_start(p):
        @pl.when(z == 0)
        def _():
            for d in range(last, 0, -1):
                chain_up(p, d).start()

        @pl.when(z == last)
        def _():
            for d in range(last, 0, -1):
                chain_down(p, last - d).start()

    def pass_on(copy, mine, came):
        copy.wait_recv()
        mine[...] = (mine[...].astype(F32) + came[...].astype(F32)).astype(BF16)
        copy.start()

    def chain_forward(p, hops):
        for hop in hops:
            @pl.when(z == hop)
            def _():
                for j in range(last, hop, -1):
                    pass_on(chain_up(p, j), partial(p, j), r.up_in[p].at[j])

            @pl.when(z == last - hop)
            def _():
                for j in range(last - hop):
                    pass_on(chain_down(p, j), partial(p, j), r.down_in[p].at[j])

    def chain_finish(p, dst):
        mine = partial(p, z)

        @pl.when(z == 0)
        def _():
            chain_down(p, z).wait_recv()
            dst[...] = (mine[...].astype(F32) + r.down_in[p][z].astype(F32)).astype(BF16)

        @pl.when(z == last)
        def _():
            chain_up(p, z).wait_recv()
            dst[...] = (mine[...].astype(F32) + r.up_in[p][z].astype(F32)).astype(BF16)

        @pl.when((z > 0) & (z < last))
        def _():
            chain_down(p, z).wait_recv()
            chain_up(p, z).wait_recv()
            dst[...] = (
                mine[...].astype(F32) + r.up_in[p][z].astype(F32) + r.down_in[p][z].astype(F32)
            ).astype(BF16)

    def spread_start(p):
        @pl.when(z < last)
        def _():
            spread_up(p, z).start()

        @pl.when(z > 0)
        def _():
            spread_down(p, z).start()

    def spread_forward(p, hops):
        for d in hops:
            @pl.when(z - d >= 0)
            def _():
                spread_up(p, z - d).wait_recv()
                if orders[p]:
                    start(row_spread(p, z - d))

                @pl.when(z < last)
                def _():
                    spread_up(p, z - d).start()

            @pl.when(z + d < outer)
            def _():
                spread_down(p, z + d).wait_recv()
                if orders[p]:
                    start(row_spread(p, z + d))

                @pl.when(z > 0)
                def _():
                    spread_down(p, z + d).start()

    def chain_sent(p):
        for d in range(1, outer):
            @pl.when(z + d < outer)
            def _():
                chain_up(p, z + d).wait_send()

            @pl.when(z - d >= 0)
            def _():
                chain_down(p, z - d).wait_send()

        for d in range(outer):
            @pl.when((z < last) & (z - d >= 0))
            def _():
                spread_up(p, z - d).wait_send()

            @pl.when((z > 0) & (z + d < outer))
            def _():
                spread_down(p, z + d).wait_send()

    def peers(p, src, dst, send, recv):
        return [
            remote(
                src((y + k) % inner), dst(k - 1), send[p].at[k - 1], recv[p].at[k - 1],
                (z * inner + (y + k) % inner, mt),
            )
            for k in range(1, inner)
        ]

    def inner_sum(p):
        if orders[p]:
            return peers(
                p, lambda to: r.loc[p].at[pl.ds(to * outer, outer)], lambda k: r.inbox[p].at[k], r.i_s, r.i_r
            )
        return peers(
            p, lambda to: r.held[p].at[pl.ds(to, 1)], lambda k: r.inbox[p].at[k], r.i_s, r.i_r
        )

    def row_spread(p, j):
        block = r.full[p].at[chunk(p, j)]
        return [
            remote(
                block, block, r.o_s[p].at[k - 1, j], r.o_r[p].at[k - 1, j],
                (z * inner + (y + k) % inner, mt),
            )
            for k in range(1, inner)
        ]

    def inner_spread(p):
        if orders[p]:
            return [copy for j in range(outer) for copy in row_spread(p, j)]
        block = r.full[p].at[pl.ds(z * inner + y, 1)]
        return [
            remote(
                block, block, r.o_s[p].at[k - 1, 0], r.o_r[p].at[k - 1, 0],
                (z * inner + (y + k) % inner, mt),
            )
            for k in range(1, inner)
        ]

    def advance(step, *which):
        for p in which:
            if orders[p]:
                inner_first_step(step, p)
            else:
                outer_first_step(step, p)

    sum_hops = np.array_split(np.arange(1, last), 2)
    spread_hops = np.array_split(np.arange(1, outer), 3)

    def inner_first_step(step, p):
        if step == 0:
            start(inner_sum(p))
        elif step == 1:
            arrive(inner_sum(p))
            acc = r.loc[p][pl.ds(y * outer, outer)].astype(F32)
            for k in range(inner - 1):
                acc = acc + r.inbox[p][k].astype(F32)
            r.held[p][...] = acc.astype(BF16)
            chain_start(p)
        elif step <= 3:
            chain_forward(p, sum_hops[step - 2].tolist())
        elif step == 4:
            chain_finish(p, r.full[p].at[chunk(p, z)])
            spread_start(p)
            start(row_spread(p, z))
        elif step <= 7:
            spread_forward(p, spread_hops[step - 5].tolist())
        else:
            arrive(inner_spread(p))

    def outer_first_step(step, p):
        if step == 0:
            chain_start(p)
        elif step <= 2:
            chain_forward(p, sum_hops[step - 1].tolist())
        elif step == 3:
            chain_finish(p, r.held[p])
            start(inner_sum(p))
        elif step == 4:
            arrive(inner_sum(p))
            acc = r.held[p][pl.ds(y, 1)].astype(F32)
            for k in range(inner - 1):
                acc = acc + r.inbox[p][k].astype(F32)
            r.full[p][pl.ds(z * inner + y, 1)] = acc.astype(BF16)
            start(inner_spread(p))
        elif step == 5:
            arrive(inner_spread(p))
            spread_start(p)
        else:
            spread_forward(p, spread_hops[step - 6].tolist())

    outs = []

    def write_out(src, dst):
        copy = pltpu.make_async_copy(src, dst, r.out_sem.at[len(outs)])
        copy.start()
        outs.append(copy)

    def small_exchange(g, src, axis):
        size = outer if axis else inner
        out = []
        for k in range(1, size):
            if axis:
                to = ((z + k) % outer) * inner + y
            else:
                to = z * inner + (y + k) % inner
            out.append(remote(
                src, g.inbox[axis].at[k - 1], g.send[axis].at[k - 1], g.recv[axis].at[k - 1], (to, mt)
            ))
        return out

    def small_tensor(g, src, slots):
        return [
            remote(
                src, slots(k), g.send[2].at[k - 1], g.recv[2].at[k - 1], (me, (mt + k) % 4)
            )
            for k in range(1, 4)
        ]

    gn, rt = SimpleNamespace(**r.gn), SimpleNamespace(**r.rt)
    lane = lax.broadcasted_iota(jnp.int32, (R, LANES), 1)
    low = lane < HEAD_SIZE
    first_half = (lane % HEAD_SIZE) < HEAD_SIZE // 2

    def swap(v):
        return jnp.where(first_half, pltpu.roll(v, 96, 1), pltpu.roll(v, 32, 1))

    CH = 32

    def row_chunks(body):
        def step(i, _):
            body(pl.ds(pl.multiple_of(i * CH, CH), CH))
            return 0

        lax.fori_loop(0, R // CH, step, 0)

    def own_chunk(rows):
        return pl.ds(pl.multiple_of(mt * R + rows.start, CH), CH)

    load[0].wait()
    load[17].wait()

    def norm_rows(rows):
        h = r.hid[rows, :].astype(F32)
        inv = lax.rsqrt(jnp.mean(h * h, axis=-1, keepdims=True) + EPS)
        r.xa[own_chunk(rows), :] = (h * inv * r.gain_attn[...]).astype(BF16)

    row_chunks(norm_rows)

    pl.semaphore_wait(barrier, 3 + (inner - 1) + (outer - 1))

    ag_xa = gather(0, r.xa)
    gather_start(ag_xa)
    load[1].wait()
    ag_cot = gather(1, r.cot)
    ag_cot[1].start()
    for copy in load[2:7] + load[16:17]:
        copy.wait()

    r.gk[...] = jnp.zeros_like(r.gk)
    r.gv[...] = jnp.zeros_like(r.gv)
    gn.own[...] = jnp.zeros_like(gn.own)

    def project(k, _):
        gather_step(k, ag_xa)
        b = block_of(3 - k)
        rows = rows_of(b)
        qkv = nn(r.xa[rows, :], r.wqkv[...])
        cos, sin = r.cos[rows, :], r.sin[rows, :]

        def rope(v):
            return v * cos + swap(v) * sin

        zero = jnp.zeros((R, LANES), F32)
        q0 = rope(qkv[:, 0:128]) * HEAD_SIZE ** (-0.5)
        q1 = rope(qkv[:, 128:256]) * HEAD_SIZE ** (-0.5)
        kk = rope(qkv[:, 256:384])
        vv = qkv[:, 384:512]
        r.q[rows, 0:128] = q0.astype(BF16)
        r.q[rows, 128:256] = q1.astype(BF16)
        r.qp[b, 0 * R:1 * R, :] = jnp.where(low, q0, zero).astype(BF16)
        r.qp[b, 1 * R:2 * R, :] = jnp.where(low, pltpu.roll(q0, 64, 1), zero).astype(BF16)
        r.qp[b, 2 * R:3 * R, :] = jnp.where(low, zero, pltpu.roll(q1, 64, 1)).astype(BF16)
        r.qp[b, 3 * R:4 * R, :] = jnp.where(low, zero, q1).astype(BF16)
        for dst, val in ((r.klh, kk), (r.vlh, vv)):
            turned = pltpu.roll(val, 64, 1)
            dst[0, rows, :] = jnp.where(low, val, zero).astype(BF16)
            dst[1, rows, :] = jnp.where(low, zero, turned).astype(BF16)
            dst[2, rows, :] = jnp.where(low, turned, zero).astype(BF16)
            dst[3, rows, :] = jnp.where(low, zero, val).astype(BF16)
        return 0

    lax.fori_loop(0, 4, project, 0)
    ag_cot[0].start()
    load[7].wait()

    KW = 3 * R
    rs1 = scatter(0, W)

    def attend(k, _):
        b = block_of(k)
        rows = rows_of(b)
        wstart = (b // 3) * R
        win = pl.ds(pl.multiple_of(wstart, R), KW)
        seg_q = r.seg[0:1, rows].astype(F32)
        seg_col = jnp.transpose(jnp.broadcast_to(seg_q, (R, R)))[:, 0:1]
        seg_k = r.seg[0:1, win].astype(F32)
        at_q = lax.broadcasted_iota(jnp.int32, (R, KW), 0) + (b * R - wstart)
        at_k = lax.broadcasted_iota(jnp.int32, (R, KW), 1)
        bias = jnp.where((seg_col == seg_k) & (at_k <= at_q), 0.0, NEGATIVE)
        for kv in range(2):
            q = r.q[rows, kv * LANES:(kv + 1) * LANES]
            mixed = jnp.zeros((R, LANES), F32)
            for h in range(2):
                i = kv * 2 + h
                s = nt(q, r.klh[i, win, :]) + bias
                e = jnp.exp(s - jnp.max(s, axis=-1, keepdims=True))
                prob = (e * (1.0 / jnp.sum(e, axis=-1, keepdims=True))).astype(BF16)
                r.prob[b, i * R:(i + 1) * R, :] = prob
                mixed = mixed + nn(prob, r.vlh[i, win, :])
            r.mixed[rows, kv * LANES:(kv + 1) * LANES] = mixed.astype(BF16)
        r.part[...] = nn(r.mixed[rows, :], r.wo[...])
        scatter_step(k, 0, rs1, r.part)
        return 0

    lax.fori_loop(0, 4, attend, 0)
    for copy in load[8:16]:
        copy.wait()
    rs1[2].wait_recv()
    rs1[1].wait_recv()

    def after_rows(rows):
        a = r.hid[rows, :].astype(F32) + (
            r.part[rows, :] + r.rp[0][1, rows, :].astype(F32) + r.rx[0][rows, :].astype(F32)
        )
        r.after[rows, :] = a
        inv = lax.rsqrt(jnp.mean(a * a, axis=-1, keepdims=True) + EPS)
        r.xf[own_chunk(rows), :] = (a * inv * r.gain_ffn[...]).astype(BF16)

    row_chunks(after_rows)
    ag_xf = gather(2, r.xf)
    gather_start(ag_xf)

    E = r.wr.shape[0]
    expert = lax.broadcasted_iota(jnp.int32, (R, E), 1)
    logits = nt(r.xf[rows_of(mt), :], r.wr[...])
    el = jnp.exp(logits - jnp.max(logits, axis=-1, keepdims=True))
    router_probs = el / jnp.sum(el, axis=-1, keepdims=True)
    routes = r.routes[...]

    def count(e):
        named = jnp.sum((routes == e).astype(F32), axis=0, keepdims=True)
        return jnp.transpose(jnp.broadcast_to(named, (R, R)))[:, 0:1]

    count0, count1 = count(0), count(1)
    counts = jnp.where(expert == 0, count0, jnp.where(expert == 1, count1, 0.0))
    r.rprobs[...] = router_probs
    r.counts[...] = counts
    r.cb[rows_of(mt), :] = jnp.zeros((R, LANES), BF16)
    r.cb[rows_of(mt), 0:E] = (router_probs * counts).astype(BF16)
    ag_cb = gather(3, r.cb)
    gather_start(ag_cb)

    ag_cot[1].wait_recv()
    ag_cot[0].wait_recv()
    ag_cot[2].start()
    H2 = r.wd.shape[0]

    def experts(k, _):
        gather_step(k, ag_xf, ag_cb)

        @pl.when(k == 3)
        def _():
            ag_cot[2].wait_recv()

        b = block_of(3 - k)
        rows = rows_of(b)
        gu = nn(r.xf[rows, :], r.wgu[...])
        down = nt(r.cot[rows, :], r.wd[...])
        cb = r.cb[rows, :].astype(F32)
        gcol = jnp.zeros((R, LANES), F32)
        for e in range(2):
            cols = slice(e * LANES, (e + 1) * LANES)
            up_cols = slice(H2 + e * LANES, H2 + (e + 1) * LANES)
            g, u, a = gu[:, cols], gu[:, up_cols], down[:, cols]
            c = cb[:, e:e + 1]
            sig = 1.0 / (1.0 + jnp.exp(-g))
            silu = g * sig
            act = silu * u
            ga = c * a
            r.ci[rows, cols] = (c * act).astype(BF16)
            r.dgu[rows, cols] = (ga * u * (sig * (1.0 + g * (1.0 - sig)))).astype(BF16)
            r.dgu[rows, up_cols] = (ga * silu).astype(BF16)
            gcol = jnp.where(lane == e, jnp.sum(act * a, axis=-1, keepdims=True), gcol)
        r.pr[rows, 0:W] = nt(r.dgu[rows, :], r.wgu[...])
        r.pr[rows, W:W + LANES] = gcol
        return 0

    lax.fori_loop(0, 4, experts, 0)
    rs2 = scatter(1, W + LANES)
    for k in (0, 2, 1):
        scatter_step(k, 1, rs2, r.pr.at[rows_of(block_of(k))])

    depth = W // n

    def store_piece(p, row, tile):
        count = tile.shape[0] // depth
        r.loc[p][pl.ds(row * count, count)] = tile.astype(BF16).reshape(count, depth, PIECE_COLS)

    def tiles(first, second, left, right):
        def step(i, _):
            cols = pl.ds(pl.multiple_of(i * 256, 256), 256)
            tile = tn(left[:, cols], right[...])
            store_piece(first, i, tile[:, 0:PIECE_COLS])
            store_piece(second, i, tile[:, PIECE_COLS:])
            return 0

        lax.fori_loop(0, W // 256, step, 0)
        advance(0, first, second)

    def tiles_by_columns(p, left, right):
        def step(i, _):
            cols = pl.ds(pl.multiple_of(i * 256, 256), 256)
            store_piece(p, i, tn(left[...], right[:, cols]))
            return 0

        lax.fori_loop(0, W // 256, step, 0)
        advance(0, p)

    tiles(GATE, UP, r.xf, r.dgu)
    tiles_by_columns(DOWN, r.ci, r.cot)

    rs2[2].wait_recv()
    rs2[1].wait_recv()
    own = rows_of(mt)
    gcomb = (
        r.pr[own, W:W + LANES]
        + r.rp[1][1, :, W:W + LANES].astype(F32)
        + r.rx[1][:, W:W + LANES].astype(F32)
    )[:, 0:E]
    grp = gcomb * r.counts[...]
    rp = r.rprobs[...]
    glog = (rp * (grp - jnp.sum(rp * grp, axis=-1, keepdims=True))).astype(BF16)
    r.ga[own, W:W + LANES] = jnp.zeros((R, LANES), BF16)
    r.ga[own, W:W + E] = glog
    r.part[...] = nn(glog, r.wr[...])

    def grad_after_rows(rows):
        a = r.after[rows, :]
        inv = lax.rsqrt(jnp.mean(a * a, axis=-1, keepdims=True) + EPS)
        unit = a * inv
        g = (
            r.part[rows, :]
            + r.pr[own_chunk(rows), 0:W]
            + r.rp[1][1, rows, 0:W].astype(F32)
            + r.rx[1][rows, 0:W].astype(F32)
        )
        gn.own[0:1, :] += jnp.sum(g * unit, axis=0, keepdims=True)
        scaled = g * r.gain_ffn[...]
        back = inv * (scaled - unit * jnp.mean(scaled * unit, axis=-1, keepdims=True))
        ga = back + r.cot[own_chunk(rows), :].astype(F32)
        r.ga_own[rows, :] = ga
        r.ga[own_chunk(rows), 0:W] = ga.astype(BF16)

    row_chunks(grad_after_rows)
    ag_ga = gather(4, r.ga)
    gather_start(ag_ga)
    advance(1, GATE, UP)

    def attend_back(k, _):
        @pl.when(k == 2)
        def _():
            advance(2, GATE, UP)
            advance(1, DOWN)

        gather_step(k, ag_ga)

        @pl.when(k == 3)
        def _():
            advance(3, GATE, UP)

        b = block_of(3 - k)
        rows = rows_of(b)
        wstart = (b // 3) * R
        win = pl.ds(pl.multiple_of(wstart, R), KW)
        gm = nt(r.ga[rows, 0:W], r.wo[...])
        zero = jnp.zeros((R, LANES), F32)
        for kv in range(2):
            cols = slice(kv * LANES, (kv + 1) * LANES)
            gmk = gm[:, cols].astype(BF16)
            gmf = gmk.astype(F32)
            turned = pltpu.roll(gmf, 64, 1)
            if kv == 0:
                r.gmp[0 * R:1 * R, :] = jnp.where(low, gmf, zero).astype(BF16)
                r.gmp[1 * R:2 * R, :] = jnp.where(low, turned, zero).astype(BF16)
            else:
                r.gmp[2 * R:3 * R, :] = jnp.where(low, zero, turned).astype(BF16)
                r.gmp[3 * R:4 * R, :] = jnp.where(low, zero, gmf).astype(BF16)
            prod = gmf * r.mixed[rows, cols].astype(F32)
            delta_lo = jnp.sum(jnp.where(low, prod, zero), axis=-1, keepdims=True)
            delta_hi = jnp.sum(jnp.where(low, zero, prod), axis=-1, keepdims=True)
            gq = zero
            for h, delta in ((0, delta_lo), (1, delta_hi)):
                i = kv * 2 + h
                head = slice(i * R, (i + 1) * R)
                dp = nt(gmk, r.vlh[i, win, :])
                ds = (r.prob[b, head, :].astype(F32) * (dp - delta)).astype(BF16)
                r.ds[head, :] = ds
                gq = gq + nn(ds, r.klh[i, win, :])
            gq = gq * HEAD_SIZE ** (-0.5)
            gq = gq * r.cos[rows, :] - swap(gq) * r.sin[rows, :]
            r.dqkv[rows, cols] = gq.astype(BF16)
        r.gk[win, :] += tn(r.ds[...], r.qp[b])
        r.gv[win, :] += tn(r.prob[b], r.gmp[...])
        return 0

    lax.fori_loop(0, 4, attend_back, 0)
    advance(4, GATE, UP)
    advance(2, DOWN)


    def finish_kv(k, _):
        rows = rows_of(k)
        gk = r.gk[rows, :]
        gk = gk * r.cos[rows, :] - swap(gk) * r.sin[rows, :]
        r.dqkv[rows, 256:384] = gk.astype(BF16)
        r.dqkv[rows, 384:512] = r.gv[rows, :].astype(BF16)
        return 0

    lax.fori_loop(0, 4, finish_kv, 0)
    tiles(QUERY, KEYS, r.xa, r.dqkv)
    tiles_by_columns(OUT, r.mixed, r.ga)
    advance(5, GATE, UP)
    advance(3, DOWN)
    rs3 = scatter(2, W)

    def input_part(k, _):
        r.part[...] = nt(r.dqkv[rows_of(block_of(k)), :], r.wqkv[...])
        scatter_step(k, 2, rs3, r.part)
        return 0

    lax.fori_loop(0, 4, input_part, 0)
    advance(6, GATE, UP)
    advance(4, DOWN)
    quarter = pl.ds(pl.multiple_of(mt * (W // 4), W // 4), W // 4)
    rt.own[...] = tn(r.ga[:, W:W + LANES], r.xf[:, quarter])[0:E, :]
    rt0 = small_exchange(rt, rt.own, 0)
    start(rt0)

    advance(1, QUERY, KEYS, OUT)
    advance(7, GATE, UP)
    advance(5, DOWN)
    advance(2, QUERY, KEYS, OUT)
    rs3[2].wait_recv()
    rs3[1].wait_recv()

    def grad_in_rows(rows):
        h = r.hid[rows, :].astype(F32)
        inv = lax.rsqrt(jnp.mean(h * h, axis=-1, keepdims=True) + EPS)
        unit = h * inv
        g = r.part[rows, :] + r.rp[2][1, rows, :].astype(F32) + r.rx[2][rows, :].astype(F32)
        gn.own[1:2, :] += jnp.sum(g * unit, axis=0, keepdims=True)
        scaled = g * r.gain_attn[...]
        back = inv * (scaled - unit * jnp.mean(scaled * unit, axis=-1, keepdims=True))
        r.grad_in_v[rows, :] = back + r.ga_own[rows, :]

    row_chunks(grad_in_rows)
    write_out(r.grad_in_v, r.grad_in)
    gt = small_tensor(gn, gn.own, lambda k: gn.inbox[2].at[k - 1])
    start(gt)
    advance(6, DOWN)
    advance(8, UP)
    advance(3, QUERY, KEYS, OUT)

    rs4 = scatter(3, W)

    def output_part(k, _):
        r.part[...] = nn(r.ci[rows_of(block_of(k)), :], r.wd[...])
        scatter_step(k, 3, rs4, r.part)
        return 0

    lax.fori_loop(0, 4, output_part, 0)
    advance(4, QUERY, KEYS, OUT)
    advance(7, DOWN)

    arrive(gt)
    total = gn.own[...]
    for k in range(3):
        total = total + gn.inbox[2][k]
    gn.first[...] = total
    g0 = small_exchange(gn, gn.first, 0)
    start(g0)
    arrive(rt0)
    total = rt.own[...]
    for k in range(inner - 1):
        total = total + rt.inbox[0][k]
    rt.first[...] = total
    rt1 = small_exchange(rt, rt.first, 1)
    start(rt1)
    advance(5, QUERY, KEYS, OUT)

    rs4[2].wait_recv()
    rs4[1].wait_recv()

    def output_rows(rows):
        a = r.part[rows, :] + r.rp[3][1, rows, :].astype(F32) + r.rx[3][rows, :].astype(F32)
        r.output_v[rows, :] = (r.after[rows, :] + a).astype(BF16)

    row_chunks(output_rows)
    write_out(r.output_v, r.output)
    advance(6, QUERY, KEYS, OUT)

    arrive(g0)
    total = gn.first[...]
    for k in range(inner - 1):
        total = total + gn.inbox[0][k]
    gn.second[...] = total
    g1 = small_exchange(gn, gn.second, 1)
    start(g1)
    arrive(rt1)
    total = rt.first[...]
    for k in range(outer - 1):
        total = total + rt.inbox[1][k]
    r.router_v[mt] = total
    rtt = small_tensor(rt, r.router_v.at[mt], lambda k: r.router_v.at[mt])
    start(rtt)
    advance(7, QUERY, KEYS, OUT)

    arrive(g1)
    total = gn.second[...]
    for k in range(outer - 1):
        total = total + gn.inbox[1][k]
    r.gains_v[...] = total
    write_out(r.gains_v, r.gains)
    arrive(rtt)
    write_out(r.router_v, r.router)
    for p in (UP, GATE, DOWN, KEYS, QUERY, OUT):
        if p != UP:
            advance(8, p)
        write_out(r.full[p], r.pieces[p])

    for copy in outs:
        copy.wait()

    for g in (ag_xa, ag_cot, ag_xf, ag_cb, ag_ga, rs1, rs2, rs3, rs4, rt0, rt1, rtt, gt, g0, g1):
        for copy in g:
            copy.wait_send()
    for p in range(6):
        chain_sent(p)
        for copy in inner_sum(p) + inner_spread(p):
            copy.wait_send()


def finish_kernel(r):
    copies = []

    def put(src, dst):
        copy = pltpu.make_async_copy(src, dst, r.sem.at[len(copies)])
        copy.start()
        copies.append(copy)
        return copy

    loads = [
        put(src, dst)
        for src, dst in list(zip(r.pieces, r.v_pieces))
        + [(r.router, r.v_router), (r.output, r.v_output), (r.grad_in, r.v_grad_in), (r.gains, r.v_gains)]
    ]
    experts, _, hidden = r.o_gate.shape
    for p, dst, out in ((GATE, r.t_gate, r.o_gate), (UP, r.t_up, r.o_up)):
        loads[p].wait()
        for e in range(experts):
            dst[e] = r.v_pieces[p][:, e * hidden:(e + 1) * hidden].astype(F32)
        put(dst, out)
    for p, dst, out in ((DOWN, r.t_down, r.o_down), (OUT, r.t_wo, r.o_wo)):
        loads[p].wait()
        rows, cols = dst.shape[0], PIECE_COLS
        for i in range(r.v_pieces[p].shape[0] // rows):
            dst[:, i * cols:(i + 1) * cols] = r.v_pieces[p][i * rows:(i + 1) * rows, :].astype(F32)
        put(dst, out)
    loads[QUERY].wait()
    r.t_wq[...] = r.v_pieces[QUERY][...].astype(F32)
    put(r.t_wq, r.o_wq)
    loads[KEYS].wait()
    cols = r.t_wk.shape[1]
    r.t_wk[...] = r.v_pieces[KEYS][:, 0:cols].astype(F32)
    put(r.t_wk, r.o_wk)
    r.t_wv[...] = r.v_pieces[KEYS][:, cols:2 * cols].astype(F32)
    put(r.t_wv, r.o_wv)
    for load in loads[KEYS + 1:]:
        load.wait()
    put(r.v_output, r.o_output)
    put(r.v_grad_in, r.o_grad_in)
    r.t_gain_ffn[...] = r.v_gains[0:1, :]
    r.t_gain_attn[...] = r.v_gains[1:2, :]
    put(r.t_gain_ffn, r.o_gain_ffn)
    put(r.t_gain_attn, r.o_gain_attn)
    cols = r.v_router.shape[2]
    for i in range(r.v_router.shape[0]):
        r.t_router[:, i * cols:(i + 1) * cols] = r.v_router[i]
    put(r.t_router, r.o_router)
    for copy in copies[len(loads):]:
        copy.wait()


def rotary_tables(rows):
    half = HEAD_SIZE // 2
    freq = THETA ** (-(np.arange(half, dtype=np.float64) * 2.0 / HEAD_SIZE))
    angles = np.arange(rows, dtype=np.float64)[:, None] * freq[None, :]
    cos, sin = np.cos(angles), np.sin(angles)
    cos = np.concatenate([cos] * 4, axis=1).astype(np.float32)
    sin = np.concatenate([-sin, sin] * 2, axis=1).astype(np.float32)
    return jnp.asarray(cos), jnp.asarray(sin)


def on_device(
    hidden_in,
    cotangent,
    segments,
    routes,
    gain_attn,
    w_query,
    key_matrix,
    value_matrix,
    attention_output_weight,
    gain_ffn,
    w_router,
    w_gate,
    w_up,
    w_down,
):
    n = lax.axis_size("dp")
    inner = math.isqrt(n)
    outer = n // inner
    R, W = hidden_in.shape
    S = segments.shape[1]
    E = w_router.shape[1]
    depth = W // n
    head_cols = attention_output_weight.shape[0]
    down_rows = w_down.shape[0] * w_down.shape[1]
    cos, sin = rotary_tables(S)
    orders = INNER_FIRST
    piece_cols = (PIECE_COLS,) * len(orders)

    hbm = pl.BlockSpec(memory_space=pl.ANY)
    in_hbm = dict(
        hidden_hbm=hidden_in,
        cot_hbm=cotangent,
        wq_hbm=w_query,
        wk_hbm=key_matrix,
        wv_hbm=value_matrix,
        cos_hbm=cos,
        sin_hbm=sin,
        wo_hbm=attention_output_weight,
        wg_hbm=w_gate,
        wu_hbm=w_up,
        wd_hbm=w_down.reshape(down_rows, W),
        seg_hbm=segments,
        routes_hbm=routes.T,
        gain_attn_hbm=gain_attn.reshape(1, W),
        gain_ffn_hbm=gain_ffn.reshape(1, W),
        wr_hbm=w_router.T,
    )
    shape = jax.ShapeDtypeStruct
    results = dict(
        output=shape((R, W), BF16),
        grad_in=shape((R, W), F32),
        gains=shape((2, W), F32),
        router=shape((4, E, W // 4), F32),
        pieces=[shape((n, depth, c), BF16) for c in piece_cols],
    )

    dma = pltpu.SemaphoreType.DMA
    half = functools.partial(pltpu.VMEM, dtype=BF16)
    full = functools.partial(pltpu.VMEM, dtype=F32)

    def small(rows, cols):
        return dict(
            own=full((rows, cols)),
            first=full((rows, cols)),
            second=full((rows, cols)),
            inbox=[full((size, rows, cols)) for size in (inner - 1, outer - 1, 3)],
            send=[dma((size,)) for size in (inner - 1, outer - 1, 3)],
            recv=[dma((size,)) for size in (inner - 1, outer - 1, 3)],
        )

    sizes = [(1, outer, outer) if order else (inner, 1, inner) for order in orders]
    sums = (W, W + LANES, W, W)
    scratch = dict(
        hid=half((R, W)),
        cot=half((S, W)),
        wqkv=half((W, 512)),
        cos=full((S, LANES)),
        sin=full((S, LANES)),
        wo=half((head_cols, W)),
        wgu=half((W, 512)),
        wd=half((down_rows, W)),
        xa=half((S, W)),
        xf=half((S, W)),
        cb=half((S, LANES)),
        ga=half((S, W + LANES)),
        q=half((S, 256)),
        qp=half((4, 4 * R, LANES)),
        klh=half((4, S, LANES)),
        vlh=half((4, S, LANES)),
        prob=half((4, 4 * R, 3 * R)),
        ds=half((4 * R, 3 * R)),
        gmp=half((4 * R, LANES)),
        mixed=half((S, head_cols)),
        part=full((R, W)),
        after=full((R, W)),
        rprobs=full((R, E)),
        counts=full((R, E)),
        ci=half((S, down_rows)),
        dgu=half((S, 512)),
        pr=full((S, W + LANES)),
        ga_own=full((R, W)),
        gk=full((S, LANES)),
        gv=full((S, LANES)),
        dqkv=half((S, 512)),
        gn=small(2, W),
        rt=small(E, W // 4),
        output_v=half((R, W)),
        grad_in_v=full((R, W)),
        gains_v=full((2, W)),
        router_v=full((4, E, W // 4)),
        full=[half((n, depth, c)) for c in piece_cols],
        seg=pltpu.VMEM((1, S), jnp.int32),
        routes=pltpu.VMEM((routes.shape[1], R), jnp.int32),
        gain_attn=full((1, W)),
        gain_ffn=full((1, W)),
        wr=half((E, W)),
        load_sem=dma((18,)),
        out_sem=dma((10,)),
        ag_send=dma((5, 3)),
        ag_recv=dma((5, 3)),
        rs_send=dma((4, 3)),
        rs_recv=dma((4, 3)),
        sb=[half((2, R, c)) for c in sums],
        sx=[half((R, c)) for c in sums],
        rp=[half((2, R, c)) for c in sums],
        rx=[half((R, c)) for c in sums],
        loc=[half((n, depth, c)) for c in piece_cols],
        held=[half((kept, depth, PIECE_COLS)) for _, _, kept in sizes],
        up_in=[half((outer, part, depth, PIECE_COLS)) for part, _, _ in sizes],
        down_in=[half((outer, part, depth, PIECE_COLS)) for part, _, _ in sizes],
        inbox=[half((inner - 1, part, depth, PIECE_COLS)) for _, part, _ in sizes],
        c_su=[dma((outer,)) for _ in sizes],
        c_ru=[dma((outer,)) for _ in sizes],
        c_sd=[dma((outer,)) for _ in sizes],
        c_rd=[dma((outer,)) for _ in sizes],
        g_su=[dma((outer,)) for _ in sizes],
        g_sd=[dma((outer,)) for _ in sizes],
        g_r=[dma((outer,)) for _ in sizes],
        i_s=[dma((inner - 1,)) for _ in sizes],
        i_r=[dma((inner - 1,)) for _ in sizes],
        o_s=[dma((inner - 1, outer)) for _ in sizes],
        o_r=[dma((inner - 1, outer)) for _ in sizes],
    )

    def call(kernel, specs, operands, results, result_spec, scratch, params):
        given, in_tree = jax.tree.flatten(operands)
        shapes, out_tree = jax.tree.flatten(results)
        inner_shapes, scratch_tree = jax.tree.flatten(scratch)

        def body(*refs):
            a, b = len(given), len(given) + len(shapes)
            named = jax.tree.unflatten(in_tree, refs[:a])
            named.update(jax.tree.unflatten(out_tree, refs[a:b]))
            named.update(jax.tree.unflatten(scratch_tree, refs[b:]))
            kernel(SimpleNamespace(**named))

        got = pl.pallas_call(
            body,
            out_shape=shapes,
            in_specs=jax.tree.flatten(specs)[0],
            out_specs=[result_spec] * len(shapes),
            scratch_shapes=inner_shapes,
            compiler_params=params,
        )(*given)
        return SimpleNamespace(**jax.tree.unflatten(out_tree, got))

    specs = {key: hbm for key in in_hbm}
    got = call(
        functools.partial(layer_kernel, n, inner, orders),
        specs, in_hbm, results, hbm, scratch,
        pltpu.CompilerParams(collective_id=0, has_side_effects=True, vmem_limit_bytes=VMEM_LIMIT),
    )

    ready = dict(
        output=got.output,
        grad_in=got.grad_in,
        gains=got.gains,
        router=got.router,
        pieces=[piece.reshape(W, PIECE_COLS) for piece in got.pieces],
    )
    finals = dict(
        o_output=shape((R, W), BF16),
        o_grad_in=shape((R, W), F32),
        o_gain_ffn=shape((1, W), F32),
        o_gain_attn=shape((1, W), F32),
        o_gate=shape(w_gate.shape, F32),
        o_up=shape(w_up.shape, F32),
        o_down=shape((down_rows, W), F32),
        o_wo=shape(attention_output_weight.shape, F32),
        o_wq=shape(w_query.shape, F32),
        o_wk=shape(key_matrix.shape, F32),
        o_wv=shape(value_matrix.shape, F32),
        o_router=shape((E, W), F32),
    )
    temps = dict(
        t_gate=full(w_gate.shape),
        t_up=full(w_up.shape),
        t_down=full((down_rows, W)),
        t_wo=full(attention_output_weight.shape),
        t_wq=full(w_query.shape),
        t_wk=full(key_matrix.shape),
        t_wv=full(value_matrix.shape),
        t_router=full((E, W)),
        v_pieces=[half((W, PIECE_COLS)) for _ in piece_cols],
        v_router=full((4, E, W // 4)),
        v_output=half((R, W)),
        v_grad_in=full((R, W)),
        v_gains=full((2, W)),
        t_gain_ffn=full((1, W)),
        t_gain_attn=full((1, W)),
        sem=dma((len(finals) + 10,)),
    )
    done = call(
        finish_kernel, jax.tree.map(lambda _: hbm, ready), ready, finals, hbm, temps,
        pltpu.CompilerParams(vmem_limit_bytes=VMEM_LIMIT),
    )
    return (
        done.o_output,
        done.o_grad_in,
        done.o_gain_attn.reshape(W),
        done.o_wq,
        done.o_wk,
        done.o_wv,
        done.o_wo,
        done.o_gain_ffn.reshape(W),
        done.o_router.T,
        done.o_gate,
        done.o_up,
        done.o_down.reshape(w_down.shape),
    )


def solution(mesh):
    rows = P(("dp", "tensor"), None)
    columns = P(None, "tensor")
    return jax.shard_map(
        on_device,
        mesh=mesh,
        in_specs=(
            rows, rows, P("dp", None), rows, P(), columns, columns, columns,
            P("tensor", None), P(), P(), P(None, None, "tensor"), P(None, None, "tensor"),
            P(None, "tensor", None),
        ),
        out_specs=(
            rows, rows, P(), columns, columns, columns, P("tensor", None), P(), P(),
            P(None, None, "tensor"), P(None, None, "tensor"), P(None, "tensor", None),
        ),
        check_vma=False,
    )
```

```python
import functools
import math
from types import SimpleNamespace

import jax
import jax.numpy as jnp
import numpy as np
from jax import lax
from jax.experimental import pallas as pl
from jax.experimental.pallas import tpu as pltpu
from jax.sharding import PartitionSpec as P

HEAD_SIZE = 64
LANES = 128
EPS = 1e-06
THETA = 10000.0
NEGATIVE = -1e30
MESH = pl.DeviceIdType.MESH
F32 = jnp.float32
BF16 = jnp.bfloat16

GATE, UP, DOWN, OUT, QUERY, KEYS = range(6)
INNER_FIRST = (True, False, True, True, True, True)
PIECE_COLS = 256
VMEM_LIMIT = 61 * 1024 * 1024


def nt(left, right):
    return lax.dot_general(left, right, (((1,), (1,)), ((), ())), preferred_element_type=F32)


def tn(left, right):
    return lax.dot_general(left, right, (((0,), (0,)), ((), ())), preferred_element_type=F32)


def nn(left, right):
    return jnp.dot(left, right, preferred_element_type=F32)


def layer_kernel(n, inner, orders, r):
    outer = n // inner
    me = lax.axis_index("dp")
    mt = lax.axis_index("tensor")
    y = me % inner
    z = me // inner
    xc = mt // 2
    core = mt % 2
    pair = xc * 2 + (1 - core)
    across = (1 - xc) * 2 + core

    R, W = r.hid.shape
    S = r.xa.shape[0]
    HC = r.wo.shape[0]

    def remote(src, dst, send, recv, device):
        return pltpu.make_async_remote_copy(
            src_ref=src, dst_ref=dst, send_sem=send, recv_sem=recv,
            device_id=device, device_id_type=MESH,
        )

    def block_of(k):
        return ((xc + 1 - k // 2) % 2) * 2 + (core + 1 - k % 2) % 2

    def rows_of(block):
        return pl.ds(pl.multiple_of(block * R, R), R)

    loads = [
        (r.hidden_hbm, r.hid),
        (r.cot_hbm, r.cot.at[rows_of(mt)]),
        (r.wq_hbm, r.wqkv.at[:, 0:256]),
        (r.wk_hbm, r.wqkv.at[:, 256:384]),
        (r.wv_hbm, r.wqkv.at[:, 384:512]),
        (r.cos_hbm, r.cos),
        (r.sin_hbm, r.sin),
        (r.wo_hbm, r.wo),
        (r.wg_hbm.at[0], r.wgu.at[:, 0:128]),
        (r.wg_hbm.at[1], r.wgu.at[:, 128:256]),
        (r.wu_hbm.at[0], r.wgu.at[:, 256:384]),
        (r.wu_hbm.at[1], r.wgu.at[:, 384:512]),
        (r.wd_hbm, r.wd),
        (r.wr_hbm, r.wr),
        (r.routes_hbm, r.routes),
        (r.gain_ffn_hbm, r.gain_ffn),
        (r.seg_hbm, r.seg),
        (r.gain_attn_hbm, r.gain_attn),
    ]
    load = [pltpu.make_async_copy(a, b, r.load_sem.at[i]) for i, (a, b) in enumerate(loads)]
    for copy in load:
        copy.start()

    barrier = pltpu.get_barrier_semaphore()
    for k in range(1, 4):
        pl.semaphore_signal(barrier, inc=1, device_id=(me, (mt + k) % 4), device_id_type=MESH)
    for k in range(1, inner):
        pl.semaphore_signal(
            barrier, inc=1, device_id=(z * inner + (y + k) % inner, mt), device_id_type=MESH
        )
    for k in range(1, outer):
        pl.semaphore_signal(
            barrier, inc=1, device_id=(((z + k) % outer) * inner + y, mt), device_id_type=MESH
        )

    def gather(i, buf):
        own = buf.at[rows_of(mt)]
        far = buf.at[rows_of(across)]
        ss, rs = r.ag_send, r.ag_recv
        return (
            remote(own, own, ss.at[i, 0], rs.at[i, 0], (me, across)),
            remote(own, own, ss.at[i, 1], rs.at[i, 1], (me, pair)),
            remote(far, far, ss.at[i, 2], rs.at[i, 2], (me, pair)),
        )

    def gather_start(g):
        g[0].start()
        g[1].start()

    def gather_step(k, *gs):
        @pl.when(k == 1)
        def _():
            for g in gs:
                g[1].wait_recv()

        @pl.when(k == 2)
        def _():
            for g in gs:
                g[0].wait_recv()
                g[2].start()

        @pl.when(k == 3)
        def _():
            for g in gs:
                g[2].wait_recv()

    def scatter(i, c):
        sb, sx, rp, rx = r.sb[i], r.sx[i], r.rp[i], r.rx[i]
        ss, rs = r.rs_send, r.rs_recv
        return (
            remote(sb.at[0], rp.at[0], ss.at[i, 0], rs.at[i, 0], (me, pair)),
            remote(sx, rx, ss.at[i, 1], rs.at[i, 1], (me, across)),
            remote(sb.at[1], rp.at[1], ss.at[i, 2], rs.at[i, 2], (me, pair)),
        )

    def scatter_step(k, i, c, part):
        sb, sx, rp = r.sb[i], r.sx[i], r.rp[i]

        @pl.when(k == 0)
        def _():
            sb[0] = part[...].astype(BF16)
            c[0].start()

        @pl.when(k == 1)
        def _():
            c[0].wait_recv()
            sx[...] = (part[...] + rp[0].astype(F32)).astype(BF16)
            c[1].start()

        @pl.when(k == 2)
        def _():
            sb[1] = part[...].astype(BF16)
            c[2].start()

    def start(copies):
        for copy in copies:
            copy.start()

    def arrive(copies):
        for copy in copies:
            copy.wait_recv()

    last = outer - 1
    ahead = ((z + 1) * inner + y, mt)
    behind = ((z - 1) * inner + y, mt)

    def chunk(p, j):
        if orders[p]:
            return pl.ds(y * outer + j, 1)
        return pl.ds(j * inner, inner)

    def partial(p, j):
        return r.held[p].at[pl.ds(j, 1)] if orders[p] else r.loc[p].at[chunk(p, j)]

    def chain_up(p, j):
        return remote(partial(p, j), r.up_in[p].at[j], r.c_su[p].at[j], r.c_ru[p].at[j], ahead)

    def chain_down(p, j):
        return remote(partial(p, j), r.down_in[p].at[j], r.c_sd[p].at[j], r.c_rd[p].at[j], behind)

    def spread_up(p, j):
        block = r.full[p].at[chunk(p, j)]
        return remote(block, block, r.g_su[p].at[j], r.g_r[p].at[j], ahead)

    def spread_down(p, j):
        block = r.full[p].at[chunk(p, j)]
        return remote(block, block, r.g_sd[p].at[j], r.g_r[p].at[j], behind)

    def chain_start(p):
        @pl.when(z == 0)
        def _():
            for d in range(last, 0, -1):
                chain_up(p, d).start()

        @pl.when(z == last)
        def _():
            for d in range(last, 0, -1):
                chain_down(p, last - d).start()

    def pass_on(copy, mine, came):
        copy.wait_recv()
        mine[...] = (mine[...].astype(F32) + came[...].astype(F32)).astype(BF16)
        copy.start()

    def chain_forward(p, hops):
        for hop in hops:
            @pl.when(z == hop)
            def _():
                for j in range(last, hop, -1):
                    pass_on(chain_up(p, j), partial(p, j), r.up_in[p].at[j])

            @pl.when(z == last - hop)
            def _():
                for j in range(last - hop):
                    pass_on(chain_down(p, j), partial(p, j), r.down_in[p].at[j])

    def chain_finish(p, dst):
        mine = partial(p, z)

        @pl.when(z == 0)
        def _():
            chain_down(p, z).wait_recv()
            dst[...] = (mine[...].astype(F32) + r.down_in[p][z].astype(F32)).astype(BF16)

        @pl.when(z == last)
        def _():
            chain_up(p, z).wait_recv()
            dst[...] = (mine[...].astype(F32) + r.up_in[p][z].astype(F32)).astype(BF16)

        @pl.when((z > 0) & (z < last))
        def _():
            chain_down(p, z).wait_recv()
            chain_up(p, z).wait_recv()
            dst[...] = (
                mine[...].astype(F32) + r.up_in[p][z].astype(F32) + r.down_in[p][z].astype(F32)
            ).astype(BF16)

    def spread_start(p):
        @pl.when(z < last)
        def _():
            spread_up(p, z).start()

        @pl.when(z > 0)
        def _():
            spread_down(p, z).start()

    def spread_forward(p, hops):
        for d in hops:
            @pl.when(z - d >= 0)
            def _():
                spread_up(p, z - d).wait_recv()
                if orders[p]:
                    start(row_spread(p, z - d))

                @pl.when(z < last)
                def _():
                    spread_up(p, z - d).start()

            @pl.when(z + d < outer)
            def _():
                spread_down(p, z + d).wait_recv()
                if orders[p]:
                    start(row_spread(p, z + d))

                @pl.when(z > 0)
                def _():
                    spread_down(p, z + d).start()

    def chain_sent(p):
        for d in range(1, outer):
            @pl.when(z + d < outer)
            def _():
                chain_up(p, z + d).wait_send()

            @pl.when(z - d >= 0)
            def _():
                chain_down(p, z - d).wait_send()

        for d in range(outer):
            @pl.when((z < last) & (z - d >= 0))
            def _():
                spread_up(p, z - d).wait_send()

            @pl.when((z > 0) & (z + d < outer))
            def _():
                spread_down(p, z + d).wait_send()

    def peers(p, src, dst, send, recv):
        return [
            remote(
                src((y + k) % inner), dst(k - 1), send[p].at[k - 1], recv[p].at[k - 1],
                (z * inner + (y + k) % inner, mt),
            )
            for k in range(1, inner)
        ]

    def inner_sum(p):
        if orders[p]:
            return peers(
                p, lambda to: r.loc[p].at[pl.ds(to * outer, outer)], lambda k: r.inbox[p].at[k], r.i_s, r.i_r
            )
        return peers(
            p, lambda to: r.held[p].at[pl.ds(to, 1)], lambda k: r.inbox[p].at[k], r.i_s, r.i_r
        )

    def row_spread(p, j):
        block = r.full[p].at[chunk(p, j)]
        return [
            remote(
                block, block, r.o_s[p].at[k - 1, j], r.o_r[p].at[k - 1, j],
                (z * inner + (y + k) % inner, mt),
            )
            for k in range(1, inner)
        ]

    def inner_spread(p):
        if orders[p]:
            return [copy for j in range(outer) for copy in row_spread(p, j)]
        block = r.full[p].at[pl.ds(z * inner + y, 1)]
        return [
            remote(
                block, block, r.o_s[p].at[k - 1, 0], r.o_r[p].at[k - 1, 0],
                (z * inner + (y + k) % inner, mt),
            )
            for k in range(1, inner)
        ]

    def advance(step, *which):
        for p in which:
            if orders[p]:
                inner_first_step(step, p)
            else:
                outer_first_step(step, p)

    sum_hops = np.array_split(np.arange(1, last), 2)
    spread_hops = np.array_split(np.arange(1, outer), 3)

    def inner_first_step(step, p):
        if step == 0:
            start(inner_sum(p))
        elif step == 1:
            arrive(inner_sum(p))
            acc = r.loc[p][pl.ds(y * outer, outer)].astype(F32)
            for k in range(inner - 1):
                acc = acc + r.inbox[p][k].astype(F32)
            r.held[p][...] = acc.astype(BF16)
            chain_start(p)
        elif step <= 3:
            chain_forward(p, sum_hops[step - 2].tolist())
        elif step == 4:
            chain_finish(p, r.full[p].at[chunk(p, z)])
            spread_start(p)
            start(row_spread(p, z))
        elif step <= 7:
            spread_forward(p, spread_hops[step - 5].tolist())
        else:
            arrive(inner_spread(p))

    def outer_first_step(step, p):
        if step == 0:
            chain_start(p)
        elif step <= 2:
            chain_forward(p, sum_hops[step - 1].tolist())
        elif step == 3:
            chain_finish(p, r.held[p])
            start(inner_sum(p))
        elif step == 4:
            arrive(inner_sum(p))
            acc = r.held[p][pl.ds(y, 1)].astype(F32)
            for k in range(inner - 1):
                acc = acc + r.inbox[p][k].astype(F32)
            r.full[p][pl.ds(z * inner + y, 1)] = acc.astype(BF16)
            start(inner_spread(p))
        elif step == 5:
            arrive(inner_spread(p))
            spread_start(p)
        else:
            spread_forward(p, spread_hops[step - 6].tolist())

    outs = []

    def write_out(src, dst):
        copy = pltpu.make_async_copy(src, dst, r.out_sem.at[len(outs)])
        copy.start()
        outs.append(copy)

    def small_exchange(g, src, axis):
        size = outer if axis else inner
        out = []
        for k in range(1, size):
            if axis:
                to = ((z + k) % outer) * inner + y
            else:
                to = z * inner + (y + k) % inner
            out.append(remote(
                src, g.inbox[axis].at[k - 1], g.send[axis].at[k - 1], g.recv[axis].at[k - 1], (to, mt)
            ))
        return out

    def small_tensor(g, src, slots):
        return [
            remote(
                src, slots(k), g.send[2].at[k - 1], g.recv[2].at[k - 1], (me, (mt + k) % 4)
            )
            for k in range(1, 4)
        ]

    gn, rt = SimpleNamespace(**r.gn), SimpleNamespace(**r.rt)
    lane = lax.broadcasted_iota(jnp.int32, (R, LANES), 1)
    low = lane < HEAD_SIZE
    first_half = (lane % HEAD_SIZE) < HEAD_SIZE // 2

    def swap(v):
        return jnp.where(first_half, pltpu.roll(v, 96, 1), pltpu.roll(v, 32, 1))

    CH = 32

    def row_chunks(body):
        def step(i, _):
            body(pl.ds(pl.multiple_of(i * CH, CH), CH))
            return 0

        lax.fori_loop(0, R // CH, step, 0)

    def own_chunk(rows):
        return pl.ds(pl.multiple_of(mt * R + rows.start, CH), CH)

    load[0].wait()
    load[17].wait()

    def norm_rows(rows):
        h = r.hid[rows, :].astype(F32)
        inv = lax.rsqrt(jnp.mean(h * h, axis=-1, keepdims=True) + EPS)
        r.xa[own_chunk(rows), :] = (h * inv * r.gain_attn[...]).astype(BF16)

    row_chunks(norm_rows)

    pl.semaphore_wait(barrier, 3 + (inner - 1) + (outer - 1))

    ag_xa = gather(0, r.xa)
    gather_start(ag_xa)
    load[1].wait()
    ag_cot = gather(1, r.cot)
    ag_cot[1].start()
    for copy in load[2:7] + load[16:17]:
        copy.wait()

    r.gk[...] = jnp.zeros_like(r.gk)
    r.gv[...] = jnp.zeros_like(r.gv)
    gn.own[...] = jnp.zeros_like(gn.own)

    def project(k, _):
        gather_step(k, ag_xa)
        b = block_of(3 - k)
        rows = rows_of(b)
        qkv = nn(r.xa[rows, :], r.wqkv[...])
        cos, sin = r.cos[rows, :], r.sin[rows, :]

        def rope(v):
            return v * cos + swap(v) * sin

        zero = jnp.zeros((R, LANES), F32)
        q0 = rope(qkv[:, 0:128]) * HEAD_SIZE ** (-0.5)
        q1 = rope(qkv[:, 128:256]) * HEAD_SIZE ** (-0.5)
        kk = rope(qkv[:, 256:384])
        vv = qkv[:, 384:512]
        r.q[rows, 0:128] = q0.astype(BF16)
        r.q[rows, 128:256] = q1.astype(BF16)
        r.qp[b, 0 * R:1 * R, :] = jnp.where(low, q0, zero).astype(BF16)
        r.qp[b, 1 * R:2 * R, :] = jnp.where(low, pltpu.roll(q0, 64, 1), zero).astype(BF16)
        r.qp[b, 2 * R:3 * R, :] = jnp.where(low, zero, pltpu.roll(q1, 64, 1)).astype(BF16)
        r.qp[b, 3 * R:4 * R, :] = jnp.where(low, zero, q1).astype(BF16)
        for dst, val in ((r.klh, kk), (r.vlh, vv)):
            turned = pltpu.roll(val, 64, 1)
            dst[0, rows, :] = jnp.where(low, val, zero).astype(BF16)
            dst[1, rows, :] = jnp.where(low, zero, turned).astype(BF16)
            dst[2, rows, :] = jnp.where(low, turned, zero).astype(BF16)
            dst[3, rows, :] = jnp.where(low, zero, val).astype(BF16)
        return 0

    lax.fori_loop(0, 4, project, 0)
    ag_cot[0].start()
    load[7].wait()

    KW = 3 * R
    rs1 = scatter(0, W)

    def attend(k, _):
        b = block_of(k)
        rows = rows_of(b)
        wstart = (b // 3) * R
        win = pl.ds(pl.multiple_of(wstart, R), KW)
        seg_q = r.seg[0:1, rows].astype(F32)
        seg_col = jnp.transpose(jnp.broadcast_to(seg_q, (R, R)))[:, 0:1]
        seg_k = r.seg[0:1, win].astype(F32)
        at_q = lax.broadcasted_iota(jnp.int32, (R, KW), 0) + (b * R - wstart)
        at_k = lax.broadcasted_iota(jnp.int32, (R, KW), 1)
        bias = jnp.where((seg_col == seg_k) & (at_k <= at_q), 0.0, NEGATIVE)
        for kv in range(2):
            q = r.q[rows, kv * LANES:(kv + 1) * LANES]
            mixed = jnp.zeros((R, LANES), F32)
            for h in range(2):
                i = kv * 2 + h
                s = nt(q, r.klh[i, win, :]) + bias
                e = jnp.exp(s - jnp.max(s, axis=-1, keepdims=True))
                prob = (e * (1.0 / jnp.sum(e, axis=-1, keepdims=True))).astype(BF16)
                r.prob[b, i * R:(i + 1) * R, :] = prob
                mixed = mixed + nn(prob, r.vlh[i, win, :])
            r.mixed[rows, kv * LANES:(kv + 1) * LANES] = mixed.astype(BF16)
        r.part[...] = nn(r.mixed[rows, :], r.wo[...])
        scatter_step(k, 0, rs1, r.part)
        return 0

    lax.fori_loop(0, 4, attend, 0)
    for copy in load[8:16]:
        copy.wait()
    rs1[2].wait_recv()
    rs1[1].wait_recv()

    def after_rows(rows):
        a = r.hid[rows, :].astype(F32) + (
            r.part[rows, :] + r.rp[0][1, rows, :].astype(F32) + r.rx[0][rows, :].astype(F32)
        )
        r.after[rows, :] = a
        inv = lax.rsqrt(jnp.mean(a * a, axis=-1, keepdims=True) + EPS)
        r.xf[own_chunk(rows), :] = (a * inv * r.gain_ffn[...]).astype(BF16)

    row_chunks(after_rows)
    ag_xf = gather(2, r.xf)
    gather_start(ag_xf)

    E = r.wr.shape[0]
    expert = lax.broadcasted_iota(jnp.int32, (R, E), 1)
    logits = nt(r.xf[rows_of(mt), :], r.wr[...])
    el = jnp.exp(logits - jnp.max(logits, axis=-1, keepdims=True))
    router_probs = el / jnp.sum(el, axis=-1, keepdims=True)
    routes = r.routes[...]

    def count(e):
        named = jnp.sum((routes == e).astype(F32), axis=0, keepdims=True)
        return jnp.transpose(jnp.broadcast_to(named, (R, R)))[:, 0:1]

    count0, count1 = count(0), count(1)
    counts = jnp.where(expert == 0, count0, jnp.where(expert == 1, count1, 0.0))
    r.rprobs[...] = router_probs
    r.counts[...] = counts
    r.cb[rows_of(mt), :] = jnp.zeros((R, LANES), BF16)
    r.cb[rows_of(mt), 0:E] = (router_probs * counts).astype(BF16)
    ag_cb = gather(3, r.cb)
    gather_start(ag_cb)

    ag_cot[1].wait_recv()
    ag_cot[0].wait_recv()
    ag_cot[2].start()
    H2 = r.wd.shape[0]

    def experts(k, _):
        gather_step(k, ag_xf, ag_cb)

        @pl.when(k == 3)
        def _():
            ag_cot[2].wait_recv()

        b = block_of(3 - k)
        rows = rows_of(b)
        gu = nn(r.xf[rows, :], r.wgu[...])
        down = nt(r.cot[rows, :], r.wd[...])
        cb = r.cb[rows, :].astype(F32)
        gcol = jnp.zeros((R, LANES), F32)
        for e in range(2):
            cols = slice(e * LANES, (e + 1) * LANES)
            up_cols = slice(H2 + e * LANES, H2 + (e + 1) * LANES)
            g, u, a = gu[:, cols], gu[:, up_cols], down[:, cols]
            c = cb[:, e:e + 1]
            sig = 1.0 / (1.0 + jnp.exp(-g))
            silu = g * sig
            act = silu * u
            ga = c * a
            r.ci[rows, cols] = (c * act).astype(BF16)
            r.dgu[rows, cols] = (ga * u * (sig * (1.0 + g * (1.0 - sig)))).astype(BF16)
            r.dgu[rows, up_cols] = (ga * silu).astype(BF16)
            gcol = jnp.where(lane == e, jnp.sum(act * a, axis=-1, keepdims=True), gcol)
        r.pr[rows, 0:W] = nt(r.dgu[rows, :], r.wgu[...])
        r.pr[rows, W:W + LANES] = gcol
        return 0

    lax.fori_loop(0, 4, experts, 0)
    rs2 = scatter(1, W + LANES)
    for k in (0, 2, 1):
        scatter_step(k, 1, rs2, r.pr.at[rows_of(block_of(k))])

    depth = W // n

    def store_piece(p, row, tile):
        count = tile.shape[0] // depth
        r.loc[p][pl.ds(row * count, count)] = tile.astype(BF16).reshape(count, depth, PIECE_COLS)

    def tiles(first, second, left, right):
        def step(i, _):
            cols = pl.ds(pl.multiple_of(i * 256, 256), 256)
            tile = tn(left[:, cols], right[...])
            store_piece(first, i, tile[:, 0:PIECE_COLS])
            store_piece(second, i, tile[:, PIECE_COLS:])
            return 0

        lax.fori_loop(0, W // 256, step, 0)
        advance(0, first, second)

    def tiles_by_columns(p, left, right):
        def step(i, _):
            cols = pl.ds(pl.multiple_of(i * 256, 256), 256)
            store_piece(p, i, tn(left[...], right[:, cols]))
            return 0

        lax.fori_loop(0, W // 256, step, 0)
        advance(0, p)

    tiles(GATE, UP, r.xf, r.dgu)
    tiles_by_columns(DOWN, r.ci, r.cot)

    rs2[2].wait_recv()
    rs2[1].wait_recv()
    own = rows_of(mt)
    gcomb = (
        r.pr[own, W:W + LANES]
        + r.rp[1][1, :, W:W + LANES].astype(F32)
        + r.rx[1][:, W:W + LANES].astype(F32)
    )[:, 0:E]
    grp = gcomb * r.counts[...]
    rp = r.rprobs[...]
    glog = (rp * (grp - jnp.sum(rp * grp, axis=-1, keepdims=True))).astype(BF16)
    r.ga[own, W:W + LANES] = jnp.zeros((R, LANES), BF16)
    r.ga[own, W:W + E] = glog
    r.part[...] = nn(glog, r.wr[...])

    def grad_after_rows(rows):
        a = r.after[rows, :]
        inv = lax.rsqrt(jnp.mean(a * a, axis=-1, keepdims=True) + EPS)
        unit = a * inv
        g = (
            r.part[rows, :]
            + r.pr[own_chunk(rows), 0:W]
            + r.rp[1][1, rows, 0:W].astype(F32)
            + r.rx[1][rows, 0:W].astype(F32)
        )
        gn.own[0:1, :] += jnp.sum(g * unit, axis=0, keepdims=True)
        scaled = g * r.gain_ffn[...]
        back = inv * (scaled - unit * jnp.mean(scaled * unit, axis=-1, keepdims=True))
        ga = back + r.cot[own_chunk(rows), :].astype(F32)
        r.ga_own[rows, :] = ga
        r.ga[own_chunk(rows), 0:W] = ga.astype(BF16)

    row_chunks(grad_after_rows)
    ag_ga = gather(4, r.ga)
    gather_start(ag_ga)
    advance(1, GATE, UP)

    def attend_back(k, _):
        @pl.when(k == 2)
        def _():
            advance(2, GATE, UP)
            advance(1, DOWN)

        gather_step(k, ag_ga)

        @pl.when(k == 3)
        def _():
            advance(3, GATE, UP)

        b = block_of(3 - k)
        rows = rows_of(b)
        wstart = (b // 3) * R
        win = pl.ds(pl.multiple_of(wstart, R), KW)
        gm = nt(r.ga[rows, 0:W], r.wo[...])
        zero = jnp.zeros((R, LANES), F32)
        for kv in range(2):
            cols = slice(kv * LANES, (kv + 1) * LANES)
            gmk = gm[:, cols].astype(BF16)
            gmf = gmk.astype(F32)
            turned = pltpu.roll(gmf, 64, 1)
            if kv == 0:
                r.gmp[0 * R:1 * R, :] = jnp.where(low, gmf, zero).astype(BF16)
                r.gmp[1 * R:2 * R, :] = jnp.where(low, turned, zero).astype(BF16)
            else:
                r.gmp[2 * R:3 * R, :] = jnp.where(low, zero, turned).astype(BF16)
                r.gmp[3 * R:4 * R, :] = jnp.where(low, zero, gmf).astype(BF16)
            prod = gmf * r.mixed[rows, cols].astype(F32)
            delta_lo = jnp.sum(jnp.where(low, prod, zero), axis=-1, keepdims=True)
            delta_hi = jnp.sum(jnp.where(low, zero, prod), axis=-1, keepdims=True)
            gq = zero
            for h, delta in ((0, delta_lo), (1, delta_hi)):
                i = kv * 2 + h
                head = slice(i * R, (i + 1) * R)
                dp = nt(gmk, r.vlh[i, win, :])
                ds = (r.prob[b, head, :].astype(F32) * (dp - delta)).astype(BF16)
                r.ds[head, :] = ds
                gq = gq + nn(ds, r.klh[i, win, :])
            gq = gq * HEAD_SIZE ** (-0.5)
            gq = gq * r.cos[rows, :] - swap(gq) * r.sin[rows, :]
            r.dqkv[rows, cols] = gq.astype(BF16)
        r.gk[win, :] += tn(r.ds[...], r.qp[b])
        r.gv[win, :] += tn(r.prob[b], r.gmp[...])
        return 0

    lax.fori_loop(0, 4, attend_back, 0)
    advance(4, GATE, UP)
    advance(2, DOWN)


    def finish_kv(k, _):
        rows = rows_of(k)
        gk = r.gk[rows, :]
        gk = gk * r.cos[rows, :] - swap(gk) * r.sin[rows, :]
        r.dqkv[rows, 256:384] = gk.astype(BF16)
        r.dqkv[rows, 384:512] = r.gv[rows, :].astype(BF16)
        return 0

    lax.fori_loop(0, 4, finish_kv, 0)
    tiles(QUERY, KEYS, r.xa, r.dqkv)
    tiles_by_columns(OUT, r.mixed, r.ga)
    advance(5, GATE, UP)
    advance(3, DOWN)
    rs3 = scatter(2, W)

    def input_part(k, _):
        r.part[...] = nt(r.dqkv[rows_of(block_of(k)), :], r.wqkv[...])
        scatter_step(k, 2, rs3, r.part)
        return 0

    lax.fori_loop(0, 4, input_part, 0)
    advance(6, GATE, UP)
    advance(4, DOWN)
    quarter = pl.ds(pl.multiple_of(mt * (W // 4), W // 4), W // 4)
    rt.own[...] = tn(r.ga[:, W:W + LANES], r.xf[:, quarter])[0:E, :]
    rt0 = small_exchange(rt, rt.own, 0)
    start(rt0)

    advance(1, QUERY, KEYS, OUT)
    advance(7, GATE, UP)
    advance(5, DOWN)
    advance(2, QUERY, KEYS, OUT)
    rs3[2].wait_recv()
    rs3[1].wait_recv()

    def grad_in_rows(rows):
        h = r.hid[rows, :].astype(F32)
        inv = lax.rsqrt(jnp.mean(h * h, axis=-1, keepdims=True) + EPS)
        unit = h * inv
        g = r.part[rows, :] + r.rp[2][1, rows, :].astype(F32) + r.rx[2][rows, :].astype(F32)
        gn.own[1:2, :] += jnp.sum(g * unit, axis=0, keepdims=True)
        scaled = g * r.gain_attn[...]
        back = inv * (scaled - unit * jnp.mean(scaled * unit, axis=-1, keepdims=True))
        r.grad_in_v[rows, :] = back + r.ga_own[rows, :]

    row_chunks(grad_in_rows)
    write_out(r.grad_in_v, r.grad_in)
    gt = small_tensor(gn, gn.own, lambda k: gn.inbox[2].at[k - 1])
    start(gt)
    advance(6, DOWN)
    advance(8, UP)
    advance(3, QUERY, KEYS, OUT)

    rs4 = scatter(3, W)

    def output_part(k, _):
        r.part[...] = nn(r.ci[rows_of(block_of(k)), :], r.wd[...])
        scatter_step(k, 3, rs4, r.part)
        return 0

    lax.fori_loop(0, 4, output_part, 0)
    advance(4, QUERY, KEYS, OUT)
    advance(7, DOWN)

    arrive(gt)
    total = gn.own[...]
    for k in range(3):
        total = total + gn.inbox[2][k]
    gn.first[...] = total
    g0 = small_exchange(gn, gn.first, 0)
    start(g0)
    arrive(rt0)
    total = rt.own[...]
    for k in range(inner - 1):
        total = total + rt.inbox[0][k]
    rt.first[...] = total
    rt1 = small_exchange(rt, rt.first, 1)
    start(rt1)
    advance(5, QUERY, KEYS, OUT)

    advance(6, QUERY, KEYS, OUT)

    arrive(g0)
    total = gn.first[...]
    for k in range(inner - 1):
        total = total + gn.inbox[0][k]
    gn.second[...] = total
    g1 = small_exchange(gn, gn.second, 1)
    start(g1)
    arrive(rt1)
    total = rt.first[...]
    for k in range(outer - 1):
        total = total + rt.inbox[1][k]
    r.router_v[mt] = total
    rtt = small_tensor(rt, r.router_v.at[mt], lambda k: r.router_v.at[mt])
    start(rtt)
    advance(7, QUERY, KEYS, OUT)
    rs4[2].wait_recv()
    rs4[1].wait_recv()

    def output_rows(rows):
        a = r.part[rows, :] + r.rp[3][1, rows, :].astype(F32) + r.rx[3][rows, :].astype(F32)
        r.output_v[rows, :] = (r.after[rows, :] + a).astype(BF16)

    row_chunks(output_rows)
    write_out(r.output_v, r.output)

    arrive(g1)
    total = gn.second[...]
    for k in range(outer - 1):
        total = total + gn.inbox[1][k]
    r.gains_v[...] = total
    write_out(r.gains_v, r.gains)
    arrive(rtt)
    write_out(r.router_v, r.router)
    for p in (UP, GATE, DOWN, KEYS, QUERY, OUT):
        if p != UP:
            advance(8, p)
        write_out(r.full[p], r.pieces[p])

    for copy in outs:
        copy.wait()

    for g in (ag_xa, ag_cot, ag_xf, ag_cb, ag_ga, rs1, rs2, rs3, rs4, rt0, rt1, rtt, gt, g0, g1):
        for copy in g:
            copy.wait_send()
    for p in range(6):
        chain_sent(p)
        for copy in inner_sum(p) + inner_spread(p):
            copy.wait_send()


def finish_kernel(r):
    copies = []

    def put(src, dst):
        copy = pltpu.make_async_copy(src, dst, r.sem.at[len(copies)])
        copy.start()
        copies.append(copy)
        return copy

    loads = [
        put(src, dst)
        for src, dst in list(zip(r.pieces, r.v_pieces))
        + [(r.router, r.v_router), (r.output, r.v_output), (r.grad_in, r.v_grad_in), (r.gains, r.v_gains)]
    ]
    experts, _, hidden = r.o_gate.shape
    for p, dst, out in ((GATE, r.t_gate, r.o_gate), (UP, r.t_up, r.o_up)):
        loads[p].wait()
        for e in range(experts):
            dst[e] = r.v_pieces[p][:, e * hidden:(e + 1) * hidden].astype(F32)
        put(dst, out)
    for p, dst, out in ((DOWN, r.t_down, r.o_down), (OUT, r.t_wo, r.o_wo)):
        loads[p].wait()
        rows, cols = dst.shape[0], PIECE_COLS
        for i in range(r.v_pieces[p].shape[0] // rows):
            dst[:, i * cols:(i + 1) * cols] = r.v_pieces[p][i * rows:(i + 1) * rows, :].astype(F32)
        put(dst, out)
    loads[QUERY].wait()
    r.t_wq[...] = r.v_pieces[QUERY][...].astype(F32)
    put(r.t_wq, r.o_wq)
    loads[KEYS].wait()
    cols = r.t_wk.shape[1]
    r.t_wk[...] = r.v_pieces[KEYS][:, 0:cols].astype(F32)
    put(r.t_wk, r.o_wk)
    r.t_wv[...] = r.v_pieces[KEYS][:, cols:2 * cols].astype(F32)
    put(r.t_wv, r.o_wv)
    for load in loads[KEYS + 1:]:
        load.wait()
    put(r.v_output, r.o_output)
    put(r.v_grad_in, r.o_grad_in)
    r.t_gain_ffn[...] = r.v_gains[0:1, :]
    r.t_gain_attn[...] = r.v_gains[1:2, :]
    put(r.t_gain_ffn, r.o_gain_ffn)
    put(r.t_gain_attn, r.o_gain_attn)
    cols = r.v_router.shape[2]
    for i in range(r.v_router.shape[0]):
        r.t_router[:, i * cols:(i + 1) * cols] = r.v_router[i]
    put(r.t_router, r.o_router)
    for copy in copies[len(loads):]:
        copy.wait()


def rotary_tables(rows):
    half = HEAD_SIZE // 2
    freq = THETA ** (-(np.arange(half, dtype=np.float64) * 2.0 / HEAD_SIZE))
    angles = np.arange(rows, dtype=np.float64)[:, None] * freq[None, :]
    cos, sin = np.cos(angles), np.sin(angles)
    cos = np.concatenate([cos] * 4, axis=1).astype(np.float32)
    sin = np.concatenate([-sin, sin] * 2, axis=1).astype(np.float32)
    return jnp.asarray(cos), jnp.asarray(sin)


def on_device(
    hidden_in,
    cotangent,
    segments,
    routes,
    gain_attn,
    w_query,
    key_matrix,
    value_matrix,
    attention_output_weight,
    gain_ffn,
    w_router,
    w_gate,
    w_up,
    w_down,
):
    n = lax.axis_size("dp")
    inner = math.isqrt(n)
    outer = n // inner
    R, W = hidden_in.shape
    S = segments.shape[1]
    E = w_router.shape[1]
    depth = W // n
    head_cols = attention_output_weight.shape[0]
    down_rows = w_down.shape[0] * w_down.shape[1]
    cos, sin = rotary_tables(S)
    orders = INNER_FIRST
    piece_cols = (PIECE_COLS,) * len(orders)

    hbm = pl.BlockSpec(memory_space=pl.ANY)
    in_hbm = dict(
        hidden_hbm=hidden_in,
        cot_hbm=cotangent,
        wq_hbm=w_query,
        wk_hbm=key_matrix,
        wv_hbm=value_matrix,
        cos_hbm=cos,
        sin_hbm=sin,
        wo_hbm=attention_output_weight,
        wg_hbm=w_gate,
        wu_hbm=w_up,
        wd_hbm=w_down.reshape(down_rows, W),
        seg_hbm=segments,
        routes_hbm=routes.T,
        gain_attn_hbm=gain_attn.reshape(1, W),
        gain_ffn_hbm=gain_ffn.reshape(1, W),
        wr_hbm=w_router.T,
    )
    shape = jax.ShapeDtypeStruct
    results = dict(
        output=shape((R, W), BF16),
        grad_in=shape((R, W), F32),
        gains=shape((2, W), F32),
        router=shape((4, E, W // 4), F32),
        pieces=[shape((n, depth, c), BF16) for c in piece_cols],
    )

    dma = pltpu.SemaphoreType.DMA
    half = functools.partial(pltpu.VMEM, dtype=BF16)
    full = functools.partial(pltpu.VMEM, dtype=F32)

    def small(rows, cols):
        return dict(
            own=full((rows, cols)),
            first=full((rows, cols)),
            second=full((rows, cols)),
            inbox=[full((size, rows, cols)) for size in (inner - 1, outer - 1, 3)],
            send=[dma((size,)) for size in (inner - 1, outer - 1, 3)],
            recv=[dma((size,)) for size in (inner - 1, outer - 1, 3)],
        )

    sizes = [(1, outer, outer) if order else (inner, 1, inner) for order in orders]
    sums = (W, W + LANES, W, W)
    scratch = dict(
        hid=half((R, W)),
        cot=half((S, W)),
        wqkv=half((W, 512)),
        cos=full((S, LANES)),
        sin=full((S, LANES)),
        wo=half((head_cols, W)),
        wgu=half((W, 512)),
        wd=half((down_rows, W)),
        xa=half((S, W)),
        xf=half((S, W)),
        cb=half((S, LANES)),
        ga=half((S, W + LANES)),
        q=half((S, 256)),
        qp=half((4, 4 * R, LANES)),
        klh=half((4, S, LANES)),
        vlh=half((4, S, LANES)),
        prob=half((4, 4 * R, 3 * R)),
        ds=half((4 * R, 3 * R)),
        gmp=half((4 * R, LANES)),
        mixed=half((S, head_cols)),
        part=full((R, W)),
        after=full((R, W)),
        rprobs=full((R, E)),
        counts=full((R, E)),
        ci=half((S, down_rows)),
        dgu=half((S, 512)),
        pr=full((S, W + LANES)),
        ga_own=full((R, W)),
        gk=full((S, LANES)),
        gv=full((S, LANES)),
        dqkv=half((S, 512)),
        gn=small(2, W),
        rt=small(E, W // 4),
        output_v=half((R, W)),
        grad_in_v=full((R, W)),
        gains_v=full((2, W)),
        router_v=full((4, E, W // 4)),
        full=[half((n, depth, c)) for c in piece_cols],
        seg=pltpu.VMEM((1, S), jnp.int32),
        routes=pltpu.VMEM((routes.shape[1], R), jnp.int32),
        gain_attn=full((1, W)),
        gain_ffn=full((1, W)),
        wr=half((E, W)),
        load_sem=dma((18,)),
        out_sem=dma((10,)),
        ag_send=dma((5, 3)),
        ag_recv=dma((5, 3)),
        rs_send=dma((4, 3)),
        rs_recv=dma((4, 3)),
        sb=[half((2, R, c)) for c in sums],
        sx=[half((R, c)) for c in sums],
        rp=[half((2, R, c)) for c in sums],
        rx=[half((R, c)) for c in sums],
        loc=[half((n, depth, c)) for c in piece_cols],
        held=[half((kept, depth, PIECE_COLS)) for _, _, kept in sizes],
        up_in=[half((outer, part, depth, PIECE_COLS)) for part, _, _ in sizes],
        down_in=[half((outer, part, depth, PIECE_COLS)) for part, _, _ in sizes],
        inbox=[half((inner - 1, part, depth, PIECE_COLS)) for _, part, _ in sizes],
        c_su=[dma((outer,)) for _ in sizes],
        c_ru=[dma((outer,)) for _ in sizes],
        c_sd=[dma((outer,)) for _ in sizes],
        c_rd=[dma((outer,)) for _ in sizes],
        g_su=[dma((outer,)) for _ in sizes],
        g_sd=[dma((outer,)) for _ in sizes],
        g_r=[dma((outer,)) for _ in sizes],
        i_s=[dma((inner - 1,)) for _ in sizes],
        i_r=[dma((inner - 1,)) for _ in sizes],
        o_s=[dma((inner - 1, outer)) for _ in sizes],
        o_r=[dma((inner - 1, outer)) for _ in sizes],
    )

    def call(kernel, specs, operands, results, result_spec, scratch, params):
        given, in_tree = jax.tree.flatten(operands)
        shapes, out_tree = jax.tree.flatten(results)
        inner_shapes, scratch_tree = jax.tree.flatten(scratch)

        def body(*refs):
            a, b = len(given), len(given) + len(shapes)
            named = jax.tree.unflatten(in_tree, refs[:a])
            named.update(jax.tree.unflatten(out_tree, refs[a:b]))
            named.update(jax.tree.unflatten(scratch_tree, refs[b:]))
            kernel(SimpleNamespace(**named))

        got = pl.pallas_call(
            body,
            out_shape=shapes,
            in_specs=jax.tree.flatten(specs)[0],
            out_specs=[result_spec] * len(shapes),
            scratch_shapes=inner_shapes,
            compiler_params=params,
        )(*given)
        return SimpleNamespace(**jax.tree.unflatten(out_tree, got))

    specs = {key: hbm for key in in_hbm}
    got = call(
        functools.partial(layer_kernel, n, inner, orders),
        specs, in_hbm, results, hbm, scratch,
        pltpu.CompilerParams(collective_id=0, has_side_effects=True, vmem_limit_bytes=VMEM_LIMIT),
    )

    ready = dict(
        output=got.output,
        grad_in=got.grad_in,
        gains=got.gains,
        router=got.router,
        pieces=[piece.reshape(W, PIECE_COLS) for piece in got.pieces],
    )
    finals = dict(
        o_output=shape((R, W), BF16),
        o_grad_in=shape((R, W), F32),
        o_gain_ffn=shape((1, W), F32),
        o_gain_attn=shape((1, W), F32),
        o_gate=shape(w_gate.shape, F32),
        o_up=shape(w_up.shape, F32),
        o_down=shape((down_rows, W), F32),
        o_wo=shape(attention_output_weight.shape, F32),
        o_wq=shape(w_query.shape, F32),
        o_wk=shape(key_matrix.shape, F32),
        o_wv=shape(value_matrix.shape, F32),
        o_router=shape((E, W), F32),
    )
    temps = dict(
        t_gate=full(w_gate.shape),
        t_up=full(w_up.shape),
        t_down=full((down_rows, W)),
        t_wo=full(attention_output_weight.shape),
        t_wq=full(w_query.shape),
        t_wk=full(key_matrix.shape),
        t_wv=full(value_matrix.shape),
        t_router=full((E, W)),
        v_pieces=[half((W, PIECE_COLS)) for _ in piece_cols],
        v_router=full((4, E, W // 4)),
        v_output=half((R, W)),
        v_grad_in=full((R, W)),
        v_gains=full((2, W)),
        t_gain_ffn=full((1, W)),
        t_gain_attn=full((1, W)),
        sem=dma((len(finals) + 10,)),
    )
    done = call(
        finish_kernel, jax.tree.map(lambda _: hbm, ready), ready, finals, hbm, temps,
        pltpu.CompilerParams(vmem_limit_bytes=VMEM_LIMIT),
    )
    return (
        done.o_output,
        done.o_grad_in,
        done.o_gain_attn.reshape(W),
        done.o_wq,
        done.o_wk,
        done.o_wv,
        done.o_wo,
        done.o_gain_ffn.reshape(W),
        done.o_router.T,
        done.o_gate,
        done.o_up,
        done.o_down.reshape(w_down.shape),
    )


def solution(mesh):
    rows = P(("dp", "tensor"), None)
    columns = P(None, "tensor")
    return jax.shard_map(
        on_device,
        mesh=mesh,
        in_specs=(
            rows, rows, P("dp", None), rows, P(), columns, columns, columns,
            P("tensor", None), P(), P(), P(None, None, "tensor"), P(None, None, "tensor"),
            P(None, "tensor", None),
        ),
        out_specs=(
            rows, rows, P(), columns, columns, columns, P("tensor", None), P(), P(),
            P(None, None, "tensor"), P(None, None, "tensor"), P(None, "tensor", None),
        ),
        check_vma=False,
    )
```
